32 devices in a mesh: dp: 8 (over z, x), tensor: 4 (over y, core).
Axes of the slice: x: 2, y: 2, z: 4, core: 2. Of those that a mesh axis runs over, the one named last changes fastest.
Arguments:
- tokens: bfloat16 [8192, 768], P(('dp', 'tensor')), may hold values from -6 to 6
- cotangent: bfloat16 [8192, 768], P(('dp', 'tensor')), may hold values from -6 to 6
- prefix: int32 [8], P('dp'), may hold values from 102 to 512
- w_qkv: bfloat16 [2, 3, 768, 768], P(None, None, None, 'tensor'), may hold values from -0.3125 to 0.3125
- bias_qv: float32 [2, 2, 768], P(None, None, 'tensor'), may hold values from -1.8 to 1.8
- w_out: bfloat16 [2, 768, 768], P(None, 'tensor'), may hold values from -0.625 to 0.625
- bias_out: float32 [2, 768], replicated, may hold values from -1.8 to 1.8
- norm_gain: float32 [2, 2, 768], replicated, may hold values from 0.5 to 1.5
- norm_bias: float32 [2, 2, 768], replicated, may hold values from -1.8 to 1.8
- w_up: bfloat16 [2, 768, 3072], P(None, None, 'tensor'), may hold values from -0.21875 to 0.21875
- bias_up: float32 [2, 3072], P(None, 'tensor'), may hold values from -3 to 3
- w_down: bfloat16 [2, 3072, 768], P(None, 'tensor'), may hold values from -0.15625 to 0.15625
- bias_down: float32 [2, 768], replicated, may hold values from -1.8 to 1.8
Outputs:
- output: float32 [8192, 768], P(('dp', 'tensor'))
- grad_tokens: float32 [8192, 768], P(('dp', 'tensor'))
- grad_w_qkv: float32 [2, 3, 768, 768], P(None, None, 'dp', 'tensor')
- grad_bias_qv: float32 [2, 2, 768], P(None, None, 'tensor')
- grad_w_out: float32 [2, 768, 768], P(None, 'tensor', 'dp')
- grad_bias_out: float32 [2, 768], replicated
- grad_norm_gain: float32 [2, 2, 768], replicated
- grad_norm_bias: float32 [2, 2, 768], replicated
- grad_w_up: float32 [2, 768, 3072], P(None, 'dp', 'tensor')
- grad_bias_up: float32 [2, 3072], P(None, 'tensor')
- grad_w_down: float32 [2, 3072, 768], P(None, 'tensor', 'dp')
- grad_bias_down: float32 [2, 768], replicated
The draws below stay inside these ranges and needn't reach their ends.
All inputs are finite; a program needn't handle non-finite values.
Results may differ from the reference program's by a relative error of at most 0.025.
The reference program's roundings to bfloat16 on the way count: a program that leaves them out, or rounds other values in their place, can miss the bound.
Values may be sent and summed in bfloat16 or wider, within the bound.
A program may use at most 192 MiB of HBM per device.

```python
import math
import jax
import jax.numpy as jnp
from jax import lax

D = 768
HEADS = 12
HDIM = 64
FF = 3072
LAYERS = 2
LEN = 1024
MEM = 10
SEQS = 8
TOKENS = 8192


def place_ends(values, own_key, smallest, largest):
    dims = values.shape
    spot = [jax.random.randint(jax.random.fold_in(own_key, axis), (), 0, dims[axis]) for axis in range(len(dims))]
    values = values.at[tuple(spot)].set(smallest)
    longest = dims.index(max(dims))
    spot[longest] = (spot[longest] + 1) % dims[longest]
    return values.at[tuple(spot)].set(largest)


def strengthened(drawn, own_key, source, target, blocks, factor):
    def block_of(dim):
        return (jnp.arange(drawn.shape[dim]) // (drawn.shape[dim] // blocks)).reshape((-1,) + (1,) * (drawn.ndim - 1 - dim))

    one_side = jax.random.permutation(own_key, blocks)[block_of(target)]
    other_side = (block_of(target) + blocks // 2) % blocks
    return jnp.where((block_of(source) == one_side) | (block_of(source) == other_side), factor * drawn, drawn)


def level_of(rng, extent, pieces, smallest, largest):
    def one(dim, shards_of):
        draws = jax.random.uniform(jax.random.fold_in(jax.random.fold_in(rng, 6), dim), (shards_of,), jnp.float32, smallest / len(pieces), largest / len(pieces))
        return jnp.repeat(jnp.exp(draws), extent[dim] // shards_of).reshape((-1,) + (1,) * (len(extent) - dim - 1))

    level = one(*pieces[0])
    for cut in pieces[1:]:
        level = level * one(*cut)
    return level


def normal_values(own_key, dims, scale, limit, split=(), kind=jnp.bfloat16):
    level = level_of(own_key, dims, split, -0.22, 0.18) if split else 1.0
    array = jax.random.normal(own_key, dims, jnp.float32) * scale * level
    return jnp.minimum(jnp.maximum(array, -limit), limit).astype(kind)


def gaussian_with(rng, dims, width, bound, pieces, heavy, held_as=jnp.bfloat16):
    array = width * jax.random.normal(rng, dims, jnp.float32)
    if pieces:
        array = array * level_of(rng, dims, pieces, -0.22, 0.18)
    return jnp.clip(strengthened(array, jax.random.fold_in(rng, 3), *heavy), -bound, bound).astype(held_as)


def setup_inputs(seed: int = 0) -> dict:
    key_of = jax.random.split(jax.random.key(seed), 14)
    return {
        "tokens": gaussian_with(key_of[0], (TOKENS, D), 1.0, 6.0, ((0, 32),), (0, 1, 32, 2.75)),
        "cotangent": gaussian_with(key_of[1], (TOKENS, D), 1.0, 6.0, ((0, 32),), (0, 1, 32, 2.75)),
        "prefix": place_ends(jax.random.randint(key_of[2], (SEQS,), LEN // 10, LEN // 2 + 1), jax.random.fold_in(key_of[2], 1), LEN // 10, (LEN // 2 + 1) - 1).astype(jnp.int32),
        "w_qkv": normal_values(key_of[3], (LAYERS, 3, D, D), (D // 2) ** -0.5, 0.3125, ((3, 4),)),
        "bias_qv": normal_values(key_of[4], (LAYERS, 2, D), 0.3, 1.8, ((2, 4),), jnp.float32),
        "w_out": normal_values(key_of[5], (LAYERS, D, D), (D // 8) ** -0.5, 0.625, ((1, 4),)),
        "bias_out": normal_values(key_of[6], (LAYERS, D), 0.3, 1.8, (), jnp.float32),
        "norm_gain": jnp.clip(1.0 + 0.1 * jax.random.normal(key_of[7], (LAYERS, 2, D), jnp.float32), 0.5, 1.5),
        "norm_bias": normal_values(key_of[8], (LAYERS, 2, D), 0.3, 1.8, (), jnp.float32),
        "w_up": normal_values(key_of[9], (LAYERS, D, FF), D ** -0.5, 0.21875, ((2, 4),)),
        "bias_up": normal_values(key_of[10], (LAYERS, FF), 0.5, 3.0, ((1, 4),), jnp.float32),
        "w_down": normal_values(key_of[11], (LAYERS, FF, D), (FF // 2) ** -0.5, 0.15625, ((1, 4),)),
        "bias_down": normal_values(key_of[12], (LAYERS, D), 0.3, 1.8, (), jnp.float32),
    }


EPSILON = 1e-06
HIGHEST = lax.Precision.HIGHEST

@jax.custom_vjp
def low(v):
    return lax.optimization_barrier(v.astype(jnp.bfloat16)).astype(jnp.float32)

@jax.custom_vjp
def low_back(v):
    return v

def low_keep(v):
    return (low(v), None)

def low_pass(kept, grad):
    return (grad,)

def back_keep(v):
    return (v, None)

def back_low(kept, grad):
    return (low(grad),)
low.defvjp(low_keep, low_pass)
low_back.defvjp(back_keep, back_low)

def matmul(left, right):
    return jnp.einsum('...i,ij->...j', left, right, precision=HIGHEST)

def layer_norm(total, gain, shift):
    row_mean = lax.optimization_barrier(jnp.mean(total, axis=-1, keepdims=True))
    centered = total - row_mean
    spread = lax.optimization_barrier(jnp.mean(centered * centered, axis=-1, keepdims=True))
    return centered * lax.rsqrt(spread + EPSILON) * gain + shift

def attend(query, keys, values, prefix_len):
    group = query.shape[0]
    block_rows = min(512, LEN)
    block_count = LEN // block_rows
    scale = 1.0 / math.sqrt(HDIM)
    blocks = jnp.moveaxis(query.reshape(group, block_count, block_rows, HEADS, HDIM), 1, 0)
    starts = jnp.arange(block_count, dtype=jnp.int32) * block_rows

    def one_block(pair):
        query_block, first_row = pair
        scores = jnp.einsum('gbhd,gkhd->ghbk', query_block, keys, precision=HIGHEST) * scale
        row_pos = first_row + lax.broadcasted_iota(jnp.int32, (block_rows, LEN), 0)
        col_pos = lax.broadcasted_iota(jnp.int32, (block_rows, LEN), 1)
        visible = (col_pos <= row_pos)[None] | (col_pos[None] < prefix_len[:, None, None])
        visible = visible | ((row_pos < MEM) | (row_pos >= LEN - MEM))[None]
        probs = jax.nn.softmax(jnp.where(visible[:, None], scores, -1e+30), axis=-1)
        return jnp.einsum('ghbk,gkhd->gbhd', low(probs), values, precision=HIGHEST)
    outcome = lax.map(jax.checkpoint(one_block), (blocks, starts))
    return jnp.moveaxis(outcome, 0, 1).reshape(group, LEN, HEADS * HDIM)

def layer_step(param_set, level, state, prefix_len):
    w_qkv, bias_qv, w_out, bias_out, norm_gain, norm_bias, w_up, bias_up, w_down, bias_down = param_set
    group = state.shape[0]
    in_low = low(state)
    query = low(matmul(in_low, w_qkv[level, 0]) + bias_qv[level, 0])
    keys = low(matmul(in_low, w_qkv[level, 1]))
    values = low(matmul(in_low, w_qkv[level, 2]) + bias_qv[level, 1])
    shape_four = (group, LEN, HEADS, HDIM)
    context = low(attend(query.reshape(shape_four), keys.reshape(shape_four), values.reshape(shape_four), prefix_len))
    attn_out = low_back(matmul(context, w_out[level]))
    normed = layer_norm(state + attn_out + bias_out[level], norm_gain[level, 0], norm_bias[level, 0])
    hidden = matmul(low(normed), w_up[level]) + bias_up[level]
    active = low(jax.nn.gelu(hidden, approximate=False))
    ffn_out = low_back(matmul(active, w_down[level]))
    return layer_norm(normed + ffn_out + bias_down[level], norm_gain[level, 1], norm_bias[level, 1])

def forward(param_set, state, prefix_len):
    for level in range(LAYERS):
        state = layer_step(param_set, level, state, prefix_len)
    return state

def reference(tokens, cotangent, prefix, w_qkv, bias_qv, w_out, bias_out, norm_gain, norm_bias, w_up, bias_up, w_down, bias_down):
    param_set = tuple((weight.astype(jnp.float32) for weight in (w_qkv, bias_qv, w_out, bias_out, norm_gain, norm_bias, w_up, bias_up, w_down, bias_down)))
    group = math.gcd(SEQS, max(1, 4096 // LEN))
    steps_count = SEQS // group
    inputs = tokens.astype(jnp.float32).reshape(steps_count, group, LEN, D)
    cotans = cotangent.astype(jnp.float32).reshape(steps_count, group, LEN, D)
    prefixes = prefix.reshape(steps_count, group)

    def one_group(running, sample):
        state, grad_out, prefix_len = sample
        outcome, pull = jax.vjp(lambda params_now, state_now: forward(params_now, state_now, prefix_len), param_set, state)
        grad_params, grad_state = pull(grad_out)
        running = jax.tree.map(jnp.add, running, grad_params)
        return (running, (outcome, grad_state))
    zeros_set = jax.tree.map(jnp.zeros_like, param_set)
    totals, (outputs, grads) = lax.scan(one_group, zeros_set, (inputs, cotans, prefixes))
    return (outputs.reshape(TOKENS, D), grads.reshape(TOKENS, D), totals[0], totals[1], totals[2], totals[3], totals[4], totals[5], totals[6], totals[7], totals[8], totals[9])
```

```python
import functools
import math

import jax
import jax.numpy as jnp
from jax import lax
from jax.experimental import pallas as pl
from jax.experimental.pallas import tpu as pltpu
from jax.sharding import PartitionSpec as P

HDIM = 64
LEN = 1024
MEM = 10
LANES = 128
GROUP = 4
PIECES = 2
EPSILON = 1e-06
VMEM_BYTES = 56 * 1024 * 1024
HIGHEST = lax.Precision.HIGHEST
MESH = pl.DeviceIdType.MESH
F32 = jnp.float32
BF16 = jnp.bfloat16
VM = pl.BlockSpec(memory_space=pltpu.VMEM)
SM = pl.BlockSpec(memory_space=pltpu.SMEM)


def dot(left, right):
    return jnp.dot(left, right, preferred_element_type=F32)


def dot_nt(left, right):
    return lax.dot_general(left, right, (((1,), (1,)), ((), ())), preferred_element_type=F32)


def remote(src, dst, send_sem, recv_sem, tensor_index):
    return pltpu.make_async_remote_copy(
        src_ref=src,
        dst_ref=dst,
        send_sem=send_sem,
        recv_sem=recv_sem,
        device_id={"tensor": tensor_index},
        device_id_type=MESH,
    )


def places():
    mine = lax.axis_index("tensor")
    chip = mine // 2
    core = mine - 2 * chip
    partner = mine + 1 - 2 * core
    across = mine + 2 - 4 * chip
    diagonal = across + 1 - 2 * core
    return mine, partner, across, diagonal


def group_barrier(others):
    barrier = pltpu.get_barrier_semaphore()
    for other in others:
        pl.semaphore_signal(barrier, inc=1, device_id={"tensor": other}, device_id_type=MESH)
    pl.semaphore_wait(barrier, len(others))


class Gather:
    def __init__(self, whole, send_sems, recv_sems):
        self.whole = whole
        self.mine, self.partner, self.across, self.diagonal = places()
        self.rows = whole.shape[1] // PIECES
        self.send_sems, self.recv_sems = send_sems, recv_sems

    def piece(self, chunk, part):
        return self.whole.at[chunk, pl.ds(part * self.rows, self.rows)]

    def to_partner(self):
        return remote(
            self.whole.at[self.mine], self.whole.at[self.mine],
            self.send_sems.at[0], self.recv_sems.at[0], self.partner,
        )

    def to_across(self, part):
        return remote(
            self.piece(self.mine, part), self.piece(self.mine, part),
            self.send_sems.at[1 + part], self.recv_sems.at[1 + part], self.across,
        )

    def onward(self, part):
        return remote(
            self.piece(self.across, part), self.piece(self.across, part),
            self.send_sems.at[1 + PIECES + part], self.recv_sems.at[1 + PIECES + part], self.partner,
        )

    def start(self):
        for part in range(PIECES):
            self.to_across(part).start()
        self.to_partner().start()

    def wait_partner(self):
        remote(
            self.whole.at[self.partner], self.whole.at[self.partner],
            self.send_sems.at[0], self.recv_sems.at[0], self.partner,
        ).wait_recv()

    def wait_across(self, part):
        remote(
            self.piece(self.across, part), self.piece(self.across, part),
            self.send_sems.at[1 + part], self.recv_sems.at[1 + part], self.across,
        ).wait_recv()

    def wait_diagonal(self, part):
        remote(
            self.piece(self.diagonal, part), self.piece(self.diagonal, part),
            self.send_sems.at[1 + PIECES + part], self.recv_sems.at[1 + PIECES + part], self.partner,
        ).wait_recv()

    def wait_sends(self):
        self.to_partner().wait_send()
        for part in range(PIECES):
            self.to_across(part).wait_send()
            self.onward(part).wait_send()


GATHER_SEMS = 1 + 2 * PIECES


def layer_norm(total, gain, shift):
    row_mean = jnp.mean(total, axis=-1, keepdims=True)
    centered = total - row_mean
    spread = jnp.mean(centered * centered, axis=-1, keepdims=True)
    recip = lax.rsqrt(spread + EPSILON)
    normal = centered * recip
    return normal * gain + shift, normal, recip


def visible_keys(chunk, rows):
    first, last = chunk * rows, (chunk + 1) * rows - 1
    if first < MEM or last >= LEN - MEM:
        return LEN
    return max(last + 1, LEN // 2)


def query_limits(chunk, rows, prefix_len):
    spots = chunk * rows + lax.broadcasted_iota(jnp.int32, (1, rows), 1)
    limits = jnp.maximum(spots, prefix_len - 1)
    return jnp.where((spots < MEM) | (spots >= LEN - MEM), LEN - 1, limits)


def attention_forward_kernel(
    state_ref, low_ref, wqkv_ref, bias_ref, wout_ref, bias_out_ref, gain_ref, shift_ref, prefix_ref,
    next_ref, next_low_ref, normal_ref, recip_ref, whole_ref, qt_ref, q2_ref, kz_ref, kt_ref,
    v2_ref, ct_ref, stats_ref,
    vt_ref, cf_ref, wo_ref,
    g_send, g_recv, c_send, c_recv, w_send, w_recv,
):
    mine, partner, across, diagonal = places()
    rows = low_ref.shape[0]
    heads = qt_ref.shape[0]
    group_barrier((partner, across, diagonal))
    gather = Gather(whole_ref, g_send, g_recv)
    whole_ref[mine] = low_ref[...]
    gather.start()
    wo_ref[mine] = wout_ref[...]
    lane_low = lax.broadcasted_iota(jnp.int32, (rows, LANES), 1) < HDIM

    def project(chunk):
        spots = pl.ds(pl.multiple_of(chunk * rows, rows), rows)
        values = whole_ref[chunk]
        for head in range(heads):
            def part(kind):
                columns = pl.ds((kind * heads + head) * LANES, LANES)
                return dot(values, wqkv_ref[:, columns]) + bias_ref[:, columns]
            query, key, value = part(0), part(1), part(2)
            q2_ref[head, spots] = query.astype(BF16)
            qt_ref[head, :, spots] = query.T.astype(BF16)
            kz_ref[head, spots] = jnp.where(lane_low, key, 0.0).astype(BF16)
            kt_ref[head, :, spots] = key.T.astype(BF16)
            v2_ref[head, spots] = value.astype(BF16)
            vt_ref[head, :, spots] = value.T[:HDIM].astype(BF16)

    def wout_to_partner(source):
        slot = 0 if source is mine else 2
        return remote(wo_ref.at[source], wo_ref.at[source], w_send.at[slot], w_recv.at[slot], partner)

    wout_to_across = remote(wo_ref.at[mine], wo_ref.at[mine], w_send.at[1], w_recv.at[1], across)
    wout_from_across = remote(wo_ref.at[across], wo_ref.at[across], w_send.at[1], w_recv.at[1], across)
    wout_from_partner = remote(wo_ref.at[partner], wo_ref.at[partner], w_send.at[0], w_recv.at[0], partner)
    wout_from_diagonal = remote(wo_ref.at[diagonal], wo_ref.at[diagonal], w_send.at[2], w_recv.at[2], partner)

    project(mine)
    gather.wait_partner()
    project(partner)
    for part in range(PIECES):
        gather.wait_across(part)
        gather.onward(part).start()
    wout_to_across.start()
    wout_to_partner(mine).start()
    project(across)
    for part in range(PIECES):
        gather.wait_diagonal(part)
    project(diagonal)

    def context_copy(step, chunk):
        return remote(ct_ref.at[chunk], cf_ref.at[mine], c_send.at[step], c_recv.at[step], chunk)

    def context_from(step, chunk):
        return remote(ct_ref.at[mine], cf_ref.at[chunk], c_send.at[step], c_recv.at[step], chunk)

    def attend(chunk):
        keys = visible_keys(chunk, rows)
        limits = query_limits(chunk, rows, prefix_ref[0])
        visible = lax.broadcasted_iota(jnp.int32, (keys, rows), 0) <= limits
        spots = pl.ds(chunk * rows, rows)

        def one_head(head, carry):
            scores = dot(kz_ref[head, pl.ds(0, keys)], qt_ref[head, :, spots])
            scores = jnp.where(visible, scores, -1e30)
            top = jnp.max(scores, axis=0, keepdims=True)
            expo = jnp.exp(scores - top)
            recip = 1.0 / jnp.sum(expo, axis=0, keepdims=True)
            probs = (expo * recip).astype(BF16)
            context = dot(vt_ref[head, :, pl.ds(0, keys)], probs)
            ct_ref[chunk, pl.ds(pl.multiple_of(head * HDIM, HDIM), HDIM)] = context.astype(BF16)
            first = lax.broadcasted_iota(jnp.int32, (8, rows), 0) == 0
            stats_ref[head, :, spots] = jnp.where(first, top, recip)
            return carry

        lax.fori_loop(0, heads, one_head, 0)

    chip, core = mine // 2, mine - 2 * (mine // 2)

    def step_chunk(step):
        near = step // 2
        flip = lax.rem(lax.rem(step, 2) + near, 2)
        to_chip = (1 - near) * (1 - chip) + near * chip
        return 2 * to_chip + core + flip * (1 - 2 * core)

    def one_step(step, carry):
        chunk = step_chunk(step)
        for each in range(GROUP):
            @pl.when(chunk == each)
            def _():
                attend(each)

        @pl.when(step < 3)
        def _():
            context_copy(step, chunk).start()

        @pl.when(step == 1)
        def _():
            wout_from_across.wait_recv()
            wout_to_partner(across).start()
        return carry

    lax.fori_loop(0, GROUP, one_step, 0)
    cf_ref[mine] = ct_ref[mine]
    wout_from_partner.wait_recv()
    wout_from_diagonal.wait_recv()
    for step, chunk in enumerate((across, diagonal, partner)):
        context_from(step, chunk).wait_recv()
    depth = GROUP * wout_ref.shape[0]
    context = cf_ref[...].reshape(depth, rows).astype(F32).T.astype(BF16)
    total = state_ref[...] + dot(context, wo_ref[...].reshape(depth, -1)) + bias_out_ref[...]
    result, normal, recip = layer_norm(total, gain_ref[...], shift_ref[...])
    next_ref[...] = result
    next_low_ref[...] = result.astype(BF16)
    normal_ref[...] = normal
    recip_ref[...] = jnp.broadcast_to(recip, recip_ref.shape)
    gather.wait_sends()
    wout_to_across.wait_send()
    wout_to_partner(mine).wait_send()
    wout_to_partner(across).wait_send()
    for step, chunk in enumerate((across, diagonal, partner)):
        context_copy(step, chunk).wait_send()


def shape(dims, kind=F32):
    return jax.ShapeDtypeStruct(dims, kind)


def dma_sems(count):
    return pltpu.SemaphoreType.DMA((count,))


def params(collective_id):
    return pltpu.CompilerParams(
        collective_id=collective_id, has_side_effects=True, vmem_limit_bytes=VMEM_BYTES
    )


def attention_layer(state, low, wqkv, bias, wout, bias_out, gain, shift, prefix):
    rows, width = low.shape
    depth = wout.shape[0]
    heads = depth // HDIM
    tall = GROUP * rows
    return pl.pallas_call(
        attention_forward_kernel,
        out_shape=(
            shape((rows, width)), shape((rows, width), BF16), shape((rows, width)),
            shape((rows, LANES)), shape((GROUP, rows, width), BF16),
            shape((heads, LANES, tall), BF16), shape((heads, tall, LANES), BF16),
            shape((heads, tall, LANES), BF16), shape((heads, LANES, tall), BF16),
            shape((heads, tall, LANES), BF16), shape((GROUP, depth, rows), BF16),
            shape((heads, 8, tall)),
        ),
        in_specs=[VM] * 8 + [SM],
        out_specs=(VM,) * 12,
        scratch_shapes=[
            pltpu.VMEM((heads, HDIM, tall), BF16),
            pltpu.VMEM((GROUP, depth, rows), BF16),
            pltpu.VMEM((GROUP, depth, width), BF16),
            dma_sems(GATHER_SEMS), dma_sems(GATHER_SEMS),
            dma_sems(3), dma_sems(3), dma_sems(3), dma_sems(3),
        ],
        compiler_params=params(1),
        name="attention_fwd",
    )(state, low, wqkv, bias, wout, bias_out, gain, shift, prefix)


def ffn_forward_kernel(
    state_ref, low_ref, wup_ref, bias_up_ref, wdown_ref, bias_down_ref, gain_ref, shift_ref,
    next_ref, next_low_ref, normal_ref, recip_ref, whole_ref, active_ref, slope_ref,
    terms_ref, near_ref, relay_ref, sum_ref, far_ref,
    g_send, g_recv, n_send, n_recv, r_send, r_recv, f_send, f_recv,
):
    mine, partner, across, diagonal = places()
    rows = low_ref.shape[0]
    part_rows = rows // PIECES
    group_barrier((partner, across, diagonal))
    gather = Gather(whole_ref, g_send, g_recv)
    whole_ref[mine] = low_ref[...]
    gather.start()

    def spot(part):
        return pl.ds(part * part_rows, part_rows)

    def units(chunk, part):
        hidden = dot(whole_ref[chunk, spot(part)], wup_ref[...]) + bias_up_ref[...]
        below = 0.5 * (1.0 + lax.erf(hidden * math.sqrt(0.5)))
        density = jnp.exp(-0.5 * hidden * hidden) * (1.0 / math.sqrt(2.0 * math.pi))
        active = (hidden * below).astype(BF16)
        active_ref[chunk, spot(part)] = active
        slope_ref[chunk, spot(part)] = below + hidden * density
        terms_ref[chunk, spot(part)] = dot(active, wdown_ref[...])

    def near_copy(part):
        return remote(
            terms_ref.at[partner, spot(part)], near_ref.at[spot(part)],
            n_send.at[part], n_recv.at[part], partner,
        )

    def relay_copy(part):
        return remote(
            terms_ref.at[diagonal, spot(part)], relay_ref.at[spot(part)],
            r_send.at[part], r_recv.at[part], partner,
        )

    def far_copy(part):
        return remote(
            sum_ref.at[spot(part)], far_ref.at[spot(part)], f_send.at[part], f_recv.at[part], across
        )

    def pass_on(part):
        relay_copy(part).wait_recv()
        sum_ref[spot(part)] = terms_ref[across, spot(part)] + relay_ref[spot(part)]
        far_copy(part).start()

    for part in range(PIECES):
        units(mine, part)
    for part in range(PIECES):
        gather.wait_across(part)
        gather.onward(part).start()
        units(across, part)
        gather.wait_diagonal(part)
        units(diagonal, part)
        relay_copy(part).start()
        if part > 0:
            pass_on(part - 1)
    gather.wait_partner()
    units(partner, 0)
    near_copy(0).start()
    pass_on(PIECES - 1)
    for part in range(1, PIECES):
        units(partner, part)
        near_copy(part).start()
    for part in range(PIECES):
        near_copy(part).wait_recv()
        far_copy(part).wait_recv()
        total = (
            state_ref[spot(part)]
            + ((terms_ref[mine, spot(part)] + near_ref[spot(part)]) + far_ref[spot(part)])
            + bias_down_ref[...]
        )
        result, normal, recip = layer_norm(total, gain_ref[...], shift_ref[...])
        next_ref[spot(part)] = result
        next_low_ref[spot(part)] = result.astype(BF16)
        normal_ref[spot(part)] = normal
        recip_ref[spot(part)] = jnp.broadcast_to(recip, (part_rows, LANES))
    gather.wait_sends()
    for part in range(PIECES):
        near_copy(part).wait_send()
        relay_copy(part).wait_send()
        far_copy(part).wait_send()


def ffn_layer(state, low, wup, bias_up, wdown, bias_down, gain, shift):
    rows, width = low.shape
    units = wup.shape[1]
    return pl.pallas_call(
        ffn_forward_kernel,
        out_shape=(
            shape((rows, width)), shape((rows, width), BF16), shape((rows, width)),
            shape((rows, LANES)), shape((GROUP, rows, width), BF16),
            shape((GROUP, rows, units), BF16), shape((GROUP, rows, units)),
        ),
        in_specs=[VM] * 8,
        out_specs=(VM,) * 7,
        scratch_shapes=[
            pltpu.VMEM((GROUP, rows, width), F32),
            pltpu.VMEM((rows, width), F32), pltpu.VMEM((rows, width), F32),
            pltpu.VMEM((rows, width), F32), pltpu.VMEM((rows, width), F32),
            dma_sems(GATHER_SEMS), dma_sems(GATHER_SEMS),
            dma_sems(PIECES), dma_sems(PIECES), dma_sems(PIECES), dma_sems(PIECES),
            dma_sems(PIECES), dma_sems(PIECES),
        ],
        compiler_params=params(2),
        name="ffn_fwd",
    )(state, low, wup, bias_up, wdown, bias_down, gain, shift)


def doubled(values, heads):
    lead = values.shape[:-1]
    split = values.reshape(lead + (heads, 1, HDIM))
    return jnp.broadcast_to(split, lead + (heads, 2, HDIM)).reshape(lead + (heads * LANES,))


def gather_rows(values_in):
    return lax.all_gather(values_in, "tensor", axis=0, tiled=True)


def sum_rows(term_fn, row_count):
    return lax.psum_scatter(
        term_fn(jnp.int32(0), lax.axis_size("tensor") * row_count),
        "tensor",
        scatter_dimension=0,
        tiled=True,
    )


def gather_grad(values_in):
    return lax.all_gather(values_in, "tensor", axis=0, tiled=True)


def sum_grad(term_fn, row_count):
    return lax.psum_scatter(
        term_fn(jnp.int32(0), lax.axis_size("tensor") * row_count),
        "tensor",
        scatter_dimension=0,
        tiled=True,
    )


def normalize_unused(total, gain, shift):
    row_mean = jnp.mean(total, axis=-1, keepdims=True)
    centered = total - row_mean
    spread = jnp.mean(centered * centered, axis=-1, keepdims=True)
    recip = lax.rsqrt(spread + EPSILON)
    normal = centered * recip
    return (normal * gain + shift, normal, recip)


def normalize_back(grad_in, normal, recip, gain):
    scaled = grad_in * gain
    inner = (
        scaled
        - jnp.mean(scaled, axis=-1, keepdims=True)
        - normal * jnp.mean(scaled * normal, axis=-1, keepdims=True)
    )
    return (recip * inner, jnp.sum(grad_in * normal, axis=0), jnp.sum(grad_in, axis=0))


def probabilities(query_block, keys_seq, first_row, prefix_len):
    block_rows = query_block.shape[0]
    scale = 1.0 / math.sqrt(HDIM)
    scores = (
        jnp.einsum("bhd,khd->hbk", query_block, keys_seq, preferred_element_type=jnp.float32)
        * scale
    )
    row_pos = first_row + lax.broadcasted_iota(jnp.int32, (block_rows, LEN), 0)
    col_pos = lax.broadcasted_iota(jnp.int32, (block_rows, LEN), 1)
    visible = (
        (col_pos <= row_pos) | (col_pos < prefix_len) | (row_pos < MEM) | (row_pos >= LEN - MEM)
    )
    scores = jnp.where(visible[None], scores, -1e30)
    row_max = jnp.max(scores, axis=-1, keepdims=True)
    expo = jnp.exp(scores - row_max)
    return expo / jnp.sum(expo, axis=-1, keepdims=True)


def attention_forward(query, keys, values, prefix):
    seq_count = prefix.shape[0]
    width = query.shape[1]
    local_heads = width // HDIM
    block_rows = min(512, LEN)
    block_count = LEN // block_rows
    shape_four = (seq_count, LEN, local_heads, HDIM)

    def per_sequence(sequence):
        query_seq, keys_seq, values_seq, prefix_len = sequence

        def per_block(block_index):
            first_row = block_index * block_rows
            query_block = lax.dynamic_slice_in_dim(query_seq, first_row, block_rows, 0)
            probs = probabilities(query_block, keys_seq, first_row, prefix_len)
            return jnp.einsum(
                "hbk,khd->bhd",
                probs.astype(jnp.bfloat16),
                values_seq,
                preferred_element_type=jnp.float32,
            ).astype(jnp.bfloat16)

        blocks = lax.map(per_block, jnp.arange(block_count, dtype=jnp.int32))
        return blocks.reshape(LEN, local_heads, HDIM)

    context = lax.map(
        per_sequence,
        (query.reshape(shape_four), keys.reshape(shape_four), values.reshape(shape_four), prefix),
    )
    return context.reshape(seq_count * LEN, width)


def attention_backward(query, keys, values, grad_context, prefix):
    seq_count = prefix.shape[0]
    width = query.shape[1]
    local_heads = width // HDIM
    block_rows = min(512, LEN)
    block_count = LEN // block_rows
    scale = 1.0 / math.sqrt(HDIM)
    shape_four = (seq_count, LEN, local_heads, HDIM)

    def per_sequence(sequence):
        query_seq, keys_seq, values_seq, grad_seq, prefix_len = sequence

        def per_block(running, block_index):
            keys_acc, values_acc = running
            first_row = block_index * block_rows
            query_block = lax.dynamic_slice_in_dim(query_seq, first_row, block_rows, 0)
            grad_block = lax.dynamic_slice_in_dim(grad_seq, first_row, block_rows, 0)
            probs = probabilities(query_block, keys_seq, first_row, prefix_len)
            probs_low = probs.astype(jnp.bfloat16)
            grad_probs = jnp.einsum(
                "bhd,khd->hbk",
                grad_block,
                values_seq,
                precision=HIGHEST,
                preferred_element_type=jnp.float32,
            )
            grad_scores = probs * (grad_probs - jnp.sum(probs * grad_probs, axis=-1, keepdims=True))
            grad_query = (
                jnp.einsum(
                    "hbk,khd->bhd",
                    grad_scores,
                    keys_seq,
                    precision=HIGHEST,
                    preferred_element_type=jnp.float32,
                )
                * scale
            )
            keys_acc = (
                keys_acc
                + jnp.einsum(
                    "hbk,bhd->khd",
                    grad_scores,
                    query_block,
                    precision=HIGHEST,
                    preferred_element_type=jnp.float32,
                )
                * scale
            )
            values_acc = values_acc + jnp.einsum(
                "hbk,bhd->khd",
                probs_low,
                grad_block,
                precision=HIGHEST,
                preferred_element_type=jnp.float32,
            )
            return ((keys_acc, values_acc), grad_query)

        zero_acc = jnp.zeros((LEN, local_heads, HDIM), jnp.float32)
        (keys_acc, values_acc), grad_query = lax.scan(
            per_block, (zero_acc, zero_acc), jnp.arange(block_count, dtype=jnp.int32)
        )
        return (grad_query.reshape(LEN, local_heads, HDIM), keys_acc, values_acc)

    grad_q, grad_k, grad_v = lax.map(
        per_sequence,
        (
            query.reshape(shape_four),
            keys.reshape(shape_four),
            values.reshape(shape_four),
            grad_context.reshape(shape_four),
            prefix,
        ),
    )
    flat = (seq_count * LEN, width)
    return (grad_q.reshape(flat), grad_k.reshape(flat), grad_v.reshape(flat))


def local(
    tokens,
    cotangent,
    prefix,
    w_qkv,
    bias_qv,
    w_out,
    bias_out,
    norm_gain,
    norm_bias,
    w_up,
    bias_up,
    w_down,
    bias_down,
):
    my_rows = tokens.shape[0]
    layer_count = w_qkv.shape[0]
    state = tokens.astype(F32)
    low = tokens
    depth = w_out.shape[1]
    heads = depth // HDIM
    scale = jnp.array([1.0 / math.sqrt(HDIM), 1.0, 1.0], BF16).reshape(1, 3, 1, 1)
    wqkv = doubled(w_qkv * scale, heads)
    wqkv = jnp.moveaxis(wqkv, 1, 2).reshape(layer_count, w_qkv.shape[2], -1)
    bias3 = jnp.stack(
        [bias_qv[:, 0] * (1.0 / math.sqrt(HDIM)), jnp.zeros_like(bias_qv[:, 0]), bias_qv[:, 1]], axis=1
    )
    bias3 = doubled(bias3, heads).reshape(layer_count, 1, -1)
    stored = []
    for layer_index in range(layer_count):
        (
            state, low, normal_one, recip_one, input_whole, qt, q2, kz, kt, v2, ct, stats,
        ) = attention_layer(
            state, low, wqkv[layer_index], bias3[layer_index], w_out[layer_index],
            bias_out[layer_index][None], norm_gain[layer_index, 0][None],
            norm_bias[layer_index, 0][None], prefix,
        )
        (
            state, low, normal_two, recip_two, normed_whole, active, slope,
        ) = ffn_layer(
            state, low, w_up[layer_index], bias_up[layer_index][None], w_down[layer_index],
            bias_down[layer_index][None], norm_gain[layer_index, 1][None],
            norm_bias[layer_index, 1][None],
        )
        total = GROUP * my_rows
        input_whole = input_whole.reshape(total, -1)
        normed_whole = normed_whole.reshape(total, -1)
        pick = lambda v: jnp.moveaxis(v[:, :, :HDIM], 0, 1).reshape(total, depth)
        stored.append(
            (
                input_whole, pick(q2) * 8, pick(kz), pick(v2),
                jnp.moveaxis(ct, 1, 2).reshape(total, depth), normal_one, recip_one[:, :1],
                normed_whole, slope.reshape(total, -1), active.reshape(total, -1), normal_two,
                recip_two[:, :1],
            )
        )
    grad_state = cotangent.astype(jnp.float32)
    weight_grads = [None] * layer_count
    bias_grads = [None] * layer_count
    shared_grads = [None] * layer_count
    for layer_index in reversed(range(layer_count)):
        (
            input_whole,
            query,
            keys,
            values,
            context,
            normal_one,
            recip_one,
            normed_whole,
            hidden,
            active,
            normal_two,
            recip_two,
        ) = stored[layer_index]
        grad_two, gain_two, shift_two = normalize_back(
            grad_state, normal_two, recip_two, norm_gain[layer_index, 1]
        )
        ffn_grad_whole = gather_grad(grad_two.astype(jnp.bfloat16))
        grad_down = jnp.einsum(
            "rf,rd->fd", active, ffn_grad_whole, preferred_element_type=jnp.float32
        )
        grad_active = jnp.einsum(
            "rd,fd->rf", ffn_grad_whole, w_down[layer_index], preferred_element_type=jnp.float32
        )
        grad_hidden = grad_active * hidden
        grad_up = jnp.einsum(
            "rd,rf->df",
            normed_whole,
            grad_hidden,
            precision=HIGHEST,
            preferred_element_type=jnp.float32,
        )
        grad_bias_up = jnp.sum(grad_hidden, axis=0)

        def ffn_back_term(row_start, row_count):
            return jnp.einsum(
                "rf,df->rd",
                grad_hidden,
                w_up[layer_index],
                precision=HIGHEST,
                preferred_element_type=jnp.float32,
            )

        grad_normed = sum_grad(ffn_back_term, my_rows) + grad_two
        grad_one, gain_one, shift_one = normalize_back(
            grad_normed, normal_one, recip_one, norm_gain[layer_index, 0]
        )
        attn_grad_whole = gather_grad(grad_one.astype(jnp.bfloat16))
        grad_out = jnp.einsum(
            "rh,rd->hd", context, attn_grad_whole, preferred_element_type=jnp.float32
        )
        grad_context = jnp.einsum(
            "rd,hd->rh", attn_grad_whole, w_out[layer_index], preferred_element_type=jnp.float32
        )
        grad_query, grad_keys, grad_values = attention_backward(
            query, keys, values, grad_context, prefix
        )
        grad_qkv = jnp.stack(
            [
                jnp.einsum(
                    "rd,rh->dh",
                    input_whole,
                    grad_query,
                    precision=HIGHEST,
                    preferred_element_type=jnp.float32,
                ),
                jnp.einsum(
                    "rd,rh->dh",
                    input_whole,
                    grad_keys,
                    precision=HIGHEST,
                    preferred_element_type=jnp.float32,
                ),
                jnp.einsum(
                    "rd,rh->dh",
                    input_whole,
                    grad_values,
                    precision=HIGHEST,
                    preferred_element_type=jnp.float32,
                ),
            ]
        )
        grad_bias_qv = jnp.stack([jnp.sum(grad_query, axis=0), jnp.sum(grad_values, axis=0)])

        def input_back_term(row_start, row_count):
            total = jnp.einsum(
                "rh,dh->rd",
                grad_query,
                w_qkv[layer_index, 0],
                precision=HIGHEST,
                preferred_element_type=jnp.float32,
            )
            total = total + jnp.einsum(
                "rh,dh->rd",
                grad_keys,
                w_qkv[layer_index, 1],
                precision=HIGHEST,
                preferred_element_type=jnp.float32,
            )
            return total + jnp.einsum(
                "rh,dh->rd",
                grad_values,
                w_qkv[layer_index, 2],
                precision=HIGHEST,
                preferred_element_type=jnp.float32,
            )

        grad_state = sum_grad(input_back_term, my_rows) + grad_one
        weight_grads[layer_index] = (grad_qkv, grad_out, grad_up, grad_down)
        bias_grads[layer_index] = (grad_bias_qv, grad_bias_up)
        shared_grads[layer_index] = (
            jnp.sum(grad_one, axis=0),
            jnp.stack([gain_one, gain_two]),
            jnp.stack([shift_one, shift_two]),
            jnp.sum(grad_two, axis=0),
        )
    stacked_weights = tuple(
        (
            jnp.stack([weight_grads[level][member] for level in range(layer_count)])
            for member in range(4)
        )
    )
    summed_qkv, summed_out, summed_up, summed_down = (
        lax.psum_scatter(stacked_weights[0], "dp", scatter_dimension=2, tiled=True),
        lax.psum_scatter(stacked_weights[1], "dp", scatter_dimension=2, tiled=True),
        lax.psum_scatter(stacked_weights[2], "dp", scatter_dimension=1, tiled=True),
        lax.psum_scatter(stacked_weights[3], "dp", scatter_dimension=2, tiled=True),
    )
    stacked_bias_qv = jnp.stack([bias_grads[level][0] for level in range(layer_count)])
    stacked_bias_up = jnp.stack([bias_grads[level][1] for level in range(layer_count)])
    summed_bias_qv, summed_bias_up = lax.psum((stacked_bias_qv, stacked_bias_up), "dp")
    stacked_shared = tuple(
        (
            jnp.stack([shared_grads[level][member] for level in range(layer_count)])
            for member in range(4)
        )
    )
    summed_bias_out, summed_gain, summed_shift, summed_bias_down = lax.psum(
        stacked_shared, ("dp", "tensor")
    )
    return (
        state,
        grad_state,
        summed_qkv,
        summed_bias_qv,
        summed_out,
        summed_bias_out,
        summed_gain,
        summed_shift,
        summed_up,
        summed_bias_up,
        summed_down,
        summed_bias_down,
    )


def solution(mesh):
    in_specs = (
        P(("dp", "tensor"), None),
        P(("dp", "tensor"), None),
        P("dp"),
        P(None, None, None, "tensor"),
        P(None, None, "tensor"),
        P(None, "tensor", None),
        P(),
        P(),
        P(),
        P(None, None, "tensor"),
        P(None, "tensor"),
        P(None, "tensor", None),
        P(),
    )
    out_specs = (
        P(("dp", "tensor"), None),
        P(("dp", "tensor"), None),
        P(None, None, "dp", "tensor"),
        P(None, None, "tensor"),
        P(None, "tensor", "dp"),
        P(),
        P(),
        P(),
        P(None, "dp", "tensor"),
        P(None, "tensor"),
        P(None, "tensor", "dp"),
        P(),
    )
    return jax.shard_map(local, mesh=mesh, in_specs=in_specs, out_specs=out_specs, check_vma=False)
```

```python
import functools
import math

import jax
import jax.numpy as jnp
from jax import lax
from jax.experimental import pallas as pl
from jax.experimental.pallas import tpu as pltpu
from jax.sharding import PartitionSpec as P

HDIM = 64
LEN = 1024
MEM = 10
LANES = 128
GROUP = 4
PIECES = 2
EPSILON = 1e-06
VMEM_BYTES = 56 * 1024 * 1024
HIGHEST = lax.Precision.HIGHEST
MESH = pl.DeviceIdType.MESH
F32 = jnp.float32
BF16 = jnp.bfloat16
VM = pl.BlockSpec(memory_space=pltpu.VMEM)
SM = pl.BlockSpec(memory_space=pltpu.SMEM)


def dot(left, right):
    return jnp.dot(left, right, preferred_element_type=F32)


def dot_nt(left, right):
    return lax.dot_general(left, right, (((1,), (1,)), ((), ())), preferred_element_type=F32)


def remote(src, dst, send_sem, recv_sem, tensor_index):
    return pltpu.make_async_remote_copy(
        src_ref=src,
        dst_ref=dst,
        send_sem=send_sem,
        recv_sem=recv_sem,
        device_id={"tensor": tensor_index},
        device_id_type=MESH,
    )


def places():
    mine = lax.axis_index("tensor")
    chip = mine // 2
    core = mine - 2 * chip
    partner = mine + 1 - 2 * core
    across = mine + 2 - 4 * chip
    diagonal = across + 1 - 2 * core
    return mine, partner, across, diagonal


def group_barrier(others):
    barrier = pltpu.get_barrier_semaphore()
    for other in others:
        pl.semaphore_signal(barrier, inc=1, device_id={"tensor": other}, device_id_type=MESH)
    pl.semaphore_wait(barrier, len(others))


class Gather:
    def __init__(self, whole, send_sems, recv_sems):
        self.whole = whole
        self.mine, self.partner, self.across, self.diagonal = places()
        self.rows = whole.shape[1] // PIECES
        self.send_sems, self.recv_sems = send_sems, recv_sems

    def piece(self, chunk, part):
        return self.whole.at[chunk, pl.ds(part * self.rows, self.rows)]

    def to_partner(self):
        return remote(
            self.whole.at[self.mine], self.whole.at[self.mine],
            self.send_sems.at[0], self.recv_sems.at[0], self.partner,
        )

    def to_across(self, part):
        return remote(
            self.piece(self.mine, part), self.piece(self.mine, part),
            self.send_sems.at[1 + part], self.recv_sems.at[1 + part], self.across,
        )

    def onward(self, part):
        return remote(
            self.piece(self.across, part), self.piece(self.across, part),
            self.send_sems.at[1 + PIECES + part], self.recv_sems.at[1 + PIECES + part], self.partner,
        )

    def start(self):
        for part in range(PIECES):
            self.to_across(part).start()
        self.to_partner().start()

    def wait_partner(self):
        remote(
            self.whole.at[self.partner], self.whole.at[self.partner],
            self.send_sems.at[0], self.recv_sems.at[0], self.partner,
        ).wait_recv()

    def wait_across(self, part):
        remote(
            self.piece(self.across, part), self.piece(self.across, part),
            self.send_sems.at[1 + part], self.recv_sems.at[1 + part], self.across,
        ).wait_recv()

    def wait_diagonal(self, part):
        remote(
            self.piece(self.diagonal, part), self.piece(self.diagonal, part),
            self.send_sems.at[1 + PIECES + part], self.recv_sems.at[1 + PIECES + part], self.partner,
        ).wait_recv()

    def wait_sends(self):
        self.to_partner().wait_send()
        for part in range(PIECES):
            self.to_across(part).wait_send()
            self.onward(part).wait_send()


GATHER_SEMS = 1 + 2 * PIECES


def layer_norm(total, gain, shift):
    row_mean = jnp.mean(total, axis=-1, keepdims=True)
    centered = total - row_mean
    spread = jnp.mean(centered * centered, axis=-1, keepdims=True)
    recip = lax.rsqrt(spread + EPSILON)
    normal = centered * recip
    return normal * gain + shift, normal, recip


def visible_keys(chunk, rows):
    first, last = chunk * rows, (chunk + 1) * rows - 1
    if first < MEM or last >= LEN - MEM:
        return LEN
    return max(last + 1, LEN // 2)


def query_limits(chunk, rows, prefix_len):
    spots = chunk * rows + lax.broadcasted_iota(jnp.int32, (1, rows), 1)
    limits = jnp.maximum(spots, prefix_len - 1)
    return jnp.where((spots < MEM) | (spots >= LEN - MEM), LEN - 1, limits)


def attention_forward_kernel(
    state_ref, low_ref, wqkv_ref, bias_ref, wout_ref, bias_out_ref, gain_ref, shift_ref, prefix_ref,
    next_ref, next_low_ref, normal_ref, recip_ref, whole_ref, qt_ref, q2_ref, kz_ref, kt_ref,
    v2_ref, ct_ref, stats_ref,
    vt_ref, cf_ref, wo_ref,
    g_send, g_recv, c_send, c_recv, w_send, w_recv,
):
    mine, partner, across, diagonal = places()
    rows = low_ref.shape[0]
    heads = qt_ref.shape[0]
    group_barrier((partner, across, diagonal))
    gather = Gather(whole_ref, g_send, g_recv)
    whole_ref[mine] = low_ref[...]
    gather.start()
    wo_ref[mine] = wout_ref[...]
    lane_low = lax.broadcasted_iota(jnp.int32, (rows, LANES), 1) < HDIM

    def project(chunk):
        spots = pl.ds(pl.multiple_of(chunk * rows, rows), rows)
        values = whole_ref[chunk]
        for head in range(heads):
            def part(kind):
                columns = pl.ds((kind * heads + head) * LANES, LANES)
                return dot(values, wqkv_ref[:, columns]) + bias_ref[:, columns]
            query, key, value = part(0), part(1), part(2)
            q2_ref[head, spots] = query.astype(BF16)
            qt_ref[head, :, spots] = query.T.astype(BF16)
            kz_ref[head, spots] = jnp.where(lane_low, key, 0.0).astype(BF16)
            kt_ref[head, :, spots] = key.T.astype(BF16)
            v2_ref[head, spots] = value.astype(BF16)
            vt_ref[head, :, spots] = value.T[:HDIM].astype(BF16)

    def wout_to_partner(source):
        slot = 0 if source is mine else 2
        return remote(wo_ref.at[source], wo_ref.at[source], w_send.at[slot], w_recv.at[slot], partner)

    wout_to_across = remote(wo_ref.at[mine], wo_ref.at[mine], w_send.at[1], w_recv.at[1], across)
    wout_from_across = remote(wo_ref.at[across], wo_ref.at[across], w_send.at[1], w_recv.at[1], across)
    wout_from_partner = remote(wo_ref.at[partner], wo_ref.at[partner], w_send.at[0], w_recv.at[0], partner)
    wout_from_diagonal = remote(wo_ref.at[diagonal], wo_ref.at[diagonal], w_send.at[2], w_recv.at[2], partner)

    project(mine)
    gather.wait_partner()
    project(partner)
    for part in range(PIECES):
        gather.wait_across(part)
        gather.onward(part).start()
    wout_to_across.start()
    wout_to_partner(mine).start()
    project(across)
    for part in range(PIECES):
        gather.wait_diagonal(part)
    project(diagonal)

    def context_copy(step, chunk):
        return remote(ct_ref.at[chunk], cf_ref.at[mine], c_send.at[step], c_recv.at[step], chunk)

    def context_from(step, chunk):
        return remote(ct_ref.at[mine], cf_ref.at[chunk], c_send.at[step], c_recv.at[step], chunk)

    def attend(chunk):
        keys = visible_keys(chunk, rows)
        limits = query_limits(chunk, rows, prefix_ref[0])
        visible = lax.broadcasted_iota(jnp.int32, (keys, rows), 0) <= limits
        spots = pl.ds(chunk * rows, rows)

        def one_head(head, carry):
            scores = dot(kz_ref[head, pl.ds(0, keys)], qt_ref[head, :, spots])
            scores = jnp.where(visible, scores, -1e30)
            top = jnp.max(scores, axis=0, keepdims=True)
            expo = jnp.exp(scores - top)
            recip = 1.0 / jnp.sum(expo, axis=0, keepdims=True)
            probs = (expo * recip).astype(BF16)
            context = dot(vt_ref[head, :, pl.ds(0, keys)], probs)
            ct_ref[chunk, pl.ds(pl.multiple_of(head * HDIM, HDIM), HDIM)] = context.astype(BF16)
            first = lax.broadcasted_iota(jnp.int32, (8, rows), 0) == 0
            stats_ref[head, :, spots] = jnp.where(first, top, recip)
            return carry

        lax.fori_loop(0, heads, one_head, 0)

    chip, core = mine // 2, mine - 2 * (mine // 2)

    def step_chunk(step):
        near = step // 2
        flip = lax.rem(lax.rem(step, 2) + near, 2)
        to_chip = (1 - near) * (1 - chip) + near * chip
        return 2 * to_chip + core + flip * (1 - 2 * core)

    def one_step(step, carry):
        chunk = step_chunk(step)
        for each in range(GROUP):
            @pl.when(chunk == each)
            def _():
                attend(each)

        @pl.when(step < 3)
        def _():
            context_copy(step, chunk).start()

        @pl.when(step == 1)
        def _():
            wout_from_across.wait_recv()
            wout_to_partner(across).start()
        return carry

    lax.fori_loop(0, GROUP, one_step, 0)
    cf_ref[mine] = ct_ref[mine]
    wout_from_partner.wait_recv()
    wout_from_diagonal.wait_recv()
    for step, chunk in enumerate((across, diagonal, partner)):
        context_from(step, chunk).wait_recv()
    depth = GROUP * wout_ref.shape[0]
    context = cf_ref[...].reshape(depth, rows).astype(F32).T.astype(BF16)
    total = state_ref[...] + dot(context, wo_ref[...].reshape(depth, -1)) + bias_out_ref[...]
    result, normal, recip = layer_norm(total, gain_ref[...], shift_ref[...])
    next_ref[...] = result
    next_low_ref[...] = result.astype(BF16)
    normal_ref[...] = normal
    recip_ref[...] = jnp.broadcast_to(recip, recip_ref.shape)
    gather.wait_sends()
    wout_to_across.wait_send()
    wout_to_partner(mine).wait_send()
    wout_to_partner(across).wait_send()
    for step, chunk in enumerate((across, diagonal, partner)):
        context_copy(step, chunk).wait_send()


def shape(dims, kind=F32):
    return jax.ShapeDtypeStruct(dims, kind)


def dma_sems(count):
    return pltpu.SemaphoreType.DMA((count,))


def params(collective_id):
    return pltpu.CompilerParams(
        collective_id=collective_id, has_side_effects=True, vmem_limit_bytes=VMEM_BYTES
    )


def attention_layer(state, low, wqkv, bias, wout, bias_out, gain, shift, prefix):
    rows, width = low.shape
    depth = wout.shape[0]
    heads = depth // HDIM
    tall = GROUP * rows
    return pl.pallas_call(
        attention_forward_kernel,
        out_shape=(
            shape((rows, width)), shape((rows, width), BF16), shape((rows, width)),
            shape((rows, LANES)), shape((GROUP, rows, width), BF16),
            shape((heads, LANES, tall), BF16), shape((heads, tall, LANES), BF16),
            shape((heads, tall, LANES), BF16), shape((heads, LANES, tall), BF16),
            shape((heads, tall, LANES), BF16), shape((GROUP, depth, rows), BF16),
            shape((heads, 8, tall)),
        ),
        in_specs=[VM] * 8 + [SM],
        out_specs=(VM,) * 12,
        scratch_shapes=[
            pltpu.VMEM((heads, HDIM, tall), BF16),
            pltpu.VMEM((GROUP, depth, rows), BF16),
            pltpu.VMEM((GROUP, depth, width), BF16),
            dma_sems(GATHER_SEMS), dma_sems(GATHER_SEMS),
            dma_sems(3), dma_sems(3), dma_sems(3), dma_sems(3),
        ],
        compiler_params=params(1),
        name="attention_fwd",
    )(state, low, wqkv, bias, wout, bias_out, gain, shift, prefix)


def ffn_forward_kernel(
    state_ref, low_ref, wup_ref, bias_up_ref, wdown_ref, bias_down_ref, gain_ref, shift_ref,
    next_ref, next_low_ref, normal_ref, recip_ref, whole_ref, active_ref, slope_ref,
    terms_ref, near_ref, relay_ref, sum_ref, far_ref,
    g_send, g_recv, n_send, n_recv, r_send, r_recv, f_send, f_recv,
):
    mine, partner, across, diagonal = places()
    rows = low_ref.shape[0]
    part_rows = rows // PIECES
    group_barrier((partner, across, diagonal))
    gather = Gather(whole_ref, g_send, g_recv)
    whole_ref[mine] = low_ref[...]
    gather.start()

    def spot(part):
        return pl.ds(part * part_rows, part_rows)

    def units(chunk, part):
        hidden = dot(whole_ref[chunk, spot(part)], wup_ref[...]) + bias_up_ref[...]
        below = 0.5 * (1.0 + lax.erf(hidden * math.sqrt(0.5)))
        density = jnp.exp(-0.5 * hidden * hidden) * (1.0 / math.sqrt(2.0 * math.pi))
        active = (hidden * below).astype(BF16)
        active_ref[chunk, spot(part)] = active
        slope_ref[chunk, spot(part)] = below + hidden * density
        terms_ref[chunk, spot(part)] = dot(active, wdown_ref[...])

    def near_copy(part):
        return remote(
            terms_ref.at[partner, spot(part)], near_ref.at[spot(part)],
            n_send.at[part], n_recv.at[part], partner,
        )

    def relay_copy(part):
        return remote(
            terms_ref.at[diagonal, spot(part)], relay_ref.at[spot(part)],
            r_send.at[part], r_recv.at[part], partner,
        )

    def far_copy(part):
        return remote(
            sum_ref.at[spot(part)], far_ref.at[spot(part)], f_send.at[part], f_recv.at[part], across
        )

    def pass_on(part):
        relay_copy(part).wait_recv()
        sum_ref[spot(part)] = terms_ref[across, spot(part)] + relay_ref[spot(part)]
        far_copy(part).start()

    for part in range(PIECES):
        units(mine, part)
    for part in range(PIECES):
        gather.wait_across(part)
        gather.onward(part).start()
        units(across, part)
        gather.wait_diagonal(part)
        units(diagonal, part)
        relay_copy(part).start()
        if part > 0:
            pass_on(part - 1)
    gather.wait_partner()
    units(partner, 0)
    near_copy(0).start()
    pass_on(PIECES - 1)
    for part in range(1, PIECES):
        units(partner, part)
        near_copy(part).start()
    for part in range(PIECES):
        near_copy(part).wait_recv()
        far_copy(part).wait_recv()
        total = (
            state_ref[spot(part)]
            + ((terms_ref[mine, spot(part)] + near_ref[spot(part)]) + far_ref[spot(part)])
            + bias_down_ref[...]
        )
        result, normal, recip = layer_norm(total, gain_ref[...], shift_ref[...])
        next_ref[spot(part)] = result
        next_low_ref[spot(part)] = result.astype(BF16)
        normal_ref[spot(part)] = normal
        recip_ref[spot(part)] = jnp.broadcast_to(recip, (part_rows, LANES))
    gather.wait_sends()
    for part in range(PIECES):
        near_copy(part).wait_send()
        relay_copy(part).wait_send()
        far_copy(part).wait_send()


def ffn_layer(state, low, wup, bias_up, wdown, bias_down, gain, shift):
    rows, width = low.shape
    units = wup.shape[1]
    return pl.pallas_call(
        ffn_forward_kernel,
        out_shape=(
            shape((rows, width)), shape((rows, width), BF16), shape((rows, width)),
            shape((rows, LANES)), shape((GROUP, rows, width), BF16),
            shape((GROUP, rows, units), BF16), shape((GROUP, rows, units)),
        ),
        in_specs=[VM] * 8,
        out_specs=(VM,) * 7,
        scratch_shapes=[
            pltpu.VMEM((GROUP, rows, width), F32),
            pltpu.VMEM((rows, width), F32), pltpu.VMEM((rows, width), F32),
            pltpu.VMEM((rows, width), F32), pltpu.VMEM((rows, width), F32),
            dma_sems(GATHER_SEMS), dma_sems(GATHER_SEMS),
            dma_sems(PIECES), dma_sems(PIECES), dma_sems(PIECES), dma_sems(PIECES),
            dma_sems(PIECES), dma_sems(PIECES),
        ],
        compiler_params=params(2),
        name="ffn_fwd",
    )(state, low, wup, bias_up, wdown, bias_down, gain, shift)


def doubled(values, heads):
    lead = values.shape[:-1]
    split = values.reshape(lead + (heads, 1, HDIM))
    return jnp.broadcast_to(split, lead + (heads, 2, HDIM)).reshape(lead + (heads * LANES,))


def layer_norm_back(grad_in, normal, recip, gain):
    scaled = grad_in * gain
    inner = (
        scaled
        - jnp.mean(scaled, axis=-1, keepdims=True)
        - normal * jnp.mean(scaled * normal, axis=-1, keepdims=True)
    )
    return recip * inner


def column_sum(values):
    return jnp.sum(values, axis=0, keepdims=True)


def high_low(values):
    high = values.astype(BF16)
    return high, (values - high.astype(F32)).astype(BF16)


def dot_tn(left, right):
    return lax.dot_general(left, right, (((0,), (0,)), ((), ())), preferred_element_type=F32)


def remote_dp(src, dst, send_sem, recv_sem, dp_index):
    return pltpu.make_async_remote_copy(
        src_ref=src,
        dst_ref=dst,
        send_sem=send_sem,
        recv_sem=recv_sem,
        device_id={"dp": dp_index},
        device_id_type=MESH,
    )


class Sequences:
    def __init__(self, count):
        self.pairs = count // 2
        self.index = lax.axis_index("dp")
        self.pair = self.index // 2
        self.side = self.index - 2 * self.pair
        self.neighbour = self.index + 1 - 2 * self.side

    def other_pair(self, offset):
        return lax.rem(self.pair + offset, self.pairs)

    def peer(self, offset):
        return 2 * self.other_pair(offset) + self.side

    def everyone(self):
        return [self.neighbour] + [self.peer(offset) for offset in range(1, self.pairs)]


def full_barrier(group, sequences):
    barrier = pltpu.get_barrier_semaphore()
    for other in group:
        pl.semaphore_signal(barrier, inc=1, device_id={"tensor": other}, device_id_type=MESH)
    others = sequences.everyone() if sequences is not None else []
    for other in others:
        pl.semaphore_signal(barrier, inc=1, device_id={"dp": other}, device_id_type=MESH)
    pl.semaphore_wait(barrier, len(group) + len(others))


class GradSum:
    def __init__(self, sequences, source, result, columns, first_out, first_in, second_out, second_in, sems):
        self.at = sequences
        self.source, self.result, self.columns = source, result, columns
        self.first_out, self.first_in = first_out, first_in
        self.second_out, self.second_in = second_out, second_in
        self.sems = sems
        self.rows = result.shape[0]

    def terms(self, pair, side):
        start = pl.multiple_of((2 * pair + side) * self.rows, 16)
        return self.source[pl.ds(start, self.rows), self.columns]

    def first_copy(self):
        return remote_dp(
            self.first_out.at[:, :, self.columns], self.first_in.at[:, :, self.columns],
            self.sems[0], self.sems[1], self.at.neighbour,
        )

    def second_copy(self, offset):
        return remote_dp(
            self.second_out.at[offset - 1, :, self.columns], self.second_in.at[offset - 1, :, self.columns],
            self.sems[2].at[offset - 1], self.sems[3].at[offset - 1], self.at.peer(offset),
        )

    def first(self):
        for pair in range(self.at.pairs):
            self.first_out[pair, :, self.columns] = self.terms(pair, 1 - self.at.side).astype(BF16)
        self.first_copy().start()

    def second(self):
        self.first_copy().wait_recv()
        for offset in range(1, self.at.pairs):
            pair = self.at.other_pair(offset)
            half = self.terms(pair, self.at.side) + self.first_in[pair, :, self.columns].astype(F32)
            self.second_out[offset - 1, :, self.columns] = half.astype(BF16)
            self.second_copy(offset).start()
        own = self.terms(self.at.pair, self.at.side)
        self.result[:, self.columns] = own + self.first_in[self.at.pair, :, self.columns].astype(F32)

    def third(self):
        total = self.result[:, self.columns]
        for offset in range(1, self.at.pairs):
            self.second_copy(offset).wait_recv()
            total = total + self.second_in[offset - 1, :, self.columns].astype(F32)
        self.result[:, self.columns] = total

    def wait_sends(self):
        self.first_copy().wait_send()
        for offset in range(1, self.at.pairs):
            self.second_copy(offset).wait_send()


def grad_sum_scratch(count, width, columns, blocks):
    rows, pairs = width // count, count // 2
    return [
        pltpu.VMEM((pairs, rows, columns), BF16), pltpu.VMEM((pairs, rows, columns), BF16),
        pltpu.VMEM((pairs - 1, rows, columns), BF16), pltpu.VMEM((pairs - 1, rows, columns), BF16),
        dma_sems(blocks), dma_sems(blocks),
        pltpu.SemaphoreType.DMA((blocks, pairs - 1)), pltpu.SemaphoreType.DMA((blocks, pairs - 1)),
    ]


def grad_sums(sequences, source, result, scratch, blocks):
    step = source.shape[1] // blocks
    sems = scratch[4:]
    return [
        GradSum(
            sequences, source, result, slice(block * step, (block + 1) * step), *scratch[:4],
            (sems[0].at[block], sems[1].at[block], sems[2].at[block], sems[3].at[block]),
        )
        for block in range(blocks)
    ]


class SmallSum:
    def __init__(self, sequences, source, result, shared_rows, slots, sems):
        self.at = sequences
        self.source, self.result, self.shared_rows = source, result, shared_rows
        self.group_slots, self.side_slots, self.pair_slots = slots
        self.g_send, self.g_recv, self.s_send, self.s_recv, self.p_send, self.p_recv = sems
        self.mine, self.partner, self.across, self.diagonal = places()

    def group_copy(self, index, to, slot):
        return remote(
            self.group_slots.at[slot], self.group_slots.at[slot],
            self.g_send.at[index], self.g_recv.at[index], to,
        )

    def start(self):
        if self.shared_rows:
            self.group_slots[self.mine] = self.source[...]
            for index, other in enumerate((self.partner, self.across, self.diagonal)):
                self.group_copy(index, other, self.mine).start()

    def side_copy(self, slot):
        return remote_dp(
            self.side_slots.at[slot], self.side_slots.at[slot],
            self.s_send.at[0], self.s_recv.at[0], self.at.neighbour,
        )

    def first(self):
        values = self.source[...]
        if self.shared_rows:
            for index, other in enumerate((self.partner, self.across, self.diagonal)):
                self.group_copy(index, other, other).wait_recv()
            total = self.group_slots[0]
            for slot in range(1, GROUP):
                total = total + self.group_slots[slot]
            shared = lax.broadcasted_iota(jnp.int32, values.shape, 0) < self.shared_rows
            values = jnp.where(shared, total, values)
        self.side_slots[self.at.side] = values
        self.side_copy(self.at.side).start()

    def pair_copy(self, offset, slot):
        return remote_dp(
            self.pair_slots.at[slot], self.pair_slots.at[slot],
            self.p_send.at[offset - 1], self.p_recv.at[offset - 1], self.at.peer(offset),
        )

    def second(self):
        self.side_copy(1 - self.at.side).wait_recv()
        self.pair_slots[self.at.pair] = self.side_slots[0] + self.side_slots[1]
        for offset in range(1, self.at.pairs):
            self.pair_copy(offset, self.at.pair).start()

    def third(self):
        for offset in range(1, self.at.pairs):
            self.pair_copy(offset, self.at.other_pair(self.at.pairs - offset)).wait_recv()
        total = self.pair_slots[0]
        for slot in range(1, self.at.pairs):
            total = total + self.pair_slots[slot]
        self.result[...] = total

    def wait_sends(self):
        if self.shared_rows:
            for index, other in enumerate((self.partner, self.across, self.diagonal)):
                self.group_copy(index, other, self.mine).wait_send()
        self.side_copy(self.at.side).wait_send()
        for offset in range(1, self.at.pairs):
            self.pair_copy(offset, self.at.pair).wait_send()


def small_sum_scratch(count, width):
    pairs = count // 2
    return [
        pltpu.VMEM((GROUP, 8, width), F32), pltpu.VMEM((2, 8, width), F32), pltpu.VMEM((pairs, 8, width), F32),
        dma_sems(3), dma_sems(3), dma_sems(1), dma_sems(1), dma_sems(pairs - 1), dma_sems(pairs - 1),
    ]


class Exchange:
    def __init__(self, terms, near, relay, total, far, sems):
        self.terms, self.near, self.relay, self.total, self.far = terms, near, relay, total, far
        self.n_send, self.n_recv, self.r_send, self.r_recv, self.f_send, self.f_recv = sems
        self.mine, self.partner, self.across, self.diagonal = places()
        self.rows = terms.shape[1] // PIECES

    def spot(self, part):
        return pl.ds(part * self.rows, self.rows)

    def near_copy(self, part):
        return remote(
            self.terms.at[self.partner, self.spot(part)], self.near.at[self.spot(part)],
            self.n_send.at[part], self.n_recv.at[part], self.partner,
        )

    def relay_copy(self, part):
        return remote(
            self.terms.at[self.diagonal, self.spot(part)], self.relay.at[self.spot(part)],
            self.r_send.at[part], self.r_recv.at[part], self.partner,
        )

    def far_copy(self, part):
        return remote(
            self.total.at[self.spot(part)], self.far.at[self.spot(part)],
            self.f_send.at[part], self.f_recv.at[part], self.across,
        )

    def pass_on(self, part):
        spot = self.spot(part)
        self.relay_copy(part).wait_recv()
        self.total[spot] = (self.terms[self.across, spot] + self.relay[spot]).astype(self.total.dtype)
        self.far_copy(part).start()

    def result(self, part):
        spot = self.spot(part)
        self.near_copy(part).wait_recv()
        self.far_copy(part).wait_recv()
        return (self.terms[self.mine, spot] + self.near[spot]) + self.far[spot].astype(F32)

    def wait_sends(self):
        for part in range(PIECES):
            self.near_copy(part).wait_send()
            self.relay_copy(part).wait_send()
            self.far_copy(part).wait_send()


def exchange_scratch(rows, width, kind):
    return [
        pltpu.VMEM((GROUP, rows, width), F32),
        pltpu.VMEM((rows, width), F32), pltpu.VMEM((rows, width), F32),
        pltpu.VMEM((rows, width), kind), pltpu.VMEM((rows, width), kind),
    ] + [dma_sems(PIECES)] * 6


class Refs:
    def __init__(self, refs):
        self.refs = list(refs)

    def take(self, count):
        taken, self.refs = self.refs[:count], self.refs[count:]
        return taken


ATTN_BLOCKS = 2
FFN_BLOCKS = 4


def ffn_backward_kernel(count, behind, *refs):
    refs = Refs(refs)
    (
        grad_ref, normal2_ref, recip2_ref, gain2_ref, wdown_ref, wup_ref, active_ref, slope_ref,
        normed_ref, normal1_ref, recip1_ref, gain1_ref,
    ) = refs.take(12)
    earlier = refs.take(1) if behind else None
    du_ref, low_ref, grads_ref, smalls_ref = refs.take(4)
    earlier_sum = refs.take(1) if behind else None
    df_ref, du2_ref, high_ref, lowbits_ref = refs.take(4)
    terms_ref, near_ref, relay_ref, sum_ref, far_ref = refs.take(5)
    exchange_sems = refs.take(6)
    g_send, g_recv = refs.take(2)
    mine, partner, across, diagonal = places()
    rows, width = grad_ref.shape
    units = wup_ref.shape[1]
    grad = grad_ref[...]
    normal2 = normal2_ref[...]
    du2 = layer_norm_back(grad, normal2, recip2_ref[:, :1], gain2_ref[...])
    du2_ref[...] = du2
    df_ref[mine] = du2.astype(BF16)
    sequences = Sequences(count) if behind else None
    full_barrier((partner, across, diagonal), sequences)
    gather = Gather(df_ref, g_send, g_recv)
    gather.start()
    blocks = grad_sums(sequences, earlier[0], earlier_sum[0], refs.take(8), ATTN_BLOCKS) if behind else []
    for block in blocks:
        block.first()
    exchange = Exchange(terms_ref, near_ref, relay_ref, sum_ref, far_ref, exchange_sems)
    smalls_ref[0:1] = column_sum(du2)
    smalls_ref[1:2] = column_sum(grad * normal2)
    smalls_ref[2:3] = column_sum(grad)
    smalls_ref[6:8] = jnp.zeros((2, width), F32)

    def back(chunk, part):
        spot = exchange.spot(part)
        grad_active = dot_nt(df_ref[chunk, spot], wdown_ref[...])
        grad_hidden = grad_active * slope_ref[chunk, spot]
        smalls_ref[6:7] = smalls_ref[6:7] + column_sum(grad_hidden)
        high, low = high_low(grad_hidden)
        high_ref[chunk, spot] = high
        lowbits_ref[chunk, spot] = low
        terms_ref[chunk, spot] = dot_nt(high, wup_ref[...]) + dot_nt(low, wup_ref[...])

    for part in range(PIECES):
        back(mine, part)
    for part in range(PIECES):
        gather.wait_across(part)
        gather.onward(part).start()
        back(across, part)
        gather.wait_diagonal(part)
        back(diagonal, part)
        exchange.relay_copy(part).start()
        if part > 0:
            exchange.pass_on(part - 1)
    gather.wait_partner()
    back(partner, 0)
    exchange.near_copy(0).start()
    exchange.pass_on(PIECES - 1)
    for part in range(1, PIECES):
        back(partner, part)
        exchange.near_copy(part).start()
    for block in blocks:
        block.second()
    tall = GROUP * rows
    grads_ref[:, :units] = dot_tn(normed_ref[...].reshape(tall, width), high_ref[...].reshape(tall, units)) + dot_tn(
        normed_ref[...].reshape(tall, width), lowbits_ref[...].reshape(tall, units)
    )
    grads_ref[:, units:] = dot_tn(df_ref[...].reshape(tall, width), active_ref[...].reshape(tall, units))
    for part in range(PIECES):
        spot = exchange.spot(part)
        grad_normed = exchange.result(part) + du2_ref[spot]
        normal1 = normal1_ref[spot]
        du = layer_norm_back(grad_normed, normal1, recip1_ref[spot, :1], gain1_ref[...])
        du_ref[spot] = du
        low_ref[spot] = du.astype(BF16)
        sums = (column_sum(grad_normed * normal1), column_sum(grad_normed), column_sum(du))
        for index, value in enumerate(sums):
            place = slice(3 + index, 4 + index)
            smalls_ref[place] = value if part == 0 else smalls_ref[place] + value
    for block in blocks:
        block.third()
    gather.wait_sends()
    exchange.wait_sends()
    for block in blocks:
        block.wait_sends()


def ffn_layer_back(count, grad, normal2, recip2, gain2, wdown, wup, active, slope, normed, normal1, recip1, gain1, earlier, collective):
    rows, width = grad.shape
    units = wup.shape[1]
    behind = earlier is not None
    outs = [shape((rows, width)), shape((rows, width), BF16), shape((width, 2 * units)), shape((8, width))]
    scratch = [
        pltpu.VMEM((GROUP, rows, width), BF16),
        pltpu.VMEM((rows, width), F32),
        pltpu.VMEM((GROUP, rows, units), BF16), pltpu.VMEM((GROUP, rows, units), BF16),
    ]
    scratch += exchange_scratch(rows, width, BF16) + [dma_sems(GATHER_SEMS), dma_sems(GATHER_SEMS)]
    extra = []
    if behind:
        extra = [earlier]
        outs.append(shape((width // count, earlier.shape[1])))
        scratch += grad_sum_scratch(count, width, earlier.shape[1], ATTN_BLOCKS)
    return pl.pallas_call(
        functools.partial(ffn_backward_kernel, count, behind),
        out_shape=tuple(outs),
        in_specs=[VM] * (12 + len(extra)),
        out_specs=(VM,) * len(outs),
        scratch_shapes=scratch,
        compiler_params=params(collective),
        name="ffn_bwd",
    )(grad, normal2, recip2, gain2, wdown, wup, active, slope, normed, normal1, recip1, gain1, *extra)


def attention_backward_kernel(count, behind, last, *refs):
    refs = Refs(refs)
    (
        low_ref, du_ref, wout_ref, qt_ref, q2_ref, kz_ref, kt_ref, v2_ref, ct_ref, stats_ref, input_ref,
        wqkv_ref, prefix_ref,
    ) = refs.take(13)
    earlier, smalls_in, bias_in = refs.take(3) if behind else (None,) * 3
    dx_ref, grads_ref, bias_ref = refs.take(3)
    earlier_sum, smalls_sum = refs.take(2) if behind else (None,) * 2
    grads_sum, bias_sum = refs.take(2) if last else (None,) * 2
    do_ref, dc_ref, dct_ref, dq_ref, dk_ref, dv_ref, packed_ref = refs.take(7)
    terms_ref, near_ref, relay_ref, sum_ref, far_ref = refs.take(5)
    exchange_sems = refs.take(6)
    g_send, g_recv = refs.take(2)
    mine, partner, across, diagonal = places()
    rows, width = low_ref.shape
    heads = qt_ref.shape[0]
    scale = 1.0 / math.sqrt(HDIM)
    sequences = Sequences(count) if behind else None
    full_barrier((partner, across, diagonal), sequences)
    gather = Gather(do_ref, g_send, g_recv)
    do_ref[mine] = low_ref[...]
    gather.start()
    exchange = Exchange(terms_ref, near_ref, relay_ref, sum_ref, far_ref, exchange_sems)
    blocks, own_blocks, small, own_small = [], [], None, None
    if behind:
        blocks = grad_sums(sequences, earlier, earlier_sum, refs.take(8), FFN_BLOCKS)
        small_source = refs.take(1)[0]
        is_bias = lax.broadcasted_iota(jnp.int32, small_source.shape, 0) == 7
        small_source[...] = jnp.where(is_bias, bias_in[...], smalls_in[...])
        small = SmallSum(sequences, small_source, smalls_sum, 6, refs.take(3), refs.take(6))
        small.start()
        blocks[0].first()
        blocks[1].first()
    if last:
        own_blocks = grad_sums(sequences, grads_ref, grads_sum, refs.take(8), ATTN_BLOCKS)
        own_small = SmallSum(sequences, bias_ref, bias_sum, 0, refs.take(3), refs.take(6))
    dk_ref[...] = jnp.zeros_like(dk_ref)
    dv_ref[...] = jnp.zeros_like(dv_ref)
    lane_low = lax.broadcasted_iota(jnp.int32, (rows, LANES), 1) < HDIM

    def pack(values):
        high = values.astype(BF16).astype(F32)
        return jnp.where(lane_low, high, values - high)

    def context_grad(chunk):
        spots = pl.ds(pl.multiple_of(chunk * rows, rows), rows)
        for head in range(heads):
            both = pack(dot(do_ref[chunk], wout_ref[:, pl.ds(head * LANES, LANES)]))
            dc_ref[head, spots] = both.astype(BF16)
            dct_ref[head, :, spots] = both.T.astype(BF16)

    def attend_back(chunk):
        keys = visible_keys(chunk, rows)
        limits = query_limits(chunk, rows, prefix_ref[0])
        visible = lax.broadcasted_iota(jnp.int32, (keys, rows), 0) <= limits
        spots = pl.ds(chunk * rows, rows)
        seen = pl.ds(0, keys)

        def one_head(head, carry):
            scores = dot(kz_ref[head, seen], qt_ref[head, :, spots])
            top = stats_ref[head, 0:1, spots]
            recip = stats_ref[head, 1:2, spots]
            probs = jnp.exp(jnp.where(visible, scores - top, -1e30)) * recip
            grad_probs = dot(v2_ref[head, seen], dct_ref[head, :, spots])
            inner = column_sum(probs * grad_probs)
            grad_scores = (probs * (grad_probs - inner)).astype(BF16)
            dv_ref[head, seen] = dv_ref[head, seen] + dot(probs.astype(BF16), dc_ref[head, spots])
            dk_ref[head, seen] = dk_ref[head, seen] + dot(grad_scores, q2_ref[head, spots])
            dq_ref[head, spots] = dot(kt_ref[head, :, seen], grad_scores).T * scale
            return carry

        lax.fori_loop(0, heads, one_head, 0)

    chip, core = mine // 2, mine - 2 * (mine // 2)

    def one_step(step, carry):
        near = 1 - step // 2
        flip = lax.rem(step, 2)
        to_chip = (1 - near) * (1 - chip) + near * chip
        chunk = 2 * to_chip + core + flip * (1 - 2 * core)

        @pl.when(step == 1)
        def _():
            gather.wait_partner()
            if behind:
                small.first()
                blocks[2].first()

        @pl.when(step == 2)
        def _():
            for part in range(PIECES):
                gather.wait_across(part)
                gather.onward(part).start()
            if behind:
                blocks[0].second()
                blocks[3].first()

        @pl.when(step == 3)
        def _():
            for part in range(PIECES):
                gather.wait_diagonal(part)
            if behind:
                blocks[1].second()

        context_grad(chunk)
        for each in range(GROUP):
            @pl.when(chunk == each)
            def _():
                attend_back(each)
        return carry

    lax.fori_loop(0, GROUP, one_step, 0)
    if behind:
        blocks[2].second()
        small.second()

    def pack_chunk(chunk, carry):
        spots = pl.ds(pl.multiple_of(chunk * rows, rows), rows)
        for head in range(heads):
            dv_wide = dv_ref[head, spots]
            parts = (dq_ref[head, spots], dk_ref[head, spots], dv_wide + pltpu.roll(dv_wide, HDIM, 1))
            for kind, values in enumerate(parts):
                packed_ref[chunk, :, pl.ds((kind * heads + head) * LANES, LANES)] = pack(values).astype(BF16)
                if kind != 1:
                    place = pl.ds(((kind // 2) * heads + head) * LANES, LANES)
                    bias_ref[:, place] = bias_ref[:, place] + column_sum(values)
        return carry

    bias_ref[...] = jnp.zeros_like(bias_ref)
    lax.fori_loop(0, GROUP, pack_chunk, 0)

    tall = GROUP * rows
    depth = heads * HDIM

    def weight_grads():
        out_wide = dot(ct_ref[0], do_ref[0])
        for chunk in range(1, GROUP):
            out_wide = out_wide + dot(ct_ref[chunk], do_ref[chunk])
        grads_ref[:, :depth] = out_wide.T
        whole_in = input_ref[...].reshape(tall, width)
        for index in range(3 * heads):
            wide = dot_tn(whole_in, packed_ref[:, :, pl.ds(index * LANES, LANES)].reshape(tall, LANES))
            wide = wide + pltpu.roll(wide, HDIM, 1)
            grads_ref[:, depth + index * HDIM : depth + (index + 1) * HDIM] = wide[:, :HDIM]

    def input_terms(chunk, part):
        spot = exchange.spot(part)
        terms_ref[chunk, spot] = dot(packed_ref[chunk, spot], wqkv_ref[...])

    if last:
        weight_grads()
        own_small.first()
        for block in own_blocks:
            block.first()
    if behind:
        blocks[3].second()
    for part in range(PIECES):
        input_terms(diagonal, part)
        exchange.relay_copy(part).start()
        input_terms(across, part)
        if part > 0:
            exchange.pass_on(part - 1)
    input_terms(partner, 0)
    exchange.near_copy(0).start()
    exchange.pass_on(PIECES - 1)
    for part in range(1, PIECES):
        input_terms(partner, part)
        exchange.near_copy(part).start()
    for part in range(PIECES):
        input_terms(mine, part)
    if behind:
        small.third()
        blocks[0].third()
        blocks[1].third()
    if last:
        own_small.second()
        for block in own_blocks:
            block.second()
    else:
        weight_grads()
    for part in range(PIECES):
        spot = exchange.spot(part)
        dx_ref[spot] = exchange.result(part) + du_ref[spot]
    if behind:
        blocks[2].third()
        blocks[3].third()
    if last:
        own_small.third()
        for block in own_blocks:
            block.third()
    gather.wait_sends()
    exchange.wait_sends()
    for item in blocks + own_blocks + [each for each in (small, own_small) if each is not None]:
        item.wait_sends()


def attention_layer_back(count, behind, last, low, du, wout, qt, q2, kz, kt, v2, ct, stats, whole, wqkv, prefix, extra, collective):
    rows, width = low.shape
    heads = qt.shape[0]
    tall = GROUP * rows
    columns = 4 * heads * HDIM
    outs = [shape((rows, width)), shape((width, columns)), shape((8, 2 * heads * LANES))]
    scratch = [
        pltpu.VMEM((GROUP, rows, width), BF16),
        pltpu.VMEM((heads, tall, LANES), BF16), pltpu.VMEM((heads, LANES, tall), BF16),
        pltpu.VMEM((heads, tall, LANES), F32), pltpu.VMEM((heads, tall, LANES), F32),
        pltpu.VMEM((heads, tall, LANES), F32),
        pltpu.VMEM((GROUP, rows, 3 * heads * LANES), BF16),
    ]
    scratch += exchange_scratch(rows, width, BF16) + [dma_sems(GATHER_SEMS), dma_sems(GATHER_SEMS)]
    if behind:
        outs += [shape((width // count, extra[0].shape[1])), shape((8, width))]
        scratch += grad_sum_scratch(count, width, extra[0].shape[1], FFN_BLOCKS)
        scratch += [pltpu.VMEM((8, width), F32)] + small_sum_scratch(count, width)
    if last:
        outs += [shape((width // count, columns)), shape((8, width))]
        scratch += grad_sum_scratch(count, width, columns, ATTN_BLOCKS) + small_sum_scratch(count, width)
    return pl.pallas_call(
        functools.partial(attention_backward_kernel, count, behind, last),
        out_shape=tuple(outs),
        in_specs=[VM] * 12 + [SM] + [VM] * len(extra),
        out_specs=(VM,) * len(outs),
        scratch_shapes=scratch,
        compiler_params=params(collective),
        name="attention_bwd",
    )(low, du, wout, qt, q2, kz, kt, v2, ct, stats, whole, wqkv, prefix, *extra)


def local(
    tokens,
    cotangent,
    prefix,
    w_qkv,
    bias_qv,
    w_out,
    bias_out,
    norm_gain,
    norm_bias,
    w_up,
    bias_up,
    w_down,
    bias_down,
):
    my_rows, width = tokens.shape
    layer_count = w_qkv.shape[0]
    depth = w_out.shape[1]
    heads = depth // HDIM
    root = 1.0 / math.sqrt(HDIM)
    scale = jnp.array([root, 1.0, 1.0], BF16).reshape(1, 3, 1, 1)
    wqkv = jnp.moveaxis(doubled(w_qkv * scale, heads), 1, 2).reshape(layer_count, width, -1)
    wqkv_back = jnp.swapaxes(doubled(w_qkv, heads), 2, 3).reshape(layer_count, -1, width)
    wout_back = doubled(jnp.swapaxes(w_out, 1, 2), heads)
    bias3 = jnp.stack([bias_qv[:, 0] * root, jnp.zeros_like(bias_qv[:, 0]), bias_qv[:, 1]], axis=1)
    bias3 = doubled(bias3, heads).reshape(layer_count, 1, -1)
    state, low = tokens.astype(F32), tokens
    stored = []
    for layer in range(layer_count):
        state, low, normal1, recip1, whole, qt, q2, kz, kt, v2, ct, stats = attention_layer(
            state, low, wqkv[layer], bias3[layer], w_out[layer], bias_out[layer][None],
            norm_gain[layer, 0][None], norm_bias[layer, 0][None], prefix,
        )
        state, low, normal2, recip2, normed, active, slope = ffn_layer(
            state, low, w_up[layer], bias_up[layer][None], w_down[layer],
            bias_down[layer][None], norm_gain[layer, 1][None], norm_bias[layer, 1][None],
        )
        stored.append(
            ((normal2, recip2), (active, slope, normed, normal1, recip1),
             (qt, q2, kz, kt, v2, ct, stats, whole))
        )
    count = lax.axis_size("dp")
    behind = count > 2 and count % 2 == 0 and (width // count) % 16 == 0
    grad = cotangent.astype(F32)
    attn_grads, ffn_grads, smalls, biases = [], [], [], []
    attn_sums, ffn_sums, small_sums = [], [], []
    earlier = None
    bias = jnp.zeros((8, width), F32)
    for layer in reversed(range(layer_count)):
        second, middle, first = stored[layer]
        last = behind and layer == 0
        du, low, ffn_grad, small, *sums = ffn_layer_back(
            count, grad, *second, norm_gain[layer, 1][None], w_down[layer], w_up[layer], *middle,
            norm_gain[layer, 0][None], earlier, 3 if earlier is None else 5,
        )
        attn_sums = sums + attn_sums
        extra = (ffn_grad, small, bias) if behind else ()
        grad, attn_grad, bias, *sums = attention_layer_back(
            count, behind, last, low, du, wout_back[layer], *first, wqkv_back[layer], prefix, extra,
            6 if last else 4,
        )
        if behind:
            earlier = attn_grad
            ffn_sums.insert(0, sums[0])
            small_sums.insert(0, sums[1])
            if last:
                attn_sums.insert(0, sums[2])
                small_sums.insert(0, sums[3])
        attn_grads.insert(0, attn_grad)
        ffn_grads.insert(0, ffn_grad)
        smalls.insert(0, small)
        biases.insert(0, bias)

    def head_columns(rows):
        return rows.reshape(layer_count, 2, heads, 2, HDIM)[:, :, :, 0].reshape(layer_count, 2, depth)

    if behind:
        attn_sum, ffn_sum = jnp.stack(attn_sums), jnp.stack(ffn_sums)
        shared = jnp.stack([each[:6] for each in small_sums[1:]])
        bias_qv_sum = head_columns(jnp.stack([each[7] for each in small_sums[: layer_count]]))
        bias_up_sum = jnp.stack([each[6] for each in small_sums[1:]])
    else:
        attn_sum = lax.psum_scatter(jnp.stack(attn_grads), "dp", scatter_dimension=1, tiled=True)
        ffn_sum = lax.psum_scatter(jnp.stack(ffn_grads), "dp", scatter_dimension=1, tiled=True)
        shared = lax.psum(jnp.stack(smalls)[:, :6], ("dp", "tensor"))
        bias_qv_sum, bias_up_sum = lax.psum(
            (head_columns(jnp.stack(biases)[:, 7]), jnp.stack(smalls)[:, 6]), "dp"
        )
    units = w_up.shape[2]
    mine = attn_sum.shape[1]
    return (
        state,
        grad,
        jnp.moveaxis(attn_sum[:, :, depth:].reshape(layer_count, mine, 3, depth), 2, 1),
        bias_qv_sum,
        jnp.swapaxes(attn_sum[:, :, :depth], 1, 2),
        shared[:, 5],
        jnp.stack([shared[:, 3], shared[:, 1]], axis=1),
        jnp.stack([shared[:, 4], shared[:, 2]], axis=1),
        ffn_sum[:, :, :units],
        bias_up_sum,
        jnp.swapaxes(ffn_sum[:, :, units:], 1, 2),
        shared[:, 0],
    )


def solution(mesh):
    in_specs = (
        P(("dp", "tensor"), None),
        P(("dp", "tensor"), None),
        P("dp"),
        P(None, None, None, "tensor"),
        P(None, None, "tensor"),
        P(None, "tensor", None),
        P(),
        P(),
        P(),
        P(None, None, "tensor"),
        P(None, "tensor"),
        P(None, "tensor", None),
        P(),
    )
    out_specs = (
        P(("dp", "tensor"), None),
        P(("dp", "tensor"), None),
        P(None, None, "dp", "tensor"),
        P(None, None, "tensor"),
        P(None, "tensor", "dp"),
        P(),
        P(),
        P(),
        P(None, "dp", "tensor"),
        P(None, "tensor"),
        P(None, "tensor", "dp"),
        P(),
    )
    return jax.shard_map(local, mesh=mesh, in_specs=in_specs, out_specs=out_specs, check_vma=False)
```

```python
import functools
import math

import jax
import jax.numpy as jnp
from jax import lax
from jax.experimental import pallas as pl
from jax.experimental.pallas import tpu as pltpu
from jax.sharding import PartitionSpec as P

HDIM = 64
LEN = 1024
MEM = 10
LANES = 128
GROUP = 4
PIECES = 2
EPSILON = 1e-06
VMEM_BYTES = 56 * 1024 * 1024
HIGHEST = lax.Precision.HIGHEST
MESH = pl.DeviceIdType.MESH
F32 = jnp.float32
BF16 = jnp.bfloat16
VM = pl.BlockSpec(memory_space=pltpu.VMEM)
SM = pl.BlockSpec(memory_space=pltpu.SMEM)
ANY = pl.BlockSpec(memory_space=pl.ANY)


def dot(left, right):
    return jnp.dot(left, right, preferred_element_type=F32)


def dot_nt(left, right):
    return lax.dot_general(left, right, (((1,), (1,)), ((), ())), preferred_element_type=F32)


def remote(src, dst, send_sem, recv_sem, tensor_index):
    return pltpu.make_async_remote_copy(
        src_ref=src,
        dst_ref=dst,
        send_sem=send_sem,
        recv_sem=recv_sem,
        device_id={"tensor": tensor_index},
        device_id_type=MESH,
    )


def places():
    mine = lax.axis_index("tensor")
    chip = mine // 2
    core = mine - 2 * chip
    partner = mine + 1 - 2 * core
    across = mine + 2 - 4 * chip
    diagonal = across + 1 - 2 * core
    return mine, partner, across, diagonal


class Refs:
    def __init__(self, refs):
        self.refs = list(refs)

    def take(self, count):
        taken, self.refs = self.refs[:count], self.refs[count:]
        return taken

    def one(self):
        return self.take(1)[0]


class Moves:
    def __init__(self, sems):
        self.sems, self.used, self.pending = sems, 0, []

    def start(self, source, target):
        move = pltpu.make_async_copy(source, target, self.sems.at[self.used])
        self.used += 1
        move.start()
        return move

    def store(self, source, target):
        self.pending.append(self.start(source, target))

    def finish(self):
        for move in self.pending:
            move.wait()


def remote_dp(src, dst, send_sem, recv_sem, dp_index):
    return pltpu.make_async_remote_copy(
        src_ref=src,
        dst_ref=dst,
        send_sem=send_sem,
        recv_sem=recv_sem,
        device_id={"dp": dp_index},
        device_id_type=MESH,
    )


class Sequences:
    def __init__(self, count):
        self.pairs = count // 2
        self.index = lax.axis_index("dp")
        self.pair = self.index // 2
        self.side = self.index - 2 * self.pair
        self.neighbour = self.index + 1 - 2 * self.side

    def other_pair(self, offset):
        return lax.rem(self.pair + offset, self.pairs)

    def peer(self, offset):
        return 2 * self.other_pair(offset) + self.side

    def everyone(self):
        return [self.neighbour] + [self.peer(offset) for offset in range(1, self.pairs)]


class Entry:
    def __init__(self, sequences=None):
        barrier = pltpu.get_barrier_semaphore()
        group = places()[1:]
        others = sequences.everyone() if sequences is not None else []
        for other in group:
            pl.semaphore_signal(barrier, inc=1, device_id={"tensor": other}, device_id_type=MESH)
        for other in others:
            pl.semaphore_signal(barrier, inc=1, device_id={"dp": other}, device_id_type=MESH)
        self.barrier, self.count = barrier, len(group) + len(others)

    def wait(self):
        pl.semaphore_wait(self.barrier, self.count)


class Gather:
    def __init__(self, whole, send_sems, recv_sems):
        self.whole = whole
        self.mine, self.partner, self.across, self.diagonal = places()
        self.rows = whole.shape[1] // PIECES
        self.send_sems, self.recv_sems = send_sems, recv_sems

    def piece(self, chunk, part):
        return self.whole.at[chunk, pl.ds(part * self.rows, self.rows)]

    def to_partner(self):
        return remote(
            self.whole.at[self.mine], self.whole.at[self.mine],
            self.send_sems.at[0], self.recv_sems.at[0], self.partner,
        )

    def to_across(self, part):
        return remote(
            self.piece(self.mine, part), self.piece(self.mine, part),
            self.send_sems.at[1 + part], self.recv_sems.at[1 + part], self.across,
        )

    def onward(self, part):
        return remote(
            self.piece(self.across, part), self.piece(self.across, part),
            self.send_sems.at[1 + PIECES + part], self.recv_sems.at[1 + PIECES + part], self.partner,
        )

    def start(self):
        for part in range(PIECES):
            self.to_across(part).start()
        self.to_partner().start()

    def wait_partner(self):
        remote(
            self.whole.at[self.partner], self.whole.at[self.partner],
            self.send_sems.at[0], self.recv_sems.at[0], self.partner,
        ).wait_recv()

    def wait_across(self, part):
        remote(
            self.piece(self.across, part), self.piece(self.across, part),
            self.send_sems.at[1 + part], self.recv_sems.at[1 + part], self.across,
        ).wait_recv()

    def wait_diagonal(self, part):
        remote(
            self.piece(self.diagonal, part), self.piece(self.diagonal, part),
            self.send_sems.at[1 + PIECES + part], self.recv_sems.at[1 + PIECES + part], self.partner,
        ).wait_recv()

    def wait_sends(self):
        self.to_partner().wait_send()
        for part in range(PIECES):
            self.to_across(part).wait_send()
            self.onward(part).wait_send()


GATHER_SEMS = 1 + 2 * PIECES


def shape(dims, kind=F32):
    return jax.ShapeDtypeStruct(dims, kind)


def dma_sems(*dims):
    return pltpu.SemaphoreType.DMA(dims)


def params(collective_id):
    return pltpu.CompilerParams(
        collective_id=collective_id, has_side_effects=True, vmem_limit_bytes=VMEM_BYTES
    )


def layer_norm(total, gain, shift):
    row_mean = jnp.mean(total, axis=-1, keepdims=True)
    centered = total - row_mean
    spread = jnp.mean(centered * centered, axis=-1, keepdims=True)
    recip = lax.rsqrt(spread + EPSILON)
    normal = centered * recip
    return normal * gain + shift, normal, recip


def visible_keys(chunk, rows):
    first, last = chunk * rows, (chunk + 1) * rows - 1
    if first < MEM or last >= LEN - MEM:
        return LEN
    return max(last + 1, LEN // 2)


def query_limits(chunk, rows, prefix_len):
    spots = chunk * rows + lax.broadcasted_iota(jnp.int32, (1, rows), 1)
    limits = jnp.maximum(spots, prefix_len - 1)
    return jnp.where((spots < MEM) | (spots >= LEN - MEM), LEN - 1, limits)


def transposed(values):
    return values.astype(F32).T


def head_pairs(values, heads):
    wide = []
    for head in range(heads):
        columns = values[:, head * HDIM : (head + 1) * HDIM]
        wide.append(jnp.concatenate([columns, columns], axis=1))
    return wide


class Exchange:
    def __init__(self, terms, near, relay, total, far, sems):
        self.terms, self.near, self.relay, self.total, self.far = terms, near, relay, total, far
        self.n_send, self.n_recv, self.r_send, self.r_recv, self.f_send, self.f_recv = sems
        self.mine, self.partner, self.across, self.diagonal = places()
        self.rows = terms.shape[1] // PIECES

    def spot(self, part):
        return pl.ds(part * self.rows, self.rows)

    def near_copy(self, part):
        return remote(
            self.terms.at[self.partner, self.spot(part)], self.near.at[self.spot(part)],
            self.n_send.at[part], self.n_recv.at[part], self.partner,
        )

    def relay_copy(self, part):
        return remote(
            self.terms.at[self.diagonal, self.spot(part)], self.relay.at[self.spot(part)],
            self.r_send.at[part], self.r_recv.at[part], self.partner,
        )

    def far_copy(self, part):
        return remote(
            self.total.at[self.spot(part)], self.far.at[self.spot(part)],
            self.f_send.at[part], self.f_recv.at[part], self.across,
        )

    def pass_on(self, part):
        spot = self.spot(part)
        self.relay_copy(part).wait_recv()
        self.total[spot] = (self.terms[self.across, spot] + self.relay[spot]).astype(self.total.dtype)
        self.far_copy(part).start()

    def result(self, part):
        spot = self.spot(part)
        self.near_copy(part).wait_recv()
        self.far_copy(part).wait_recv()
        return (self.terms[self.mine, spot] + self.near[spot]) + self.far[spot].astype(F32)

    def wait_sends(self):
        for part in range(PIECES):
            self.near_copy(part).wait_send()
            self.relay_copy(part).wait_send()
            self.far_copy(part).wait_send()


def exchange_scratch(rows, width, kind):
    return [
        pltpu.VMEM((GROUP, rows, width), F32),
        pltpu.VMEM((rows, width), F32), pltpu.VMEM((rows, width), F32),
        pltpu.VMEM((rows, width), kind), pltpu.VMEM((rows, width), kind),
    ] + [dma_sems(PIECES)] * 6


def attention_forward_kernel(layer, *refs):
    refs = Refs(refs)
    state_hbm, low_ref, wqkv_hbm, bias_ref, wout_hbm, bias_out_ref, gain_ref, shift_ref, prefix_ref = refs.take(9)
    next_ref, next_low_ref, normal_ref, recip_ref = refs.take(4)
    saved_hbm = refs.take(8)
    saved = refs.take(8)
    whole_ref, qt_ref, q2_ref, kz_ref, kt_ref, v2_ref, ct_ref, stats_ref = saved
    state_ref, wqkv_ref, vt_ref, cf_ref, wo_ref = refs.take(5)
    moves = Moves(refs.one())
    g_send, g_recv, c_send, c_recv, w_send, w_recv = refs.take(6)
    mine, partner, across, diagonal = places()
    rows = low_ref.shape[0]
    heads = qt_ref.shape[0]
    root = 1.0 / math.sqrt(HDIM)
    entry = Entry()
    wqkv_in = moves.start(wqkv_hbm.at[layer], wqkv_ref)
    wout_in = moves.start(wout_hbm.at[layer], wo_ref.at[mine])
    state_in = moves.start(state_hbm, state_ref)
    gather = Gather(whole_ref, g_send, g_recv)
    whole_ref[mine] = low_ref[...]
    entry.wait()
    gather.start()
    lane_low = lax.broadcasted_iota(jnp.int32, (rows, LANES), 1) < HDIM

    def project(chunk):
        spots = pl.ds(pl.multiple_of(chunk * rows, rows), rows)
        values = whole_ref[chunk]
        query = (dot(values, wqkv_ref[0]) + bias_ref[layer, 0:1]) * root
        key = dot(values, wqkv_ref[1])
        value = dot(values, wqkv_ref[2]) + bias_ref[layer, 1:2]
        queries, keys, valuess = [head_pairs(each, heads) for each in (query, key, value)]
        query_t, key_t, value_t = [each.T.astype(BF16) for each in (query, key, value)]
        for head in range(heads):
            part = slice(head * HDIM, (head + 1) * HDIM)
            q2_ref[head, spots] = queries[head].astype(BF16)
            kz_ref[head, spots] = jnp.where(lane_low, keys[head], 0.0).astype(BF16)
            v2_ref[head, spots] = valuess[head].astype(BF16)
            for half in (slice(0, HDIM), slice(HDIM, 2 * HDIM)):
                qt_ref[head, half, spots] = query_t[part]
                kt_ref[head, half, spots] = key_t[part]
            vt_ref[head, :, spots] = value_t[part]

    def wout_to_partner(source):
        slot = 0 if source is mine else 2
        return remote(wo_ref.at[source], wo_ref.at[source], w_send.at[slot], w_recv.at[slot], partner)

    wout_to_across = remote(wo_ref.at[mine], wo_ref.at[mine], w_send.at[1], w_recv.at[1], across)
    wout_from_across = remote(wo_ref.at[across], wo_ref.at[across], w_send.at[1], w_recv.at[1], across)
    wout_from_partner = remote(wo_ref.at[partner], wo_ref.at[partner], w_send.at[0], w_recv.at[0], partner)
    wout_from_diagonal = remote(wo_ref.at[diagonal], wo_ref.at[diagonal], w_send.at[2], w_recv.at[2], partner)

    wqkv_in.wait()
    project(mine)
    gather.wait_partner()
    project(partner)
    wout_in.wait()
    for part in range(PIECES):
        gather.wait_across(part)
        gather.onward(part).start()
    wout_to_across.start()
    wout_to_partner(mine).start()
    project(across)
    for part in range(PIECES):
        gather.wait_diagonal(part)
    project(diagonal)
    for source, target in zip(saved[:6], saved_hbm[:6]):
        moves.store(source, target)

    def context_copy(step, chunk):
        return remote(ct_ref.at[chunk], cf_ref.at[mine], c_send.at[step], c_recv.at[step], chunk)

    def context_from(step, chunk):
        return remote(ct_ref.at[mine], cf_ref.at[chunk], c_send.at[step], c_recv.at[step], chunk)

    def attend(chunk):
        keys = visible_keys(chunk, rows)
        limits = query_limits(chunk, rows, prefix_ref[0])
        visible = lax.broadcasted_iota(jnp.int32, (keys, rows), 0) <= limits
        spots = pl.ds(chunk * rows, rows)

        def one_head(head, carry):
            scores = dot(kz_ref[head, pl.ds(0, keys)], qt_ref[head, :, spots])
            scores = jnp.where(visible, scores, -1e30)
            top = jnp.max(scores, axis=0, keepdims=True)
            expo = jnp.exp(scores - top)
            recip = 1.0 / jnp.sum(expo, axis=0, keepdims=True)
            probs = (expo * recip).astype(BF16)
            context = dot(vt_ref[head, :, pl.ds(0, keys)], probs)
            ct_ref[chunk, pl.ds(pl.multiple_of(head * HDIM, HDIM), HDIM)] = context.astype(BF16)
            first = lax.broadcasted_iota(jnp.int32, (8, rows), 0) == 0
            stats_ref[head, :, spots] = jnp.where(first, top, recip)
            return carry

        lax.fori_loop(0, heads, one_head, 0)

    chip, core = mine // 2, mine - 2 * (mine // 2)

    def one_step(step, carry):
        near = step // 2
        flip = lax.rem(lax.rem(step, 2) + near, 2)
        to_chip = (1 - near) * (1 - chip) + near * chip
        chunk = 2 * to_chip + core + flip * (1 - 2 * core)
        for each in range(GROUP):
            @pl.when(chunk == each)
            def _():
                attend(each)

        @pl.when(step < 3)
        def _():
            context_copy(step, chunk).start()

        @pl.when(step == 1)
        def _():
            wout_from_across.wait_recv()
            wout_to_partner(across).start()
        return carry

    lax.fori_loop(0, GROUP, one_step, 0)
    for source, target in zip(saved[6:], saved_hbm[6:]):
        moves.store(source, target)
    cf_ref[mine] = ct_ref[mine]
    wout_from_partner.wait_recv()
    wout_from_diagonal.wait_recv()
    for step, chunk in enumerate((across, diagonal, partner)):
        context_from(step, chunk).wait_recv()
    depth = GROUP * wo_ref.shape[1]
    context = transposed(cf_ref[...].reshape(depth, rows)).astype(BF16)
    state_in.wait()
    total = (
        state_ref[...].astype(F32) + dot(context, wo_ref[...].reshape(depth, -1)) + bias_out_ref[layer : layer + 1]
    )
    result, normal, recip = layer_norm(total, gain_ref[layer, 0:1], shift_ref[layer, 0:1])
    next_ref[...] = result
    next_low_ref[...] = result.astype(BF16)
    normal_ref[...] = normal
    recip_ref[...] = jnp.broadcast_to(recip, recip_ref.shape)
    gather.wait_sends()
    wout_to_across.wait_send()
    wout_to_partner(mine).wait_send()
    wout_to_partner(across).wait_send()
    for step, chunk in enumerate((across, diagonal, partner)):
        context_copy(step, chunk).wait_send()
    moves.finish()


def attention_layer(layer, state, low, wqkv, bias, wout, bias_out, gain, shift, prefix):
    rows, width = low.shape
    depth = wout.shape[1]
    heads = depth // HDIM
    tall = GROUP * rows
    saved = [
        ((GROUP, rows, width), BF16),
        ((heads, LANES, tall), BF16), ((heads, tall, LANES), BF16), ((heads, tall, LANES), BF16),
        ((heads, LANES, tall), BF16), ((heads, tall, LANES), BF16), ((GROUP, depth, rows), BF16),
        ((heads, 8, tall), F32),
    ]
    return pl.pallas_call(
        functools.partial(attention_forward_kernel, layer),
        out_shape=[
            shape((rows, width)), shape((rows, width), BF16), shape((rows, width)), shape((rows, LANES)),
        ] + [shape(*each) for each in saved],
        in_specs=[ANY, VM, ANY, VM, ANY, VM, VM, VM, SM],
        out_specs=[VM] * 4 + [ANY] * 8,
        scratch_shapes=[pltpu.VMEM(*each) for each in saved] + [
            pltpu.VMEM((rows, width), state.dtype),
            pltpu.VMEM(wqkv.shape[1:], BF16),
            pltpu.VMEM((heads, HDIM, tall), BF16),
            pltpu.VMEM((GROUP, depth, rows), BF16),
            pltpu.VMEM((GROUP, depth, width), BF16),
            dma_sems(11),
            dma_sems(GATHER_SEMS), dma_sems(GATHER_SEMS),
            dma_sems(3), dma_sems(3), dma_sems(3), dma_sems(3),
        ],
        compiler_params=params(1 + layer),
        name="attention_fwd",
    )(state, low, wqkv, bias, wout, bias_out, gain, shift, prefix)


def ffn_forward_kernel(layer, *refs):
    refs = Refs(refs)
    state_hbm, low_ref, wup_hbm, bias_up_ref, wdown_hbm, bias_down_ref, gain_ref, shift_ref = refs.take(8)
    next_ref, next_low_ref, normal_ref, recip_ref = refs.take(4)
    saved_hbm = refs.take(3)
    whole_ref, active_ref, slope_ref = refs.take(3)
    state_ref, wup_ref, wdown_ref = refs.take(3)
    moves = Moves(refs.one())
    exchange_refs = refs.take(11)
    g_send, g_recv = refs.take(2)
    mine, partner, across, diagonal = places()
    rows = low_ref.shape[0]
    part_rows = rows // PIECES
    entry = Entry()
    wup_in = moves.start(wup_hbm.at[layer], wup_ref)
    wdown_in = moves.start(wdown_hbm.at[layer], wdown_ref)
    state_in = moves.start(state_hbm, state_ref)
    gather = Gather(whole_ref, g_send, g_recv)
    whole_ref[mine] = low_ref[...]
    entry.wait()
    gather.start()
    exchange = Exchange(*exchange_refs[:5], exchange_refs[5:])
    terms_ref = exchange.terms

    def units(chunk, part):
        spot = exchange.spot(part)
        hidden = dot(whole_ref[chunk, spot], wup_ref[...]) + bias_up_ref[layer : layer + 1]
        below = 0.5 * (1.0 + lax.erf(hidden * math.sqrt(0.5)))
        density = jnp.exp(-0.5 * hidden * hidden) * (1.0 / math.sqrt(2.0 * math.pi))
        active = (hidden * below).astype(BF16)
        active_ref[chunk, spot] = active
        slope_ref[chunk, spot] = below + hidden * density
        terms_ref[chunk, spot] = dot(active, wdown_ref[...])

    wup_in.wait()
    wdown_in.wait()
    for part in range(PIECES):
        units(mine, part)
    for part in range(PIECES):
        gather.wait_across(part)
        gather.onward(part).start()
        units(across, part)
        gather.wait_diagonal(part)
        units(diagonal, part)
        exchange.relay_copy(part).start()
        if part > 0:
            exchange.pass_on(part - 1)
    gather.wait_partner()
    moves.store(whole_ref, saved_hbm[0])
    units(partner, 0)
    exchange.near_copy(0).start()
    exchange.pass_on(PIECES - 1)
    for part in range(1, PIECES):
        units(partner, part)
        exchange.near_copy(part).start()
    moves.store(active_ref, saved_hbm[1])
    moves.store(slope_ref, saved_hbm[2])
    state_in.wait()
    for part in range(PIECES):
        spot = exchange.spot(part)
        total = state_ref[spot] + exchange.result(part) + bias_down_ref[layer : layer + 1]
        result, normal, recip = layer_norm(total, gain_ref[layer, 1:2], shift_ref[layer, 1:2])
        next_ref[spot] = result
        next_low_ref[spot] = result.astype(BF16)
        normal_ref[spot] = normal
        recip_ref[spot] = jnp.broadcast_to(recip, (part_rows, LANES))
    gather.wait_sends()
    exchange.wait_sends()
    moves.finish()


def ffn_layer(layer, state, low, wup, bias_up, wdown, bias_down, gain, shift):
    rows, width = low.shape
    units = wup.shape[2]
    saved = [((GROUP, rows, width), BF16), ((GROUP, rows, units), BF16), ((GROUP, rows, units), F32)]
    return pl.pallas_call(
        functools.partial(ffn_forward_kernel, layer),
        out_shape=[
            shape((rows, width)), shape((rows, width), BF16), shape((rows, width)), shape((rows, LANES)),
        ] + [shape(*each) for each in saved],
        in_specs=[ANY, VM, ANY, VM, ANY, VM, VM, VM],
        out_specs=[VM] * 4 + [ANY] * 3,
        scratch_shapes=[pltpu.VMEM(*each) for each in saved]
        + [
            pltpu.VMEM((rows, width), F32), pltpu.VMEM(wup.shape[1:], BF16), pltpu.VMEM(wdown.shape[1:], BF16),
            dma_sems(6),
        ]
        + exchange_scratch(rows, width, F32)
        + [dma_sems(GATHER_SEMS), dma_sems(GATHER_SEMS)],
        compiler_params=params(3 + layer),
        name="ffn_fwd",
    )(state, low, wup, bias_up, wdown, bias_down, gain, shift)


def layer_norm_back(grad_in, normal, recip, gain):
    scaled = grad_in * gain
    inner = (
        scaled
        - jnp.mean(scaled, axis=-1, keepdims=True)
        - normal * jnp.mean(scaled * normal, axis=-1, keepdims=True)
    )
    return recip * inner


def column_sum(values):
    return jnp.sum(values, axis=0, keepdims=True)


def high_low(values):
    high = values.astype(BF16)
    return high, (values - high.astype(F32)).astype(BF16)


def dot_tn(left, right):
    return lax.dot_general(left, right, (((0,), (0,)), ((), ())), preferred_element_type=F32)


class PairSum:
    def __init__(self, sequences, source, half, columns, buffers, sems):
        self.at, self.source, self.half, self.columns = sequences, source, half, columns
        self.out, self.into = buffers
        self.sems = sems
        self.rows = half.shape[1]

    def terms(self, pair, side):
        start = pl.multiple_of((2 * pair + side) * self.rows, 16)
        return self.source[pl.ds(start, self.rows), self.columns]

    def copy(self):
        return remote_dp(
            self.out.at[:, :, self.columns], self.into.at[:, :, self.columns], *self.sems, self.at.neighbour
        )

    def start(self):
        for pair in range(self.at.pairs):
            self.out[pair, :, self.columns] = self.terms(pair, 1 - self.at.side).astype(BF16)
        self.copy().start()

    def finish(self):
        self.copy().wait_recv()
        for pair in range(self.at.pairs):
            own = self.terms(pair, self.at.side)
            self.half[pair, :, self.columns] = own + self.into[pair, :, self.columns].astype(F32)

    def wait_sends(self):
        self.copy().wait_send()


class OwnerSum:
    def __init__(self, sequences, half, result, columns, buffers, sems):
        self.at, self.half, self.result, self.columns = sequences, half, result, columns
        self.out, self.into = buffers
        self.sems = sems

    def copy(self, offset):
        return remote_dp(
            self.out.at[offset - 1, :, self.columns], self.into.at[offset - 1, :, self.columns],
            self.sems[0].at[offset - 1], self.sems[1].at[offset - 1], self.at.peer(offset),
        )

    def start(self):
        for offset in range(1, self.at.pairs):
            pair = self.at.other_pair(offset)
            self.out[offset - 1, :, self.columns] = self.half[pair, :, self.columns].astype(BF16)
            self.copy(offset).start()

    def finish(self):
        total = self.half[self.at.pair, :, self.columns]
        for offset in range(1, self.at.pairs):
            self.copy(offset).wait_recv()
            total = total + self.into[offset - 1, :, self.columns].astype(F32)
        self.result[:, self.columns] = total

    def wait_sends(self):
        for offset in range(1, self.at.pairs):
            self.copy(offset).wait_send()


def column_blocks(columns, blocks):
    step = columns // blocks
    return [slice(block * step, (block + 1) * step) for block in range(blocks)]


def pair_scratch(count, width, columns, blocks):
    dims = (count // 2, width // count, columns)
    return [pltpu.VMEM(dims, BF16), pltpu.VMEM(dims, BF16), dma_sems(blocks), dma_sems(blocks)]


def pair_sums(sequences, source, half, scratch, blocks):
    out, into, send, recv = scratch
    return [
        PairSum(sequences, source, half, columns, (out, into), (send.at[block], recv.at[block]))
        for block, columns in enumerate(column_blocks(source.shape[1], blocks))
    ]


def owner_scratch(count, width, columns, blocks):
    pairs = count // 2
    dims = (pairs - 1, width // count, columns)
    return [
        pltpu.VMEM(dims, BF16), pltpu.VMEM(dims, BF16), dma_sems(blocks, pairs - 1), dma_sems(blocks, pairs - 1)
    ]


def owner_sums(sequences, half, result, scratch, blocks):
    out, into, send, recv = scratch
    return [
        OwnerSum(sequences, half, result, columns, (out, into), (send.at[block], recv.at[block]))
        for block, columns in enumerate(column_blocks(result.shape[1], blocks))
    ]


class SmallSum:
    def __init__(self, sequences, source, result, shared_rows, slots, sems):
        self.at = sequences
        self.source, self.result, self.shared_rows = source, result, shared_rows
        self.group_slots, self.side_slots, self.pair_slots = slots
        self.g_send, self.g_recv, self.s_send, self.s_recv, self.p_send, self.p_recv = sems
        self.mine, self.partner, self.across, self.diagonal = places()

    def group_copy(self, index, to, slot):
        return remote(
            self.group_slots.at[slot], self.group_slots.at[slot],
            self.g_send.at[index], self.g_recv.at[index], to,
        )

    def start(self):
        if self.shared_rows:
            self.group_slots[self.mine] = self.source[...]
            for index, other in enumerate((self.partner, self.across, self.diagonal)):
                self.group_copy(index, other, self.mine).start()

    def side_copy(self, slot):
        return remote_dp(
            self.side_slots.at[slot], self.side_slots.at[slot],
            self.s_send.at[0], self.s_recv.at[0], self.at.neighbour,
        )

    def first(self):
        values = self.source[...]
        if self.shared_rows:
            for index, other in enumerate((self.partner, self.across, self.diagonal)):
                self.group_copy(index, other, other).wait_recv()
            total = self.group_slots[0]
            for slot in range(1, GROUP):
                total = total + self.group_slots[slot]
            shared = lax.broadcasted_iota(jnp.int32, values.shape, 0) < self.shared_rows
            values = jnp.where(shared, total, values)
        self.side_slots[self.at.side] = values
        self.side_copy(self.at.side).start()

    def pair_copy(self, offset, slot):
        return remote_dp(
            self.pair_slots.at[slot], self.pair_slots.at[slot],
            self.p_send.at[offset - 1], self.p_recv.at[offset - 1], self.at.peer(offset),
        )

    def second(self):
        self.side_copy(1 - self.at.side).wait_recv()
        self.pair_slots[self.at.pair] = self.side_slots[0] + self.side_slots[1]
        for offset in range(1, self.at.pairs):
            self.pair_copy(offset, self.at.pair).start()

    def third(self):
        for offset in range(1, self.at.pairs):
            self.pair_copy(offset, self.at.other_pair(self.at.pairs - offset)).wait_recv()
        total = self.pair_slots[0]
        for slot in range(1, self.at.pairs):
            total = total + self.pair_slots[slot]
        self.result[...] = total

    def wait_sends(self):
        if self.shared_rows:
            for index, other in enumerate((self.partner, self.across, self.diagonal)):
                self.group_copy(index, other, self.mine).wait_send()
        self.side_copy(self.at.side).wait_send()
        for offset in range(1, self.at.pairs):
            self.pair_copy(offset, self.at.pair).wait_send()


def small_sum_scratch(count, width):
    pairs = count // 2
    return [
        pltpu.VMEM((GROUP, 8, width), F32), pltpu.VMEM((2, 8, width), F32), pltpu.VMEM((pairs, 8, width), F32),
        dma_sems(3), dma_sems(3), dma_sems(1), dma_sems(1), dma_sems(pairs - 1), dma_sems(pairs - 1),
    ]


BLOCKS = 2


def ffn_backward_kernel(layer, count, split, behind, *refs):
    refs = Refs(refs)
    grad_ref, normal2_ref, recip2_ref, gain_ref, wdown_hbm, wup_hbm = refs.take(6)
    active_hbm, slope_hbm, normed_hbm, normal1_hbm, recip1_ref = refs.take(5)
    earlier_hbm = refs.one() if behind else None
    du_ref, low_ref, up_hbm, down_out, smalls_ref = refs.take(5)
    earlier_sum = refs.one() if behind else None
    df_ref, du2_ref, high_ref, lowbits_ref = refs.take(4)
    wdown_ref, wup_ref, active_ref, slope_ref, normed_ref, normal1_ref, up_ref, down_ref = refs.take(8)
    moves = Moves(refs.one())
    exchange_refs = refs.take(11)
    g_send, g_recv = refs.take(2)
    mine, partner, across, diagonal = places()
    rows, width = grad_ref.shape
    units = wup_ref.shape[1]
    tall = GROUP * rows
    sequences = Sequences(count) if split else None
    entry = Entry(sequences)
    wdown_in = moves.start(wdown_hbm.at[layer], wdown_ref)
    slope_in = moves.start(slope_hbm, slope_ref)
    wup_in = moves.start(wup_hbm.at[layer], wup_ref)
    earlier_pairs, earlier_owners, down_pairs = [], [], []
    if behind:
        earlier_ref, half_ref = refs.take(2)
        earlier_in = moves.start(earlier_hbm, earlier_ref)
        earlier_pairs = pair_sums(sequences, earlier_ref, half_ref, refs.take(4), BLOCKS)
        earlier_owners = owner_sums(sequences, half_ref, earlier_sum, refs.take(4), BLOCKS)
    if split:
        down_pairs = pair_sums(sequences, down_ref, down_out, refs.take(4), BLOCKS)
    active_in = moves.start(active_hbm, active_ref)
    normed_in = moves.start(normed_hbm, normed_ref)
    normal1_in = moves.start(normal1_hbm, normal1_ref)
    gather = Gather(df_ref, g_send, g_recv)
    exchange = Exchange(*exchange_refs[:5], exchange_refs[5:])
    terms_ref = exchange.terms
    grad = grad_ref[...].astype(F32)
    normal2 = normal2_ref[...]
    du2 = layer_norm_back(grad, normal2, recip2_ref[:, :1], gain_ref[layer, 1:2])
    du2_ref[...] = du2
    df_ref[mine] = du2.astype(BF16)
    entry.wait()
    gather.start()
    smalls_ref[0:1] = column_sum(du2)
    smalls_ref[1:2] = column_sum(grad * normal2)
    smalls_ref[2:3] = column_sum(grad)
    smalls_ref[6:8] = jnp.zeros((2, width), F32)
    if behind:
        earlier_in.wait()
        for item in earlier_pairs:
            item.start()

    def back(chunk, part):
        spot = exchange.spot(part)
        grad_active = dot_nt(df_ref[chunk, spot], wdown_ref[...])
        grad_hidden = grad_active * slope_ref[chunk, spot]
        smalls_ref[6:7] = smalls_ref[6:7] + column_sum(grad_hidden)
        high, low = high_low(grad_hidden)
        high_ref[chunk, spot] = high
        lowbits_ref[chunk, spot] = low
        terms_ref[chunk, spot] = dot_nt(high, wup_ref[...]) + dot_nt(low, wup_ref[...])

    wdown_in.wait()
    slope_in.wait()
    wup_in.wait()
    for part in range(PIECES):
        back(mine, part)
    for part in range(PIECES):
        gather.wait_across(part)
        gather.onward(part).start()
        back(across, part)
        gather.wait_diagonal(part)
        back(diagonal, part)
        exchange.relay_copy(part).start()
        if part > 0:
            exchange.pass_on(part - 1)
    gather.wait_partner()
    back(partner, 0)
    exchange.near_copy(0).start()
    exchange.pass_on(PIECES - 1)
    for pair, owner in zip(earlier_pairs, earlier_owners):
        pair.finish()
        owner.start()
    active_in.wait()
    down_ref[...] = dot_tn(df_ref[...].reshape(tall, width), active_ref[...].reshape(tall, units))
    if split:
        for item in down_pairs:
            item.start()
    else:
        moves.store(down_ref, down_out)
    for part in range(1, PIECES):
        back(partner, part)
        exchange.near_copy(part).start()
    normed_in.wait()
    normed = normed_ref[...].reshape(tall, width)
    up_ref[...] = dot_tn(normed, high_ref[...].reshape(tall, units)) + dot_tn(
        normed, lowbits_ref[...].reshape(tall, units)
    )
    moves.store(up_ref, up_hbm)
    normal1_in.wait()
    for part in range(PIECES):
        spot = exchange.spot(part)
        grad_normed = exchange.result(part) + du2_ref[spot]
        normal1 = normal1_ref[spot]
        du = layer_norm_back(grad_normed, normal1, recip1_ref[spot, :1], gain_ref[layer, 0:1])
        du_ref[spot] = du
        low_ref[spot] = du.astype(BF16)
        sums = (column_sum(grad_normed * normal1), column_sum(grad_normed), column_sum(du))
        for index, value in enumerate(sums):
            place = slice(3 + index, 4 + index)
            smalls_ref[place] = value if part == 0 else smalls_ref[place] + value
    for item in earlier_owners + down_pairs:
        item.finish()
    gather.wait_sends()
    exchange.wait_sends()
    for item in earlier_pairs + earlier_owners + down_pairs:
        item.wait_sends()
    moves.finish()


def ffn_layer_back(layer, count, split, grad, normal2, recip2, gain, wdown, wup, active, slope, normed, normal1, recip1, earlier):
    rows, width = grad.shape
    units = wup.shape[2]
    behind = split and earlier is not None
    share = width // count
    down = (count // 2, share, units) if split else (width, units)
    outs = [
        shape((rows, width)), shape((rows, width), BF16), shape((width, units)), shape(down), shape((8, width)),
    ]
    out_specs = [VM, VM, ANY, VM if split else ANY, VM]
    scratch = [
        pltpu.VMEM((GROUP, rows, width), BF16),
        pltpu.VMEM((rows, width), F32),
        pltpu.VMEM((GROUP, rows, units), BF16), pltpu.VMEM((GROUP, rows, units), BF16),
        pltpu.VMEM(wdown.shape[1:], BF16), pltpu.VMEM(wup.shape[1:], BF16),
        pltpu.VMEM(active.shape, BF16), pltpu.VMEM(slope.shape, F32), pltpu.VMEM(normed.shape, BF16),
        pltpu.VMEM((rows, width), F32), pltpu.VMEM((width, units), F32), pltpu.VMEM((width, units), F32),
        dma_sems(9),
    ]
    scratch += exchange_scratch(rows, width, BF16) + [dma_sems(GATHER_SEMS), dma_sems(GATHER_SEMS)]
    extra = []
    if behind:
        extra = [earlier]
        columns = earlier.shape[1]
        outs.append(shape((share, columns)))
        out_specs.append(VM)
        scratch += [pltpu.VMEM((width, columns), F32), pltpu.VMEM((count // 2, share, columns), F32)]
        scratch += pair_scratch(count, width, columns, BLOCKS) + owner_scratch(count, width, columns, BLOCKS)
    if split:
        scratch += pair_scratch(count, width, units, BLOCKS)
    return pl.pallas_call(
        functools.partial(ffn_backward_kernel, layer, count, split, behind),
        out_shape=outs,
        in_specs=[VM] * 4 + [ANY] * 6 + [VM] + [ANY] * len(extra),
        out_specs=out_specs,
        scratch_shapes=scratch,
        compiler_params=params(5 + layer),
        name="ffn_bwd",
    )(grad, normal2, recip2, gain, wdown, wup, active, slope, normed, normal1, recip1, *extra)


def attention_backward_kernel(layer, count, split, last, *refs):
    refs = Refs(refs)
    low_ref, du_hbm, wout_hbm, wqkv_hbm = refs.take(4)
    saved_hbm = refs.take(8)
    prefix_ref = refs.one()
    up_hbm, half_hbm, smalls_in, bias_in = refs.take(4) if split else (None,) * 4
    dx_ref, grads_hbm, bias_ref = refs.take(3)
    up_sum, down_sum, smalls_sum = refs.take(3) if split else (None,) * 3
    grads_sum, bias_sum = refs.take(2) if last else (None,) * 2
    saved = refs.take(8)
    whole_ref, qt_ref, q2_ref, kz_ref, kt_ref, v2_ref, ct_ref, stats_ref = saved
    du_ref, wout_ref, wqkv_ref, grads_ref = refs.take(4)
    do_ref, dc_ref, dct_ref, dq_ref, dk_ref, dv_ref, high_ref, lowbits_ref, xt_ref = refs.take(9)
    moves = Moves(refs.one())
    exchange_refs = refs.take(11)
    g_send, g_recv = refs.take(2)
    mine, partner, across, diagonal = places()
    rows, width = low_ref.shape
    heads = qt_ref.shape[0]
    depth = heads * HDIM
    scale = 1.0 / math.sqrt(HDIM)
    sequences = Sequences(count) if split else None
    entry = Entry(sequences)
    wout_in = moves.start(wout_hbm.at[layer], wout_ref)
    saved_in = [moves.start(source, target) for source, target in zip(saved_hbm, saved)]
    up_pairs, up_owners, down_owners, small = [], [], [], None
    own_pairs, own_owners, own_small = [], [], None
    if split:
        half_ref, up_ref, up_half, small_source = refs.take(4)
        half_in = moves.start(half_hbm, half_ref)
        up_in = moves.start(up_hbm, up_ref)
        down_owners = owner_sums(sequences, half_ref, down_sum, refs.take(4), BLOCKS)
        up_pairs = pair_sums(sequences, up_ref, up_half, refs.take(4), BLOCKS)
        up_owners = owner_sums(sequences, up_half, up_sum, refs.take(4), BLOCKS)
        small = SmallSum(sequences, small_source, smalls_sum, 6, refs.take(3), refs.take(6))
    if last:
        own_half = refs.one()
        own_pairs = pair_sums(sequences, grads_ref, own_half, refs.take(4), BLOCKS)
        own_owners = owner_sums(sequences, own_half, grads_sum, refs.take(4), BLOCKS)
        own_small = SmallSum(sequences, bias_ref, bias_sum, 0, refs.take(3), refs.take(6))
    wqkv_in = moves.start(wqkv_hbm.at[layer], wqkv_ref)
    du_in = moves.start(du_hbm, du_ref)
    gather = Gather(do_ref, g_send, g_recv)
    exchange = Exchange(*exchange_refs[:5], exchange_refs[5:])
    terms_ref = exchange.terms
    do_ref[mine] = low_ref[...]
    entry.wait()
    gather.start()
    if split:
        is_bias = lax.broadcasted_iota(jnp.int32, small_source.shape, 0) == 7
        small_source[...] = jnp.where(is_bias, bias_in[...], smalls_in[...])
        small.start()
        half_in.wait()
        for item in down_owners:
            item.start()
        up_in.wait()
        for item in up_pairs:
            item.start()
    dk_ref[...] = jnp.zeros_like(dk_ref)
    dv_ref[...] = jnp.zeros_like(dv_ref)
    lane_low = lax.broadcasted_iota(jnp.int32, (rows, LANES), 1) < HDIM

    def context_grad(chunk):
        spots = pl.ds(pl.multiple_of(chunk * rows, rows), rows)
        wide = head_pairs(dot_nt(do_ref[chunk], wout_ref[...]), heads)
        for head in range(heads):
            high = wide[head].astype(BF16).astype(F32)
            both = jnp.where(lane_low, high, wide[head] - high)
            dc_ref[head, spots] = both.astype(BF16)
            dct_ref[head, :, spots] = both.T.astype(BF16)

    def attend_back(chunk):
        keys = visible_keys(chunk, rows)
        limits = query_limits(chunk, rows, prefix_ref[0])
        visible = lax.broadcasted_iota(jnp.int32, (keys, rows), 0) <= limits
        spots = pl.ds(chunk * rows, rows)
        seen = pl.ds(0, keys)

        def one_head(head, carry):
            scores = dot(kz_ref[head, seen], qt_ref[head, :, spots])
            top = stats_ref[head, 0:1, spots]
            recip = stats_ref[head, 1:2, spots]
            probs = jnp.exp(jnp.where(visible, scores - top, -1e30)) * recip
            grad_probs = dot(v2_ref[head, seen], dct_ref[head, :, spots])
            inner = column_sum(probs * grad_probs)
            grad_scores = (probs * (grad_probs - inner)).astype(BF16)
            dv_ref[head, seen] = dv_ref[head, seen] + dot(probs.astype(BF16), dc_ref[head, spots])
            dk_ref[head, seen] = dk_ref[head, seen] + dot(grad_scores, q2_ref[head, spots])
            dq_ref[head, spots] = dot(kt_ref[head, :, seen], grad_scores).T * scale
            return carry

        lax.fori_loop(0, heads, one_head, 0)

    chip, core = mine // 2, mine - 2 * (mine // 2)

    def one_step(step, carry):
        near = 1 - step // 2
        flip = lax.rem(step, 2)
        to_chip = (1 - near) * (1 - chip) + near * chip
        chunk = 2 * to_chip + core + flip * (1 - 2 * core)

        @pl.when(step == 1)
        def _():
            gather.wait_partner()
            if split:
                small.first()

        @pl.when(step == 2)
        def _():
            for part in range(PIECES):
                gather.wait_across(part)
                gather.onward(part).start()
            if split:
                up_pairs[0].finish()
                up_owners[0].start()

        @pl.when(step == 3)
        def _():
            for part in range(PIECES):
                gather.wait_diagonal(part)
            if split:
                up_pairs[1].finish()
                up_owners[1].start()
                small.second()

        context_grad(chunk)
        for each in range(GROUP):
            @pl.when(chunk == each)
            def _():
                attend_back(each)
        return carry

    wout_in.wait()
    for move in saved_in:
        move.wait()
    lax.fori_loop(0, GROUP, one_step, 0)

    def pack_chunk(chunk, carry):
        spots = pl.ds(pl.multiple_of(chunk * rows, rows), rows)
        xt_ref[:, spots] = transposed(whole_ref[chunk]).astype(BF16)
        for kind, wide_ref in enumerate((dq_ref, dk_ref, dv_ref)):
            parts = []
            for head in range(heads):
                wide = wide_ref[head, spots]
                if kind == 2:
                    wide = wide + pltpu.roll(wide, HDIM, 1)
                parts.append(wide[:, :HDIM])
            values = jnp.concatenate(parts, axis=1)
            high_ref[kind, spots], lowbits_ref[kind, spots] = high_low(values)
            if kind != 1:
                place = slice((kind // 2) * depth, (kind // 2 + 1) * depth)
                bias_ref[:, place] = bias_ref[:, place] + column_sum(values)
        return carry

    bias_ref[...] = jnp.zeros_like(bias_ref)
    lax.fori_loop(0, GROUP, pack_chunk, 0)

    def weight_grads():
        out_wide = dot(ct_ref[0], do_ref[0])
        for chunk in range(1, GROUP):
            out_wide = out_wide + dot(ct_ref[chunk], do_ref[chunk])
        grads_ref[:, :depth] = out_wide.T
        for kind in range(3):
            place = slice((kind + 1) * depth, (kind + 2) * depth)
            grads_ref[:, place] = dot(xt_ref[...], high_ref[kind]) + dot(xt_ref[...], lowbits_ref[kind])

    def input_terms(chunk, part):
        spot = exchange.spot(part)
        spots = pl.ds(pl.multiple_of(chunk * rows + part * (rows // PIECES), rows // PIECES), rows // PIECES)
        total = None
        for kind in range(3):
            for values in (high_ref, lowbits_ref):
                term = dot_nt(values[kind, spots], wqkv_ref[kind])
                total = term if total is None else total + term
        terms_ref[chunk, spot] = total

    wqkv_in.wait()
    if last:
        weight_grads()
        own_small.first()
        for item in own_pairs:
            item.start()
    for part in range(PIECES):
        input_terms(diagonal, part)
        exchange.relay_copy(part).start()
        input_terms(across, part)
        if part > 0:
            exchange.pass_on(part - 1)
    input_terms(partner, 0)
    exchange.near_copy(0).start()
    exchange.pass_on(PIECES - 1)
    for part in range(1, PIECES):
        input_terms(partner, part)
        exchange.near_copy(part).start()
    if last:
        own_pairs[0].finish()
        own_owners[0].start()
    for part in range(PIECES):
        input_terms(mine, part)
    if not last:
        weight_grads()
        moves.store(grads_ref, grads_hbm)
    if split:
        small.third()
        for item in down_owners:
            item.finish()
    if last:
        own_pairs[1].finish()
        own_owners[1].start()
        own_small.second()
    for item in up_owners:
        item.finish()
    du_in.wait()
    for part in range(PIECES):
        spot = exchange.spot(part)
        dx_ref[spot] = exchange.result(part) + du_ref[spot]
    if last:
        own_small.third()
        for item in own_owners:
            item.finish()
        grads_hbm[...] = bias_ref[...]
    gather.wait_sends()
    exchange.wait_sends()
    for item in down_owners + up_pairs + up_owners + own_pairs + own_owners:
        item.wait_sends()
    for item in (small, own_small):
        if item is not None:
            item.wait_sends()
    moves.finish()


def attention_layer_back(layer, count, split, low, du, wout, wqkv, saved, prefix, extra):
    rows, width = low.shape
    last = split and layer == 0
    depth = wout.shape[1]
    heads = depth // HDIM
    tall = GROUP * rows
    columns = 4 * depth
    share = width // count
    outs = [shape((rows, width)), shape((8, width) if last else (width, columns)), shape((8, width))]
    out_specs = [VM, VM if last else ANY, VM]
    scratch = [pltpu.VMEM(each.shape, each.dtype) for each in saved]
    scratch += [
        pltpu.VMEM((rows, width), F32), pltpu.VMEM(wout.shape[1:], BF16), pltpu.VMEM(wqkv.shape[1:], BF16),
        pltpu.VMEM((width, columns), F32),
        pltpu.VMEM((GROUP, rows, width), BF16),
        pltpu.VMEM((heads, tall, LANES), BF16), pltpu.VMEM((heads, LANES, tall), BF16),
        pltpu.VMEM((heads, tall, LANES), F32), pltpu.VMEM((heads, tall, LANES), F32),
        pltpu.VMEM((heads, tall, LANES), F32),
        pltpu.VMEM((3, tall, depth), BF16), pltpu.VMEM((3, tall, depth), BF16),
        pltpu.VMEM((width, tall), BF16),
        dma_sems(14),
    ]
    scratch += exchange_scratch(rows, width, BF16) + [dma_sems(GATHER_SEMS), dma_sems(GATHER_SEMS)]
    if split:
        units = extra[0].shape[1]
        outs += [shape((share, units)), shape((share, units)), shape((8, width))]
        out_specs += [VM] * 3
        half = pltpu.VMEM((count // 2, share, units), F32)
        scratch += [half, pltpu.VMEM((width, units), F32), half, pltpu.VMEM((8, width), F32)]
        scratch += owner_scratch(count, width, units, BLOCKS)
        scratch += pair_scratch(count, width, units, BLOCKS) + owner_scratch(count, width, units, BLOCKS)
        scratch += small_sum_scratch(count, width)
    if last:
        outs += [shape((share, columns)), shape((8, width))]
        out_specs += [VM] * 2
        scratch += [pltpu.VMEM((count // 2, share, columns), F32)]
        scratch += pair_scratch(count, width, columns, BLOCKS) + owner_scratch(count, width, columns, BLOCKS)
        scratch += small_sum_scratch(count, width)
    return pl.pallas_call(
        functools.partial(attention_backward_kernel, layer, count, split, last),
        out_shape=outs,
        in_specs=[VM, ANY, ANY, ANY] + [ANY] * 8 + [SM] + ([ANY, ANY, VM, VM] if split else []),
        out_specs=out_specs,
        scratch_shapes=scratch,
        compiler_params=params(7 + layer),
        name="attention_bwd",
    )(low, du, wout, wqkv, *saved, prefix, *extra)


def results_kernel(depth, *refs):
    refs = Refs(refs)
    state_in, grad_in = refs.take(2)
    attn, up, down = refs.take(2), refs.take(2), refs.take(2)
    tail, smalls = refs.one(), refs.take(2)
    state, grad, wqkv, bias_qv, wout, bias_out, gain, shift, wup, bias_up, wdown, bias_down = refs.take(12)
    state[...] = state_in[...]
    grad[...] = grad_in[...]
    for layer in range(2):
        wout[layer] = attn[layer][:, :depth].T
        for kind in range(3):
            wqkv[layer, kind] = attn[layer][:, (kind + 1) * depth : (kind + 2) * depth]
        wup[layer] = up[layer][...]
        wdown[layer] = down[layer][...].T
        sums = smalls[layer]
        row = slice(layer, layer + 1)
        bias_down[row] = sums[0:1]
        gain[layer, 1:2] = sums[1:2]
        shift[layer, 1:2] = sums[2:3]
        gain[layer, 0:1] = sums[3:4]
        shift[layer, 0:1] = sums[4:5]
        bias_out[row] = sums[5:6]
        bias_up[row] = sums[6:7]
        biases = tail if layer == 0 else smalls[0]
        for kind in range(2):
            bias_qv[layer, kind : kind + 1] = biases[7:8, kind * depth : (kind + 1) * depth]


def results(state, grad, attn, up, down, tail, smalls, depth):
    rows, width = state.shape
    share, units = up[0].shape
    layers = len(attn)
    return pl.pallas_call(
        functools.partial(results_kernel, depth),
        out_shape=[
            shape((rows, width)), shape((rows, width)), shape((layers, 3, share, depth)),
            shape((layers, 2, depth)), shape((layers, depth, share)), shape((layers, width)),
            shape((layers, 2, width)), shape((layers, 2, width)), shape((layers, share, units)),
            shape((layers, units)), shape((layers, units, share)), shape((layers, width)),
        ],
        in_specs=[VM] * 11,
        out_specs=[VM] * 12,
        compiler_params=pltpu.CompilerParams(vmem_limit_bytes=VMEM_BYTES),
        name="results",
    )(state, grad, *attn, *up, *down, tail, *smalls)


def local(
    tokens,
    cotangent,
    prefix,
    w_qkv,
    bias_qv,
    w_out,
    bias_out,
    norm_gain,
    norm_bias,
    w_up,
    bias_up,
    w_down,
    bias_down,
):
    width = tokens.shape[1]
    layer_count = w_qkv.shape[0]
    depth = w_out.shape[1]
    state, low = tokens, tokens
    stored = []
    for layer in range(layer_count):
        state, low, normal1, recip1, *saved = attention_layer(
            layer, state, low, w_qkv, bias_qv, w_out, bias_out, norm_gain, norm_bias, prefix
        )
        state, low, normal2, recip2, normed, active, slope = ffn_layer(
            layer, state, low, w_up, bias_up, w_down, bias_down, norm_gain, norm_bias
        )
        stored.append(((normal2, recip2), (active, slope, normed, normal1, recip1), saved))
    count = lax.axis_size("dp")
    split = count > 2 and count % 2 == 0 and (width // count) % 16 == 0
    grad = cotangent
    bias = jnp.zeros((8, width), F32)
    earlier = None
    attn, up, down, smalls, biases = [], [], [], [], []
    for layer in reversed(range(layer_count)):
        second, middle, saved = stored[layer]
        du, low, up_grad, down_grad, small, *sums = ffn_layer_back(
            layer, count, split, grad, *second, norm_gain, w_down, w_up, *middle, earlier
        )
        attn = (sums + attn) if split else attn
        extra = (up_grad, down_grad, small, bias) if split else ()
        grad, earlier, bias, *sums = attention_layer_back(
            layer, count, split, low, du, w_out, w_qkv, saved, prefix, extra
        )
        if split:
            up.insert(0, sums[0])
            down.insert(0, sums[1])
            smalls.insert(0, sums[2])
            if layer == 0:
                attn.insert(0, sums[3])
                return results(state, grad, attn, up, down, sums[4], smalls, depth)
            continue
        attn.insert(0, earlier)
        up.insert(0, up_grad)
        down.insert(0, down_grad)
        smalls.insert(0, small)
        biases.insert(0, bias[7, : 2 * depth].reshape(2, depth))
    scatter = functools.partial(lax.psum_scatter, axis_name="dp", scatter_dimension=1, tiled=True)
    attn_sum, up_sum, down_sum = [scatter(jnp.stack(each)) for each in (attn, up, down)]
    shared = lax.psum(jnp.stack(smalls)[:, :6], ("dp", "tensor"))
    bias_qv_sum, bias_up_sum = lax.psum((jnp.stack(biases), jnp.stack(smalls)[:, 6]), "dp")
    share = attn_sum.shape[1]
    return (
        state,
        grad,
        jnp.moveaxis(attn_sum[:, :, depth:].reshape(layer_count, share, 3, depth), 2, 1),
        bias_qv_sum,
        jnp.swapaxes(attn_sum[:, :, :depth], 1, 2),
        shared[:, 5],
        jnp.stack([shared[:, 3], shared[:, 1]], axis=1),
        jnp.stack([shared[:, 4], shared[:, 2]], axis=1),
        up_sum,
        bias_up_sum,
        jnp.swapaxes(down_sum, 1, 2),
        shared[:, 0],
    )


def solution(mesh):
    in_specs = (
        P(("dp", "tensor"), None),
        P(("dp", "tensor"), None),
        P("dp"),
        P(None, None, None, "tensor"),
        P(None, None, "tensor"),
        P(None, "tensor", None),
        P(),
        P(),
        P(),
        P(None, None, "tensor"),
        P(None, "tensor"),
        P(None, "tensor", None),
        P(),
    )
    out_specs = (
        P(("dp", "tensor"), None),
        P(("dp", "tensor"), None),
        P(None, None, "dp", "tensor"),
        P(None, None, "tensor"),
        P(None, "tensor", "dp"),
        P(),
        P(),
        P(),
        P(None, "dp", "tensor"),
        P(None, "tensor"),
        P(None, "tensor", "dp"),
        P(),
    )
    return jax.shard_map(local, mesh=mesh, in_specs=in_specs, out_specs=out_specs, check_vma=False)
```

```python
import functools
import math

import jax
import jax.numpy as jnp
from jax import lax
from jax.experimental import pallas as pl
from jax.experimental.pallas import tpu as pltpu
from jax.sharding import PartitionSpec as P

HDIM = 64
LEN = 1024
MEM = 10
LANES = 128
GROUP = 4
EPSILON = 1e-06
VMEM_BYTES = 62 * 1024 * 1024
HIGHEST = lax.Precision.HIGHEST
MESH = pl.DeviceIdType.MESH
F32 = jnp.float32
BF16 = jnp.bfloat16
VM = pl.BlockSpec(memory_space=pltpu.VMEM)
SM = pl.BlockSpec(memory_space=pltpu.SMEM)
ANY = pl.BlockSpec(memory_space=pl.ANY)


def dot(left, right):
    return jnp.dot(left, right, preferred_element_type=F32)


def dot_nt(left, right):
    return lax.dot_general(left, right, (((1,), (1,)), ((), ())), preferred_element_type=F32)


def remote(src, dst, send_sem, recv_sem, tensor_index):
    return pltpu.make_async_remote_copy(
        src_ref=src,
        dst_ref=dst,
        send_sem=send_sem,
        recv_sem=recv_sem,
        device_id={"tensor": tensor_index},
        device_id_type=MESH,
    )


def places():
    mine = lax.axis_index("tensor")
    chip = mine // 2
    core = mine - 2 * chip
    partner = mine + 1 - 2 * core
    across = mine + 2 - 4 * chip
    diagonal = across + 1 - 2 * core
    return mine, partner, across, diagonal


class Refs:
    def __init__(self, refs):
        self.refs = list(refs)

    def take(self, count):
        taken, self.refs = self.refs[:count], self.refs[count:]
        return taken

    def one(self):
        return self.take(1)[0]


class Moves:
    def __init__(self, sems):
        self.sems, self.used, self.pending = sems, 0, []

    def start(self, source, target):
        move = pltpu.make_async_copy(source, target, self.sems.at[self.used])
        self.used += 1
        move.start()
        return move

    def store(self, source, target):
        self.pending.append(self.start(source, target))

    def finish(self):
        for move in self.pending:
            move.wait()


def remote_dp(src, dst, send_sem, recv_sem, dp_index):
    return pltpu.make_async_remote_copy(
        src_ref=src,
        dst_ref=dst,
        send_sem=send_sem,
        recv_sem=recv_sem,
        device_id={"dp": dp_index},
        device_id_type=MESH,
    )


class Sequences:
    def __init__(self, count):
        self.pairs = count // 2
        self.index = lax.axis_index("dp")
        self.pair = self.index // 2
        self.side = self.index - 2 * self.pair
        self.neighbour = self.index + 1 - 2 * self.side

    def other_pair(self, offset):
        return lax.rem(self.pair + offset, self.pairs)

    def peer(self, offset):
        return 2 * self.other_pair(offset) + self.side

    def everyone(self):
        return [self.neighbour] + [self.peer(offset) for offset in range(1, self.pairs)]


class Entry:
    def __init__(self, sequences=None):
        barrier = pltpu.get_barrier_semaphore()
        group = places()[1:]
        others = sequences.everyone() if sequences is not None else []
        for other in group:
            pl.semaphore_signal(barrier, inc=1, device_id={"tensor": other}, device_id_type=MESH)
        for other in others:
            pl.semaphore_signal(barrier, inc=1, device_id={"dp": other}, device_id_type=MESH)
        self.barrier, self.count = barrier, len(group) + len(others)

    def wait(self):
        pl.semaphore_wait(self.barrier, self.count)


class Gather:
    def __init__(self, whole, send_sems, recv_sems, pieces):
        self.whole = whole
        self.pieces = pieces
        self.mine, self.partner, self.across, self.diagonal = places()
        self.rows = whole.shape[1] // pieces
        self.send_sems, self.recv_sems = send_sems, recv_sems

    def piece(self, chunk, part):
        return self.whole.at[chunk, pl.ds(part * self.rows, self.rows)]

    def to_partner(self):
        return remote(
            self.whole.at[self.mine], self.whole.at[self.mine],
            self.send_sems.at[0], self.recv_sems.at[0], self.partner,
        )

    def to_across(self, part):
        return remote(
            self.piece(self.mine, part), self.piece(self.mine, part),
            self.send_sems.at[1 + part], self.recv_sems.at[1 + part], self.across,
        )

    def onward(self, part):
        return remote(
            self.piece(self.across, part), self.piece(self.across, part),
            self.send_sems.at[1 + self.pieces + part], self.recv_sems.at[1 + self.pieces + part], self.partner,
        )

    def start(self):
        for part in range(self.pieces):
            self.to_across(part).start()
        self.to_partner().start()

    def wait_partner(self):
        remote(
            self.whole.at[self.partner], self.whole.at[self.partner],
            self.send_sems.at[0], self.recv_sems.at[0], self.partner,
        ).wait_recv()

    def wait_across(self, part):
        remote(
            self.piece(self.across, part), self.piece(self.across, part),
            self.send_sems.at[1 + part], self.recv_sems.at[1 + part], self.across,
        ).wait_recv()

    def wait_diagonal(self, part):
        remote(
            self.piece(self.diagonal, part), self.piece(self.diagonal, part),
            self.send_sems.at[1 + self.pieces + part], self.recv_sems.at[1 + self.pieces + part], self.partner,
        ).wait_recv()

    def wait_sends(self):
        self.to_partner().wait_send()
        for part in range(self.pieces):
            self.to_across(part).wait_send()
            self.onward(part).wait_send()


ATTN_PIECES = 2
FFN_PIECES = 4
BACK_PIECES = 2


def gather_sems(pieces):
    return [dma_sems(1 + 2 * pieces), dma_sems(1 + 2 * pieces)]


def shape(dims, kind=F32):
    return jax.ShapeDtypeStruct(dims, kind)


def dma_sems(*dims):
    return pltpu.SemaphoreType.DMA(dims)


def params(collective_id):
    return pltpu.CompilerParams(
        collective_id=collective_id, has_side_effects=True, vmem_limit_bytes=VMEM_BYTES
    )


def layer_norm(total, gain, shift):
    row_mean = jnp.mean(total, axis=-1, keepdims=True)
    centered = total - row_mean
    spread = jnp.mean(centered * centered, axis=-1, keepdims=True)
    recip = lax.rsqrt(spread + EPSILON)
    normal = centered * recip
    return normal * gain + shift, normal, recip


def visible_keys(chunk, rows):
    first, last = chunk * rows, (chunk + 1) * rows - 1
    if first < MEM or last >= LEN - MEM:
        return LEN
    return max(last + 1, LEN // 2)


def query_limits(chunk, rows, prefix_len):
    spots = chunk * rows + lax.broadcasted_iota(jnp.int32, (1, rows), 1)
    limits = jnp.maximum(spots, prefix_len - 1)
    return jnp.where((spots < MEM) | (spots >= LEN - MEM), LEN - 1, limits)


def transposed(values):
    return values.astype(F32).T


def head_pairs(values, heads):
    wide = []
    for head in range(heads):
        columns = values[:, head * HDIM : (head + 1) * HDIM]
        wide.append(jnp.concatenate([columns, columns], axis=1))
    return wide


class Exchange:
    def __init__(self, terms, near, relay, total, far, sems, pieces):
        self.terms, self.near, self.relay, self.total, self.far = terms, near, relay, total, far
        self.n_send, self.n_recv, self.r_send, self.r_recv, self.f_send, self.f_recv = sems
        self.mine, self.partner, self.across, self.diagonal = places()
        self.pieces = pieces
        self.rows = terms.shape[1] // pieces

    def spot(self, part):
        return pl.ds(part * self.rows, self.rows)

    def near_copy(self, part):
        return remote(
            self.terms.at[self.partner, self.spot(part)], self.near.at[self.spot(part)],
            self.n_send.at[part], self.n_recv.at[part], self.partner,
        )

    def relay_copy(self, part):
        return remote(
            self.terms.at[self.diagonal, self.spot(part)], self.relay.at[self.spot(part)],
            self.r_send.at[part], self.r_recv.at[part], self.partner,
        )

    def far_copy(self, part):
        return remote(
            self.total.at[self.spot(part)], self.far.at[self.spot(part)],
            self.f_send.at[part], self.f_recv.at[part], self.across,
        )

    def pass_on(self, part):
        spot = self.spot(part)
        self.relay_copy(part).wait_recv()
        self.total[spot] = (self.terms[self.across, spot] + self.relay[spot]).astype(self.total.dtype)
        self.far_copy(part).start()

    def result(self, part):
        spot = self.spot(part)
        self.near_copy(part).wait_recv()
        self.far_copy(part).wait_recv()
        return (self.terms[self.mine, spot] + self.near[spot]) + self.far[spot].astype(F32)

    def wait_sends(self):
        for part in range(self.pieces):
            self.near_copy(part).wait_send()
            self.relay_copy(part).wait_send()
            self.far_copy(part).wait_send()


def exchange_scratch(rows, width, kind, pieces):
    return [
        pltpu.VMEM((GROUP, rows, width), F32),
        pltpu.VMEM((rows, width), F32), pltpu.VMEM((rows, width), F32),
        pltpu.VMEM((rows, width), kind), pltpu.VMEM((rows, width), kind),
    ] + [dma_sems(pieces)] * 6


def attention_forward_kernel(layer, *refs):
    refs = Refs(refs)
    state_hbm, low_ref, wqkv_hbm, bias_ref, wout_hbm, bias_out_ref, gain_ref, shift_ref, prefix_ref = refs.take(9)
    next_ref, next_low_ref, normal_ref, recip_ref = refs.take(4)
    saved_hbm = refs.take(8)
    saved = refs.take(8)
    whole_ref, qt_ref, q2_ref, kz_ref, kt_ref, v2_ref, ct_ref, stats_ref = saved
    state_ref, wqkv_ref, vt_ref, cf_ref, wo_ref = refs.take(5)
    moves = Moves(refs.one())
    g_send, g_recv, c_send, c_recv, w_send, w_recv = refs.take(6)
    mine, partner, across, diagonal = places()
    rows = low_ref.shape[0]
    heads = qt_ref.shape[0]
    root = 1.0 / math.sqrt(HDIM)
    entry = Entry()
    wqkv_in = moves.start(wqkv_hbm.at[layer], wqkv_ref)
    wout_in = moves.start(wout_hbm.at[layer], wo_ref.at[mine])
    state_in = moves.start(state_hbm, state_ref)
    gather = Gather(whole_ref, g_send, g_recv, ATTN_PIECES)
    whole_ref[mine] = low_ref[...]
    entry.wait()
    gather.start()
    lane_low = lax.broadcasted_iota(jnp.int32, (rows, LANES), 1) < HDIM

    def project(chunk):
        spots = pl.ds(pl.multiple_of(chunk * rows, rows), rows)
        values = whole_ref[chunk]
        query = (dot(values, wqkv_ref[0]) + bias_ref[layer, 0:1]) * root
        key = dot(values, wqkv_ref[1])
        value = dot(values, wqkv_ref[2]) + bias_ref[layer, 1:2]
        queries, keys, valuess = [head_pairs(each, heads) for each in (query, key, value)]
        query_t, key_t, value_t = [each.T.astype(BF16) for each in (query, key, value)]
        for head in range(heads):
            part = slice(head * HDIM, (head + 1) * HDIM)
            q2_ref[head, spots] = queries[head].astype(BF16)
            kz_ref[head, spots] = jnp.where(lane_low, keys[head], 0.0).astype(BF16)
            v2_ref[head, spots] = valuess[head].astype(BF16)
            for half in (slice(0, HDIM), slice(HDIM, 2 * HDIM)):
                qt_ref[head, half, spots] = query_t[part]
                kt_ref[head, half, spots] = key_t[part]
            vt_ref[head, :, spots] = value_t[part]

    def wout_to_partner(source):
        slot = 0 if source is mine else 2
        return remote(wo_ref.at[source], wo_ref.at[source], w_send.at[slot], w_recv.at[slot], partner)

    wout_to_across = remote(wo_ref.at[mine], wo_ref.at[mine], w_send.at[1], w_recv.at[1], across)
    wout_from_across = remote(wo_ref.at[across], wo_ref.at[across], w_send.at[1], w_recv.at[1], across)
    wout_from_partner = remote(wo_ref.at[partner], wo_ref.at[partner], w_send.at[0], w_recv.at[0], partner)
    wout_from_diagonal = remote(wo_ref.at[diagonal], wo_ref.at[diagonal], w_send.at[2], w_recv.at[2], partner)

    wqkv_in.wait()
    project(mine)
    gather.wait_partner()
    project(partner)
    wout_in.wait()
    for part in range(ATTN_PIECES):
        gather.wait_across(part)
        gather.onward(part).start()
    wout_to_across.start()
    wout_to_partner(mine).start()
    project(across)
    for part in range(ATTN_PIECES):
        gather.wait_diagonal(part)
    project(diagonal)
    for source, target in zip(saved[:6], saved_hbm[:6]):
        moves.store(source, target)

    def context_copy(step, chunk):
        return remote(ct_ref.at[chunk], cf_ref.at[mine], c_send.at[step], c_recv.at[step], chunk)

    def context_from(step, chunk):
        return remote(ct_ref.at[mine], cf_ref.at[chunk], c_send.at[step], c_recv.at[step], chunk)

    def attend(chunk):
        keys = visible_keys(chunk, rows)
        limits = query_limits(chunk, rows, prefix_ref[0])
        visible = lax.broadcasted_iota(jnp.int32, (keys, rows), 0) <= limits
        spots = pl.ds(chunk * rows, rows)

        def one_head(head, carry):
            scores = dot(kz_ref[head, pl.ds(0, keys)], qt_ref[head, :, spots])
            scores = jnp.where(visible, scores, -1e30)
            top = jnp.max(scores, axis=0, keepdims=True)
            expo = jnp.exp(scores - top)
            recip = 1.0 / jnp.sum(expo, axis=0, keepdims=True)
            probs = (expo * recip).astype(BF16)
            context = dot(vt_ref[head, :, pl.ds(0, keys)], probs)
            ct_ref[chunk, pl.ds(pl.multiple_of(head * HDIM, HDIM), HDIM)] = context.astype(BF16)
            first = lax.broadcasted_iota(jnp.int32, (8, rows), 0) == 0
            stats_ref[head, :, spots] = jnp.where(first, top, recip)
            return carry

        lax.fori_loop(0, heads, one_head, 0)

    chip, core = mine // 2, mine - 2 * (mine // 2)

    def one_step(step, carry):
        near = step // 2
        flip = lax.rem(lax.rem(step, 2) + near, 2)
        to_chip = (1 - near) * (1 - chip) + near * chip
        chunk = 2 * to_chip + core + flip * (1 - 2 * core)
        for each in range(GROUP):
            @pl.when(chunk == each)
            def _():
                attend(each)

        @pl.when(step < 3)
        def _():
            context_copy(step, chunk).start()

        @pl.when(step == 1)
        def _():
            wout_from_across.wait_recv()
            wout_to_partner(across).start()
        return carry

    lax.fori_loop(0, GROUP, one_step, 0)
    for source, target in zip(saved[6:], saved_hbm[6:]):
        moves.store(source, target)
    cf_ref[mine] = ct_ref[mine]
    wout_from_partner.wait_recv()
    wout_from_diagonal.wait_recv()
    for step, chunk in enumerate((across, diagonal, partner)):
        context_from(step, chunk).wait_recv()
    depth = GROUP * wo_ref.shape[1]
    context = transposed(cf_ref[...].reshape(depth, rows)).astype(BF16)
    state_in.wait()
    total = (
        state_ref[...].astype(F32) + dot(context, wo_ref[...].reshape(depth, -1)) + bias_out_ref[layer : layer + 1]
    )
    result, normal, recip = layer_norm(total, gain_ref[layer, 0:1], shift_ref[layer, 0:1])
    next_ref[...] = result
    next_low_ref[...] = result.astype(BF16)
    normal_ref[...] = normal
    recip_ref[...] = jnp.broadcast_to(recip, recip_ref.shape)
    gather.wait_sends()
    wout_to_across.wait_send()
    wout_to_partner(mine).wait_send()
    wout_to_partner(across).wait_send()
    for step, chunk in enumerate((across, diagonal, partner)):
        context_copy(step, chunk).wait_send()
    moves.finish()


def attention_layer(layer, state, low, wqkv, bias, wout, bias_out, gain, shift, prefix):
    rows, width = low.shape
    depth = wout.shape[1]
    heads = depth // HDIM
    tall = GROUP * rows
    saved = [
        ((GROUP, rows, width), BF16),
        ((heads, LANES, tall), BF16), ((heads, tall, LANES), BF16), ((heads, tall, LANES), BF16),
        ((heads, LANES, tall), BF16), ((heads, tall, LANES), BF16), ((GROUP, depth, rows), BF16),
        ((heads, 8, tall), F32),
    ]
    return pl.pallas_call(
        functools.partial(attention_forward_kernel, layer),
        out_shape=[
            shape((rows, width)), shape((rows, width), BF16), shape((rows, width)), shape((rows, LANES)),
        ] + [shape(*each) for each in saved],
        in_specs=[ANY, VM, ANY, VM, ANY, VM, VM, VM, SM],
        out_specs=[VM] * 4 + [ANY] * 8,
        scratch_shapes=[pltpu.VMEM(*each) for each in saved] + [
            pltpu.VMEM((rows, width), state.dtype),
            pltpu.VMEM(wqkv.shape[1:], BF16),
            pltpu.VMEM((heads, HDIM, tall), BF16),
            pltpu.VMEM((GROUP, depth, rows), BF16),
            pltpu.VMEM((GROUP, depth, width), BF16),
            dma_sems(11),
            *gather_sems(ATTN_PIECES),
            dma_sems(3), dma_sems(3), dma_sems(3), dma_sems(3),
        ],
        compiler_params=params(1 + layer),
        name="attention_fwd",
    )(state, low, wqkv, bias, wout, bias_out, gain, shift, prefix)


def ffn_forward_kernel(layer, *refs):
    refs = Refs(refs)
    state_hbm, low_ref, wup_hbm, bias_up_ref, wdown_hbm, bias_down_ref, gain_ref, shift_ref = refs.take(8)
    next_ref, next_low_ref, normal_ref, recip_ref = refs.take(4)
    saved_hbm = refs.take(3)
    whole_ref, active_ref, slope_ref = refs.take(3)
    state_ref, wup_ref, wdown_ref = refs.take(3)
    moves = Moves(refs.one())
    exchange_refs = refs.take(11)
    g_send, g_recv = refs.take(2)
    mine, partner, across, diagonal = places()
    rows = low_ref.shape[0]
    part_rows = rows // FFN_PIECES
    entry = Entry()
    wup_in = moves.start(wup_hbm.at[layer], wup_ref)
    wdown_in = moves.start(wdown_hbm.at[layer], wdown_ref)
    state_in = moves.start(state_hbm, state_ref)
    gather = Gather(whole_ref, g_send, g_recv, FFN_PIECES)
    whole_ref[mine] = low_ref[...]
    entry.wait()
    gather.start()
    exchange = Exchange(*exchange_refs[:5], exchange_refs[5:], FFN_PIECES)
    terms_ref = exchange.terms

    def units(chunk, part):
        spot = exchange.spot(part)
        hidden = dot(whole_ref[chunk, spot], wup_ref[...]) + bias_up_ref[layer : layer + 1]
        below = 0.5 * (1.0 + lax.erf(hidden * math.sqrt(0.5)))
        density = jnp.exp(-0.5 * hidden * hidden) * (1.0 / math.sqrt(2.0 * math.pi))
        active = (hidden * below).astype(BF16)
        active_ref[chunk, spot] = active
        slope_ref[chunk, spot] = below + hidden * density
        terms_ref[chunk, spot] = dot(active, wdown_ref[...])

    wup_in.wait()
    wdown_in.wait()
    for part in range(FFN_PIECES):
        units(mine, part)
    for part in range(FFN_PIECES):
        gather.wait_across(part)
        gather.onward(part).start()
        units(across, part)
        gather.wait_diagonal(part)
        units(diagonal, part)
        exchange.relay_copy(part).start()
        if part > 0:
            exchange.pass_on(part - 1)
    gather.wait_partner()
    moves.store(whole_ref, saved_hbm[0])
    units(partner, 0)
    exchange.near_copy(0).start()
    exchange.pass_on(FFN_PIECES - 1)
    for part in range(1, FFN_PIECES):
        units(partner, part)
        exchange.near_copy(part).start()
    moves.store(active_ref, saved_hbm[1])
    moves.store(slope_ref, saved_hbm[2])
    state_in.wait()
    for part in range(FFN_PIECES):
        spot = exchange.spot(part)
        total = state_ref[spot] + exchange.result(part) + bias_down_ref[layer : layer + 1]
        result, normal, recip = layer_norm(total, gain_ref[layer, 1:2], shift_ref[layer, 1:2])
        next_ref[spot] = result
        next_low_ref[spot] = result.astype(BF16)
        normal_ref[spot] = normal
        recip_ref[spot] = jnp.broadcast_to(recip, (part_rows, LANES))
    gather.wait_sends()
    exchange.wait_sends()
    moves.finish()


def ffn_layer(layer, state, low, wup, bias_up, wdown, bias_down, gain, shift):
    rows, width = low.shape
    units = wup.shape[2]
    saved = [((GROUP, rows, width), BF16), ((GROUP, rows, units), BF16), ((GROUP, rows, units), F32)]
    return pl.pallas_call(
        functools.partial(ffn_forward_kernel, layer),
        out_shape=[
            shape((rows, width)), shape((rows, width), BF16), shape((rows, width)), shape((rows, LANES)),
        ] + [shape(*each) for each in saved],
        in_specs=[ANY, VM, ANY, VM, ANY, VM, VM, VM],
        out_specs=[VM] * 4 + [ANY] * 3,
        scratch_shapes=[pltpu.VMEM(*each) for each in saved]
        + [
            pltpu.VMEM((rows, width), F32), pltpu.VMEM(wup.shape[1:], BF16), pltpu.VMEM(wdown.shape[1:], BF16),
            dma_sems(6),
        ]
        + exchange_scratch(rows, width, F32, FFN_PIECES)
        + gather_sems(FFN_PIECES),
        compiler_params=params(3 + layer),
        name="ffn_fwd",
    )(state, low, wup, bias_up, wdown, bias_down, gain, shift)


def layer_norm_back(grad_in, normal, recip, gain):
    scaled = grad_in * gain
    inner = (
        scaled
        - jnp.mean(scaled, axis=-1, keepdims=True)
        - normal * jnp.mean(scaled * normal, axis=-1, keepdims=True)
    )
    return recip * inner


def column_sum(values):
    return jnp.sum(values, axis=0, keepdims=True)


def high_low(values):
    high = values.astype(BF16)
    return high, (values - high.astype(F32)).astype(BF16)


def dot_tn(left, right):
    return lax.dot_general(left, right, (((0,), (0,)), ((), ())), preferred_element_type=F32)


def owner_rows(pair, side, rows):
    return pl.ds(pl.multiple_of((2 * pair + side) * rows, 16), rows)


class PairSum:
    def __init__(self, sequences, source, columns, buffers, sems):
        self.at, self.source, self.columns = sequences, source, columns
        self.out, self.into = buffers
        self.sems = sems
        self.rows = self.out.shape[1]

    def copy(self):
        return remote_dp(
            self.out.at[:, :, self.columns], self.into.at[:, :, self.columns], *self.sems, self.at.neighbour
        )

    def start(self):
        for pair in range(self.at.pairs):
            place = (owner_rows(pair, 1 - self.at.side, self.rows), self.columns)
            self.out[pair, :, self.columns] = self.source[place].astype(BF16)
        self.copy().start()

    def finish(self):
        self.copy().wait_recv()
        for pair in range(self.at.pairs):
            place = (owner_rows(pair, self.at.side, self.rows), self.columns)
            self.source[place] = self.source[place] + self.into[pair, :, self.columns].astype(F32)

    def wait_sends(self):
        self.copy().wait_send()


class OwnerSum:
    def __init__(self, sequences, source, result, columns, buffers, sems):
        self.at, self.source, self.result, self.columns = sequences, source, result, columns
        self.out, self.into = buffers
        self.sems = sems
        self.rows = result.shape[0]

    def terms(self, pair):
        return self.source[owner_rows(pair, self.at.side, self.rows), self.columns]

    def copy(self, offset):
        return remote_dp(
            self.out.at[offset - 1, :, self.columns], self.into.at[offset - 1, :, self.columns],
            self.sems[0].at[offset - 1], self.sems[1].at[offset - 1], self.at.peer(offset),
        )

    def start(self):
        for offset in range(1, self.at.pairs):
            pair = self.at.other_pair(offset)
            self.out[offset - 1, :, self.columns] = self.terms(pair).astype(BF16)
            self.copy(offset).start()

    def finish(self):
        total = self.terms(self.at.pair)
        for offset in range(1, self.at.pairs):
            self.copy(offset).wait_recv()
            total = total + self.into[offset - 1, :, self.columns].astype(F32)
        self.result[:, self.columns] = total

    def wait_sends(self):
        for offset in range(1, self.at.pairs):
            self.copy(offset).wait_send()


def halves(columns):
    return (slice(0, columns // 2), slice(columns // 2, columns))


def tile_blocks(columns):
    tiles = columns // LANES
    ends = [0, 1, 1 + (tiles - 1) * 2 // 5, 1 + (tiles - 1) * 4 // 5, tiles]
    return [slice(first * LANES, end * LANES) for first, end in zip(ends, ends[1:])]


def pair_scratch(count, width, columns, blocks):
    dims = (count // 2, width // count, columns)
    return [pltpu.VMEM(dims, BF16), pltpu.VMEM(dims, BF16), dma_sems(blocks), dma_sems(blocks)]


def owner_scratch(count, width, columns, blocks):
    pairs = count // 2
    dims = (pairs - 1, width // count, columns)
    return [
        pltpu.VMEM(dims, BF16), pltpu.VMEM(dims, BF16), dma_sems(blocks, pairs - 1), dma_sems(blocks, pairs - 1)
    ]


def total_scratch(count, width, columns, blocks):
    return pair_scratch(count, width, columns, blocks) + owner_scratch(count, width, columns, blocks)


def total_sums(sequences, source, result, scratch, blocks):
    first_out, first_in, n_send, n_recv, second_out, second_in, p_send, p_recv = scratch
    sums = []
    for block, columns in enumerate(blocks):
        pair = PairSum(sequences, source, columns, (first_out, first_in), (n_send.at[block], n_recv.at[block]))
        owner = OwnerSum(
            sequences, source, result, columns, (second_out, second_in), (p_send.at[block], p_recv.at[block])
        )
        sums.append(BlockSum(pair, owner))
    return sums


TOTAL_REFS = 8


class BlockSum:
    def __init__(self, pair, owner):
        self.pair, self.owner = pair, owner
        self.start, self.finish = pair.start, owner.finish

    def turn(self):
        self.pair.finish()
        self.owner.start()

    def wait_sends(self):
        self.pair.wait_sends()
        self.owner.wait_sends()


class SmallSum:
    def __init__(self, sequences, source, result, shared_rows, slots, sems):
        self.at = sequences
        self.source, self.result, self.shared_rows = source, result, shared_rows
        self.group_slots, self.side_slots, self.pair_slots = slots
        self.g_send, self.g_recv, self.s_send, self.s_recv, self.p_send, self.p_recv = sems
        self.mine, self.partner, self.across, self.diagonal = places()

    def group_copy(self, index, to, slot):
        return remote(
            self.group_slots.at[slot], self.group_slots.at[slot],
            self.g_send.at[index], self.g_recv.at[index], to,
        )

    def start(self):
        if self.shared_rows:
            self.group_slots[self.mine] = self.source[...]
            for index, other in enumerate((self.partner, self.across, self.diagonal)):
                self.group_copy(index, other, self.mine).start()

    def side_copy(self, slot):
        return remote_dp(
            self.side_slots.at[slot], self.side_slots.at[slot],
            self.s_send.at[0], self.s_recv.at[0], self.at.neighbour,
        )

    def first(self):
        values = self.source[...]
        if self.shared_rows:
            for index, other in enumerate((self.partner, self.across, self.diagonal)):
                self.group_copy(index, other, other).wait_recv()
            total = self.group_slots[0]
            for slot in range(1, GROUP):
                total = total + self.group_slots[slot]
            shared = lax.broadcasted_iota(jnp.int32, values.shape, 0) < self.shared_rows
            values = jnp.where(shared, total, values)
        self.side_slots[self.at.side] = values
        self.side_copy(self.at.side).start()

    def pair_copy(self, offset, slot):
        return remote_dp(
            self.pair_slots.at[slot], self.pair_slots.at[slot],
            self.p_send.at[offset - 1], self.p_recv.at[offset - 1], self.at.peer(offset),
        )

    def second(self):
        self.side_copy(1 - self.at.side).wait_recv()
        self.pair_slots[self.at.pair] = self.side_slots[0] + self.side_slots[1]
        for offset in range(1, self.at.pairs):
            self.pair_copy(offset, self.at.pair).start()

    def third(self):
        for offset in range(1, self.at.pairs):
            self.pair_copy(offset, self.at.other_pair(self.at.pairs - offset)).wait_recv()
        total = self.pair_slots[0]
        for slot in range(1, self.at.pairs):
            total = total + self.pair_slots[slot]
        self.result[...] = total

    def wait_sends(self):
        if self.shared_rows:
            for index, other in enumerate((self.partner, self.across, self.diagonal)):
                self.group_copy(index, other, self.mine).wait_send()
        self.side_copy(self.at.side).wait_send()
        for offset in range(1, self.at.pairs):
            self.pair_copy(offset, self.at.pair).wait_send()


def small_sum_scratch(count, width):
    pairs = count // 2
    return [
        pltpu.VMEM((GROUP, 8, width), F32), pltpu.VMEM((2, 8, width), F32), pltpu.VMEM((pairs, 8, width), F32),
        dma_sems(3), dma_sems(3), dma_sems(1), dma_sems(1), dma_sems(pairs - 1), dma_sems(pairs - 1),
    ]


def layer_backward_kernel(layer, count, split, behind, last, *refs):
    refs = Refs(refs)
    grad_ref, normal2_ref, recip2_ref, gain_ref, recip1_ref = refs.take(5)
    wdown_hbm, wup_hbm, active_hbm, slope_hbm, normed_hbm, normal1_hbm, wout_hbm, wqkv_hbm = refs.take(8)
    whole_hbm, *saved_hbm = refs.take(8)
    prefix_ref = refs.one()
    earlier_hbm, bias_in = refs.take(2) if behind else (None,) * 2
    dx_ref, bias_ref = refs.take(2)
    grads_hbm = None if last else refs.one()
    up_out, down_out, smalls_out = refs.take(3)
    earlier_sum = refs.one() if behind else None
    grads_sum, bias_sum = refs.take(2) if last else (None,) * 2
    df_ref, do_ref, du_ref, high_ref, lowbits_ref = refs.take(5)
    wdown_ref, wup_ref, active_ref, wide_ref, normed_ref, normal1_ref = refs.take(6)
    up_ref, down_ref, grads_ref, smalls_ref = refs.take(4)
    saved = refs.take(7)
    qt_ref, q2_ref, kz_ref, kt_ref, v2_ref, ct_ref, stats_ref = saved
    wout_ref, wqkv_ref, wqkv_t_ref = refs.take(3)
    dc_ref, dct_ref, dv_ref, xt_ref = refs.take(4)
    moves = Moves(refs.one())
    exchange_refs = refs.take(11)
    first_sems, second_sems = refs.take(2), refs.take(2)
    mine, partner, across, diagonal = places()
    rows, width = grad_ref.shape
    units = wup_ref.shape[1]
    tall = GROUP * rows
    part_rows = rows // BACK_PIECES
    heads = qt_ref.shape[0]
    depth = heads * HDIM
    span = width // 3
    scale = 1.0 / math.sqrt(HDIM)
    sequences = Sequences(count) if split else None
    entry = Entry(sequences)
    wdown_in = moves.start(wdown_hbm.at[layer], wdown_ref)
    wup_in = moves.start(wup_hbm.at[layer], wup_ref)
    slope_in = [
        moves.start(slope_hbm.at[chunk], wide_ref.at[pl.ds(chunk * rows, rows)]) for chunk in range(GROUP)
    ]
    earlier, ups, downs, own, small, own_small = [], [], [], [], None, None
    if behind:
        earlier_in = moves.start(earlier_hbm, grads_ref)
        earlier = total_sums(sequences, grads_ref, earlier_sum, refs.take(TOTAL_REFS), halves(width))
    if split:
        downs = total_sums(sequences, down_ref, down_out, refs.take(TOTAL_REFS), halves(units))
        ups = total_sums(sequences, up_ref, up_out, refs.take(TOTAL_REFS), halves(units))
        small = SmallSum(sequences, smalls_ref, smalls_out, 6, refs.take(3), refs.take(6))
    if last:
        own = total_sums(sequences, grads_ref, grads_sum, refs.take(TOTAL_REFS), tile_blocks(width))
        own_small = SmallSum(sequences, bias_ref, bias_sum, 0, refs.take(3), refs.take(6))
    active_in = moves.start(active_hbm, active_ref)
    normed_in = moves.start(normed_hbm, normed_ref)
    normal1_in = moves.start(normal1_hbm, normal1_ref)
    wout_in = moves.start(wout_hbm.at[layer], wout_ref)
    wqkv_in = moves.start(wqkv_hbm.at[layer], wqkv_ref)
    saved_in = [moves.start(source, target) for source, target in zip(saved_hbm, saved)]
    first_gather = Gather(df_ref, *first_sems, BACK_PIECES)
    second_gather = Gather(do_ref, *second_sems, BACK_PIECES)
    exchange = Exchange(*exchange_refs[:5], exchange_refs[5:], BACK_PIECES)
    terms_ref = exchange.terms

    grad = grad_ref[...].astype(F32)
    normal2 = normal2_ref[...]
    du2 = layer_norm_back(grad, normal2, recip2_ref[:, :1], gain_ref[layer, 1:2])
    du_ref[...] = du2
    df_ref[mine] = du2.astype(BF16)
    entry.wait()
    first_gather.start()
    smalls_ref[0:1] = column_sum(du2)
    smalls_ref[1:2] = column_sum(grad * normal2)
    smalls_ref[2:3] = column_sum(grad)
    smalls_ref[6:7] = jnp.zeros((1, width), F32)
    smalls_ref[7:8] = bias_in[7:8] if behind else jnp.zeros((1, width), F32)
    wdown_in.wait()
    wdown_ref[...] = transposed(wdown_ref[...]).astype(BF16)
    wup_in.wait()
    wup_ref[...] = transposed(wup_ref[...]).astype(BF16)
    if behind:
        earlier_in.wait()
        for item in earlier:
            item.start()

    def part_spots(chunk, part):
        return pl.ds(pl.multiple_of(chunk * rows + part * part_rows, part_rows), part_rows)

    def back(chunk, part):
        spot, spots = exchange.spot(part), part_spots(chunk, part)
        grad_active = dot(df_ref[chunk, spot], wdown_ref[...])
        grad_hidden = grad_active * wide_ref[spots]
        smalls_ref[6:7] = smalls_ref[6:7] + column_sum(grad_hidden)
        high, low = high_low(grad_hidden)
        high_ref[spots] = high
        lowbits_ref[spots] = low
        terms_ref[chunk, spot] = dot(high, wup_ref[...]) + dot(low, wup_ref[...])

    for move in slope_in:
        move.wait()
    for part in range(BACK_PIECES):
        back(mine, part)
    for part in range(BACK_PIECES):
        first_gather.wait_across(part)
        first_gather.onward(part).start()
        back(across, part)
        first_gather.wait_diagonal(part)
        back(diagonal, part)
        exchange.relay_copy(part).start()
        if part > 0:
            exchange.pass_on(part - 1)
        if behind and part == 0:
            earlier[0].turn()
    first_gather.wait_partner()
    back(partner, 0)
    exchange.near_copy(0).start()
    exchange.pass_on(BACK_PIECES - 1)
    active_in.wait()
    down_ref[...] = dot_tn(df_ref[...].reshape(tall, width), active_ref[...].reshape(tall, units))
    for item in downs:
        item.start()
    for part in range(1, BACK_PIECES):
        back(partner, part)
        exchange.near_copy(part).start()
    if behind:
        earlier[1].turn()
    normed_in.wait()
    normed = normed_ref[...].reshape(tall, width)
    up_ref[...] = dot_tn(normed, high_ref[...]) + dot_tn(normed, lowbits_ref[...])
    for item in ups:
        item.start()
    whole_in = moves.start(whole_hbm, normed_ref)
    if not split:
        moves.store(down_ref, down_out)
        moves.store(up_ref, up_out)
    normal1_in.wait()
    for part in range(BACK_PIECES):
        spot = exchange.spot(part)
        grad_normed = exchange.result(part) + du_ref[spot]
        normal1 = normal1_ref[spot]
        du = layer_norm_back(grad_normed, normal1, recip1_ref[spot, :1], gain_ref[layer, 0:1])
        du_ref[spot] = du
        do_ref[mine, spot] = du.astype(BF16)
        second_gather.to_across(part).start()
        sums = (column_sum(grad_normed * normal1), column_sum(grad_normed), column_sum(du))
        for index, value in enumerate(sums):
            place = slice(3 + index, 4 + index)
            smalls_ref[place] = value if part == 0 else smalls_ref[place] + value
    second_gather.to_partner().start()
    if split:
        small.start()
    else:
        smalls_out[...] = smalls_ref[...]
    exchange.wait_sends()
    first_gather.wait_sends()

    lane_low = lax.broadcasted_iota(jnp.int32, (rows, LANES), 1) < HDIM
    wide_ref[:, width // 2 :] = jnp.zeros((tall, width // 2), F32)
    dv_ref[...] = jnp.zeros_like(dv_ref)

    def context_grad(chunk):
        spots = pl.ds(pl.multiple_of(chunk * rows, rows), rows)
        wide = head_pairs(dot_nt(do_ref[chunk], wout_ref[...]), heads)
        for head in range(heads):
            high = wide[head].astype(BF16).astype(F32)
            both = jnp.where(lane_low, high, wide[head] - high)
            dc_ref[head, spots] = both.astype(BF16)
            dct_ref[head, :, spots] = both.T.astype(BF16)

    def attend_back(chunk, head):
        keys = visible_keys(chunk, rows)
        limits = query_limits(chunk, rows, prefix_ref[0])
        visible = lax.broadcasted_iota(jnp.int32, (keys, rows), 0) <= limits
        spots = pl.ds(chunk * rows, rows)
        seen = pl.ds(0, keys)
        dq_lanes = pl.ds(pl.multiple_of(head * LANES, LANES), LANES)
        dk_lanes = pl.ds(pl.multiple_of((heads + head) * LANES, LANES), LANES)
        scores = dot(kz_ref[head, seen], qt_ref[head, :, spots])
        top = stats_ref[head, 0:1, spots]
        recip = stats_ref[head, 1:2, spots]
        probs = jnp.exp(jnp.where(visible, scores - top, -1e30)) * recip
        grad_probs = dot(v2_ref[head, seen], dct_ref[head, :, spots])
        inner = column_sum(probs * grad_probs)
        grad_scores = (probs * (grad_probs - inner)).astype(BF16)
        dv_ref[head, seen] = dv_ref[head, seen] + dot(probs.astype(BF16), dc_ref[head, spots])
        wide_ref[seen, dk_lanes] = wide_ref[seen, dk_lanes] + dot(grad_scores, q2_ref[head, spots])
        wide_ref[spots, dq_lanes] = dot(kt_ref[head, :, seen], grad_scores).T * scale

    chip, core = mine // 2, mine - 2 * (mine // 2)

    def weight_grad_out():
        out_wide = dot(ct_ref[0], do_ref[0])
        for chunk in range(1, GROUP):
            out_wide = out_wide + dot(ct_ref[chunk], do_ref[chunk])
        grads_ref[:, :depth] = out_wide.T

    def gathered(step):
        if step == 1:
            second_gather.wait_partner()
        if step == 2:
            for part in range(BACK_PIECES):
                second_gather.wait_across(part)
                second_gather.onward(part).start()
        if step == 3:
            for part in range(BACK_PIECES):
                second_gather.wait_diagonal(part)

    beside = {heads: [lambda: gathered(1)], 2 * heads: [lambda: gathered(2)], 3 * heads: [lambda: gathered(3)]}
    if split:
        beside[heads].append(downs[0].turn)
        beside[2 * heads].append(small.first)
        beside[2 * heads].append(downs[1].turn)
        beside[4 * heads - 1] = [ups[0].turn]
        for item in earlier:
            beside[2 * heads].append(item.finish)
    if last:
        beside[3 * heads] += [weight_grad_out, own[0].start]

    def one_turn(turn, carry):
        step = turn // heads
        head = lax.rem(turn, heads)
        near = 1 - step // 2
        flip = lax.rem(step, 2)
        to_chip = (1 - near) * (1 - chip) + near * chip
        chunk = 2 * to_chip + core + flip * (1 - 2 * core)
        for when in sorted(beside):
            @pl.when(turn == when)
            def _():
                for action in beside[when]:
                    action()

        @pl.when(head == 0)
        def _():
            context_grad(chunk)

        for each in range(GROUP):
            @pl.when(chunk == each)
            def _():
                attend_back(each, head)
        return carry

    wout_in.wait()
    wqkv_in.wait()
    for kind in range(3):
        wqkv_t_ref[kind] = transposed(wqkv_ref[kind]).astype(BF16)
    for move in saved_in:
        move.wait()
    lax.fori_loop(0, GROUP * heads, one_turn, 0)

    def kind_lanes(kind):
        return slice(kind * span, kind * span + depth)

    def pack_chunk(chunk, carry):
        spots = pl.ds(pl.multiple_of(chunk * rows, rows), rows)
        xt_ref[:, spots] = transposed(normed_ref[chunk]).astype(BF16)
        for kind in range(3):
            parts = []
            for head in range(heads):
                if kind < 2:
                    wide = wide_ref[spots, slice((kind * heads + head) * LANES, (kind * heads + head + 1) * LANES)]
                else:
                    wide = dv_ref[head, spots]
                    wide = wide + pltpu.roll(wide, HDIM, 1)
                parts.append(wide[:, :HDIM])
            values = jnp.concatenate(parts, axis=1)
            high, low = high_low(values)
            high_ref[spots, kind_lanes(kind)] = high
            lowbits_ref[spots, kind_lanes(kind)] = low
            if kind != 1:
                place = slice((kind // 2) * depth, (kind // 2 + 1) * depth)
                bias_ref[:, place] = bias_ref[:, place] + column_sum(values)
        return carry

    bias_ref[...] = jnp.zeros_like(bias_ref)
    whole_in.wait()
    lax.fori_loop(0, GROUP, pack_chunk, 0)

    def weight_grad(kind):
        place = slice((kind + 1) * depth, (kind + 2) * depth)
        lanes = kind_lanes(kind)
        grads_ref[:, place] = dot(xt_ref[...], high_ref[:, lanes]) + dot(xt_ref[...], lowbits_ref[:, lanes])

    def input_terms(chunk, part):
        spots = part_spots(chunk, part)
        total = None
        for kind in range(3):
            for values in (high_ref, lowbits_ref):
                term = dot(values[spots, kind_lanes(kind)], wqkv_t_ref[kind])
                total = term if total is None else total + term
        terms_ref[chunk, exchange.spot(part)] = total

    if last:
        own_small.first()
        weight_grad(0)
        own[1].start()
        weight_grad(1)
        weight_grad(2)
        own[2].start()
        own[3].start()
    for part in range(BACK_PIECES):
        input_terms(diagonal, part)
        exchange.relay_copy(part).start()
        input_terms(across, part)
        if part > 0:
            exchange.pass_on(part - 1)
    input_terms(partner, 0)
    exchange.near_copy(0).start()
    exchange.pass_on(BACK_PIECES - 1)
    for part in range(1, BACK_PIECES):
        input_terms(partner, part)
        exchange.near_copy(part).start()
    for part in range(BACK_PIECES):
        input_terms(mine, part)
    if split:
        ups[1].turn()
        small.second()
    if last:
        own[0].turn()
        own[1].turn()
        own[2].turn()
        own[3].turn()
        own_small.second()
    else:
        weight_grad_out()
        for kind in range(3):
            weight_grad(kind)
        moves.store(grads_ref, grads_hbm)
    for item in downs + ups:
        item.finish()
    for part in range(BACK_PIECES):
        spot = exchange.spot(part)
        dx_ref[spot] = exchange.result(part) + du_ref[spot]
    if split:
        small.third()
    if last:
        own_small.third()
        for item in own:
            item.finish()
    second_gather.wait_sends()
    exchange.wait_sends()
    for item in earlier + downs + ups + own:
        item.wait_sends()
    for item in (small, own_small):
        if item is not None:
            item.wait_sends()
    moves.finish()


def layer_back(layer, count, split, grad, normal2, recip2, gain, recip1, hbm, prefix, earlier):
    rows, width = grad.shape
    wdown, wup, active, slope, normed, normal1, wout, wqkv, *saved = hbm
    units, depth = wup.shape[2], wout.shape[1]
    heads = depth // HDIM
    tall = GROUP * rows
    share = width // count
    behind = split and earlier is not None
    last = split and layer == 0
    columns = 4 * depth
    if not (columns == width == units == 2 * heads * LANES):
        raise ValueError("unsupported sizes")
    outs, out_specs = [shape((rows, width)), shape((8, width))], [VM, VM]
    if not last:
        outs.append(shape((width, columns)))
        out_specs.append(ANY)
    outs += [shape((share if split else width, units))] * 2 + [shape((8, width))]
    out_specs += [VM, VM, VM] if split else [ANY, ANY, VM]
    if behind:
        outs.append(shape((share, columns)))
        out_specs.append(VM)
    if last:
        outs += [shape((share, columns)), shape((8, width))]
        out_specs += [VM, VM]
    whole_rows = pltpu.VMEM((GROUP, rows, width), BF16)
    square = pltpu.VMEM((width, units), F32)
    scratch = [
        whole_rows, whole_rows, pltpu.VMEM((rows, width), F32),
        pltpu.VMEM((tall, units), BF16), pltpu.VMEM((tall, units), BF16),
        pltpu.VMEM(wdown.shape[1:], BF16), pltpu.VMEM(wup.shape[1:], BF16), whole_rows,
        pltpu.VMEM((tall, units), F32), whole_rows, pltpu.VMEM((rows, width), F32),
        square, square, square, pltpu.VMEM((8, width), F32),
    ]
    scratch += [pltpu.VMEM(each.shape, each.dtype) for each in saved[1:]]
    scratch += [
        pltpu.VMEM(wout.shape[1:], BF16), pltpu.VMEM(wqkv.shape[1:], BF16), pltpu.VMEM((3, depth, width), BF16),
        pltpu.VMEM((heads, tall, LANES), BF16), pltpu.VMEM((heads, LANES, tall), BF16),
        pltpu.VMEM((heads, tall, LANES), F32), pltpu.VMEM((width, tall), BF16),
        dma_sems(24),
    ]
    scratch += exchange_scratch(rows, width, BF16, BACK_PIECES) + gather_sems(BACK_PIECES) + gather_sems(BACK_PIECES)
    if behind:
        scratch += total_scratch(count, width, columns, 2)
    if split:
        scratch += total_scratch(count, width, units, 2) + total_scratch(count, width, units, 2)
        scratch += small_sum_scratch(count, width)
    if last:
        scratch += total_scratch(count, width, columns, 4) + small_sum_scratch(count, width)
    return pl.pallas_call(
        functools.partial(layer_backward_kernel, layer, count, split, behind, last),
        out_shape=outs,
        in_specs=[VM] * 5 + [ANY] * 16 + [SM] + ([ANY, VM] if behind else []),
        out_specs=out_specs,
        scratch_shapes=scratch,
        compiler_params=params(5 + layer),
        name="layer_bwd",
    )(grad, normal2, recip2, gain, recip1, *hbm, prefix, *(earlier if behind else ()))


def results_kernel(depth, *refs):
    refs = Refs(refs)
    state_in, grad_in = refs.take(2)
    attn, up, down = refs.take(2), refs.take(2), refs.take(2)
    tail, smalls = refs.one(), refs.take(2)
    state, grad, wqkv, bias_qv, wout, bias_out, gain, shift, wup, bias_up, wdown, bias_down = refs.take(12)
    state[...] = state_in[...]
    grad[...] = grad_in[...]
    for layer in range(2):
        wout[layer] = attn[layer][:, :depth].T
        for kind in range(3):
            wqkv[layer, kind] = attn[layer][:, (kind + 1) * depth : (kind + 2) * depth]
        wup[layer] = up[layer][...]
        wdown[layer] = down[layer][...].T
        sums = smalls[layer]
        row = slice(layer, layer + 1)
        bias_down[row] = sums[0:1]
        gain[layer, 1:2] = sums[1:2]
        shift[layer, 1:2] = sums[2:3]
        gain[layer, 0:1] = sums[3:4]
        shift[layer, 0:1] = sums[4:5]
        bias_out[row] = sums[5:6]
        bias_up[row] = sums[6:7]
        biases = tail if layer == 0 else smalls[0]
        for kind in range(2):
            bias_qv[layer, kind : kind + 1] = biases[7:8, kind * depth : (kind + 1) * depth]


def results(state, grad, attn, up, down, tail, smalls, depth):
    rows, width = state.shape
    share, units = up[0].shape
    layers = len(attn)
    return pl.pallas_call(
        functools.partial(results_kernel, depth),
        out_shape=[
            shape((rows, width)), shape((rows, width)), shape((layers, 3, share, depth)),
            shape((layers, 2, depth)), shape((layers, depth, share)), shape((layers, width)),
            shape((layers, 2, width)), shape((layers, 2, width)), shape((layers, share, units)),
            shape((layers, units)), shape((layers, units, share)), shape((layers, width)),
        ],
        in_specs=[VM] * 11,
        out_specs=[VM] * 12,
        compiler_params=pltpu.CompilerParams(vmem_limit_bytes=VMEM_BYTES),
        name="results",
    )(state, grad, *attn, *up, *down, tail, *smalls)


def local(
    tokens,
    cotangent,
    prefix,
    w_qkv,
    bias_qv,
    w_out,
    bias_out,
    norm_gain,
    norm_bias,
    w_up,
    bias_up,
    w_down,
    bias_down,
):
    width = tokens.shape[1]
    layer_count = w_qkv.shape[0]
    depth = w_out.shape[1]
    state, low = tokens, tokens
    stored = []
    for layer in range(layer_count):
        state, low, normal1, recip1, *saved = attention_layer(
            layer, state, low, w_qkv, bias_qv, w_out, bias_out, norm_gain, norm_bias, prefix
        )
        state, low, normal2, recip2, normed, active, slope = ffn_layer(
            layer, state, low, w_up, bias_up, w_down, bias_down, norm_gain, norm_bias
        )
        stored.append(((normal2, recip2), (active, slope, normed, normal1, recip1), saved))
    count = lax.axis_size("dp")
    split = count > 2 and count % 2 == 0 and (width // count) % 16 == 0
    grad = cotangent
    earlier = None
    attn, up, down, smalls, biases = [], [], [], [], []
    for layer in reversed(range(layer_count)):
        (normal2, recip2), (active, slope, normed, normal1, recip1), saved = stored[layer]
        hbm = (w_down, w_up, active, slope, normed, normal1, w_out, w_qkv, *saved)
        grad, bias, *rest = layer_back(
            layer, count, split, grad, normal2, recip2, norm_gain, recip1, hbm, prefix, earlier
        )
        if split and layer == 0:
            up_sum, down_sum, small, *rest = rest
            attn = rest[: len(rest) - 2] + attn
            attn.insert(0, rest[-2])
            return results(
                state, grad, attn, [up_sum] + up, [down_sum] + down, rest[-1], [small] + smalls, depth
            )
        attn_grad, up_grad, down_grad, small, *rest = rest
        if split:
            earlier = (attn_grad, bias)
            attn = rest + attn
        else:
            attn.insert(0, attn_grad)
        up.insert(0, up_grad)
        down.insert(0, down_grad)
        smalls.insert(0, small)
        biases.insert(0, bias[7, : 2 * depth].reshape(2, depth))
    scatter = functools.partial(lax.psum_scatter, axis_name="dp", scatter_dimension=1, tiled=True)
    attn_sum, up_sum, down_sum = [scatter(jnp.stack(each)) for each in (attn, up, down)]
    shared = lax.psum(jnp.stack(smalls)[:, :6], ("dp", "tensor"))
    bias_qv_sum, bias_up_sum = lax.psum((jnp.stack(biases), jnp.stack(smalls)[:, 6]), "dp")
    share = attn_sum.shape[1]
    return (
        state,
        grad,
        jnp.moveaxis(attn_sum[:, :, depth:].reshape(layer_count, share, 3, depth), 2, 1),
        bias_qv_sum,
        jnp.swapaxes(attn_sum[:, :, :depth], 1, 2),
        shared[:, 5],
        jnp.stack([shared[:, 3], shared[:, 1]], axis=1),
        jnp.stack([shared[:, 4], shared[:, 2]], axis=1),
        up_sum,
        bias_up_sum,
        jnp.swapaxes(down_sum, 1, 2),
        shared[:, 0],
    )


def solution(mesh):
    in_specs = (
        P(("dp", "tensor"), None),
        P(("dp", "tensor"), None),
        P("dp"),
        P(None, None, None, "tensor"),
        P(None, None, "tensor"),
        P(None, "tensor", None),
        P(),
        P(),
        P(),
        P(None, None, "tensor"),
        P(None, "tensor"),
        P(None, "tensor", None),
        P(),
    )
    out_specs = (
        P(("dp", "tensor"), None),
        P(("dp", "tensor"), None),
        P(None, None, "dp", "tensor"),
        P(None, None, "tensor"),
        P(None, "tensor", "dp"),
        P(),
        P(),
        P(),
        P(None, "dp", "tensor"),
        P(None, "tensor"),
        P(None, "tensor", "dp"),
        P(),
    )
    return jax.shard_map(local, mesh=mesh, in_specs=in_specs, out_specs=out_specs, check_vma=False)
```

```python
import functools
import math

import jax
import jax.numpy as jnp
from jax import lax
from jax.experimental import pallas as pl
from jax.experimental.pallas import tpu as pltpu
from jax.sharding import PartitionSpec as P

HDIM = 64
LEN = 1024
MEM = 10
LANES = 128
GROUP = 4
EPSILON = 1e-06
VMEM_BYTES = 62 * 1024 * 1024
HIGHEST = lax.Precision.HIGHEST
MESH = pl.DeviceIdType.MESH
F32 = jnp.float32
BF16 = jnp.bfloat16
VM = pl.BlockSpec(memory_space=pltpu.VMEM)
SM = pl.BlockSpec(memory_space=pltpu.SMEM)
ANY = pl.BlockSpec(memory_space=pl.ANY)


def dot(left, right):
    return jnp.dot(left, right, preferred_element_type=F32)


def dot_nt(left, right):
    return lax.dot_general(left, right, (((1,), (1,)), ((), ())), preferred_element_type=F32)


def remote(src, dst, send_sem, recv_sem, tensor_index):
    return pltpu.make_async_remote_copy(
        src_ref=src,
        dst_ref=dst,
        send_sem=send_sem,
        recv_sem=recv_sem,
        device_id={"tensor": tensor_index},
        device_id_type=MESH,
    )


def places():
    mine = lax.axis_index("tensor")
    chip = mine // 2
    core = mine - 2 * chip
    partner = mine + 1 - 2 * core
    across = mine + 2 - 4 * chip
    diagonal = across + 1 - 2 * core
    return mine, partner, across, diagonal


class Refs:
    def __init__(self, refs):
        self.refs = list(refs)

    def take(self, count):
        taken, self.refs = self.refs[:count], self.refs[count:]
        return taken

    def one(self):
        return self.take(1)[0]


class Moves:
    def __init__(self, sems):
        self.sems, self.used, self.pending = sems, 0, []

    def start(self, source, target):
        move = pltpu.make_async_copy(source, target, self.sems.at[self.used])
        self.used += 1
        move.start()
        return move

    def store(self, source, target):
        self.pending.append(self.start(source, target))

    def finish(self):
        for move in self.pending:
            move.wait()


def remote_dp(src, dst, send_sem, recv_sem, dp_index):
    return pltpu.make_async_remote_copy(
        src_ref=src,
        dst_ref=dst,
        send_sem=send_sem,
        recv_sem=recv_sem,
        device_id={"dp": dp_index},
        device_id_type=MESH,
    )


class Sequences:
    def __init__(self, count):
        self.pairs = count // 2
        self.index = lax.axis_index("dp")
        self.pair = self.index // 2
        self.side = self.index - 2 * self.pair
        self.neighbour = self.index + 1 - 2 * self.side

    def other_pair(self, offset):
        return lax.rem(self.pair + offset, self.pairs)

    def peer(self, offset):
        return 2 * self.other_pair(offset) + self.side

    def everyone(self):
        return [self.neighbour] + [self.peer(offset) for offset in range(1, self.pairs)]


class Entry:
    def __init__(self, sequences=None):
        barrier = pltpu.get_barrier_semaphore()
        group = places()[1:]
        others = sequences.everyone() if sequences is not None else []
        for other in group:
            pl.semaphore_signal(barrier, inc=1, device_id={"tensor": other}, device_id_type=MESH)
        for other in others:
            pl.semaphore_signal(barrier, inc=1, device_id={"dp": other}, device_id_type=MESH)
        self.barrier, self.count = barrier, len(group) + len(others)

    def wait(self):
        pl.semaphore_wait(self.barrier, self.count)


class Gather:
    def __init__(self, whole, send_sems, recv_sems, pieces):
        self.whole = whole
        self.pieces = pieces
        self.mine, self.partner, self.across, self.diagonal = places()
        self.rows = whole.shape[1] // pieces
        self.send_sems, self.recv_sems = send_sems, recv_sems

    def piece(self, chunk, part):
        return self.whole.at[chunk, pl.ds(part * self.rows, self.rows)]

    def to_partner(self):
        return remote(
            self.whole.at[self.mine], self.whole.at[self.mine],
            self.send_sems.at[0], self.recv_sems.at[0], self.partner,
        )

    def to_across(self, part):
        return remote(
            self.piece(self.mine, part), self.piece(self.mine, part),
            self.send_sems.at[1 + part], self.recv_sems.at[1 + part], self.across,
        )

    def onward(self, part):
        return remote(
            self.piece(self.across, part), self.piece(self.across, part),
            self.send_sems.at[1 + self.pieces + part], self.recv_sems.at[1 + self.pieces + part], self.partner,
        )

    def start(self):
        for part in range(self.pieces):
            self.to_across(part).start()
        self.to_partner().start()

    def wait_partner(self):
        remote(
            self.whole.at[self.partner], self.whole.at[self.partner],
            self.send_sems.at[0], self.recv_sems.at[0], self.partner,
        ).wait_recv()

    def wait_across(self, part):
        remote(
            self.piece(self.across, part), self.piece(self.across, part),
            self.send_sems.at[1 + part], self.recv_sems.at[1 + part], self.across,
        ).wait_recv()

    def wait_diagonal(self, part):
        remote(
            self.piece(self.diagonal, part), self.piece(self.diagonal, part),
            self.send_sems.at[1 + self.pieces + part], self.recv_sems.at[1 + self.pieces + part], self.partner,
        ).wait_recv()

    def wait_sends(self):
        self.to_partner().wait_send()
        for part in range(self.pieces):
            self.to_across(part).wait_send()
            self.onward(part).wait_send()


ATTN_PIECES = 2
FFN_PIECES = 4
BACK_PIECES = 2


def gather_sems(pieces):
    return [dma_sems(1 + 2 * pieces), dma_sems(1 + 2 * pieces)]


def shape(dims, kind=F32):
    return jax.ShapeDtypeStruct(dims, kind)


def dma_sems(*dims):
    return pltpu.SemaphoreType.DMA(dims)


def params(collective_id):
    return pltpu.CompilerParams(
        collective_id=collective_id, has_side_effects=True, vmem_limit_bytes=VMEM_BYTES
    )


def layer_norm(total, gain, shift):
    row_mean = jnp.mean(total, axis=-1, keepdims=True)
    centered = total - row_mean
    spread = jnp.mean(centered * centered, axis=-1, keepdims=True)
    recip = lax.rsqrt(spread + EPSILON)
    normal = centered * recip
    return normal * gain + shift, normal, recip


def visible_keys(chunk, rows):
    first, last = chunk * rows, (chunk + 1) * rows - 1
    if first < MEM or last >= LEN - MEM:
        return LEN
    return max(last + 1, LEN // 2)


def query_limits(chunk, rows, prefix_len):
    spots = chunk * rows + lax.broadcasted_iota(jnp.int32, (1, rows), 1)
    limits = jnp.maximum(spots, prefix_len - 1)
    return jnp.where((spots < MEM) | (spots >= LEN - MEM), LEN - 1, limits)


def transposed(values):
    return values.astype(F32).T


def head_pairs(values, heads):
    wide = []
    for head in range(heads):
        columns = values[:, head * HDIM : (head + 1) * HDIM]
        wide.append(jnp.concatenate([columns, columns], axis=1))
    return wide


class Exchange:
    def __init__(self, terms, near, relay, total, far, sems, pieces):
        self.terms, self.near, self.relay, self.total, self.far = terms, near, relay, total, far
        self.n_send, self.n_recv, self.r_send, self.r_recv, self.f_send, self.f_recv = sems
        self.mine, self.partner, self.across, self.diagonal = places()
        self.pieces = pieces
        self.rows = terms.shape[1] // pieces

    def spot(self, part):
        return pl.ds(part * self.rows, self.rows)

    def near_copy(self, part):
        return remote(
            self.terms.at[self.partner, self.spot(part)], self.near.at[self.spot(part)],
            self.n_send.at[part], self.n_recv.at[part], self.partner,
        )

    def relay_copy(self, part):
        return remote(
            self.terms.at[self.diagonal, self.spot(part)], self.relay.at[self.spot(part)],
            self.r_send.at[part], self.r_recv.at[part], self.partner,
        )

    def far_copy(self, part):
        return remote(
            self.total.at[self.spot(part)], self.far.at[self.spot(part)],
            self.f_send.at[part], self.f_recv.at[part], self.across,
        )

    def pass_on(self, part):
        spot = self.spot(part)
        self.relay_copy(part).wait_recv()
        self.total[spot] = (self.terms[self.across, spot] + self.relay[spot]).astype(self.total.dtype)
        self.far_copy(part).start()

    def result(self, part):
        spot = self.spot(part)
        self.near_copy(part).wait_recv()
        self.far_copy(part).wait_recv()
        return (self.terms[self.mine, spot] + self.near[spot]) + self.far[spot].astype(F32)

    def wait_sends(self):
        for part in range(self.pieces):
            self.near_copy(part).wait_send()
            self.relay_copy(part).wait_send()
            self.far_copy(part).wait_send()


def exchange_scratch(rows, width, kind, pieces):
    return [
        pltpu.VMEM((GROUP, rows, width), F32),
        pltpu.VMEM((rows, width), F32), pltpu.VMEM((rows, width), F32),
        pltpu.VMEM((rows, width), kind), pltpu.VMEM((rows, width), kind),
    ] + [dma_sems(pieces)] * 6


def layer_forward_kernel(layer, *refs):
    refs = Refs(refs)
    state_hbm, low_ref, wqkv_hbm, bias_ref, wout_hbm, bias_out_ref, gain_ref, shift_ref = refs.take(8)
    wup_hbm, bias_up_ref, wdown_hbm, bias_down_ref, prefix_ref = refs.take(5)
    next_ref, next_low_ref, normal1_ref, recip1_ref, normal2_ref, recip2_ref = refs.take(6)
    saved_hbm, ffn_saved_hbm = refs.take(8), refs.take(3)
    saved = refs.take(8)
    whole_ref, qt_ref, q2_ref, kz_ref, kt_ref, v2_ref, ct_ref, stats_ref = saved
    state_ref, wqkv_ref, vt_ref, cf_ref, wo_ref = refs.take(5)
    normed_ref, active_ref, slope_ref = refs.take(3)
    total_ref, wup_ref, wdown_ref = refs.take(3)
    moves = Moves(refs.one())
    g_send, g_recv, c_send, c_recv, w_send, w_recv = refs.take(6)
    exchange_refs, second_sems = refs.take(11), refs.take(2)
    mine, partner, across, diagonal = places()
    rows = low_ref.shape[0]
    heads = qt_ref.shape[0]
    root = 1.0 / math.sqrt(HDIM)
    entry = Entry()
    wqkv_in = moves.start(wqkv_hbm.at[layer], wqkv_ref)
    wout_in = moves.start(wout_hbm.at[layer], wo_ref.at[mine])
    state_in = moves.start(state_hbm, state_ref)
    wup_in = moves.start(wup_hbm.at[layer], wup_ref)
    wdown_in = moves.start(wdown_hbm.at[layer], wdown_ref)
    gather = Gather(whole_ref, g_send, g_recv, ATTN_PIECES)
    whole_ref[mine] = low_ref[...]
    entry.wait()
    gather.start()
    lane_low = lax.broadcasted_iota(jnp.int32, (rows, LANES), 1) < HDIM

    def project(chunk):
        spots = pl.ds(pl.multiple_of(chunk * rows, rows), rows)
        values = whole_ref[chunk]
        query = (dot_nt(values, wqkv_ref[0]) + bias_ref[layer, 0:1]) * root
        key = dot_nt(values, wqkv_ref[1])
        value = dot_nt(values, wqkv_ref[2]) + bias_ref[layer, 1:2]
        queries, keys, valuess = [head_pairs(each, heads) for each in (query, key, value)]
        query_t, key_t, value_t = [each.T.astype(BF16) for each in (query, key, value)]
        for head in range(heads):
            part = slice(head * HDIM, (head + 1) * HDIM)
            q2_ref[head, spots] = queries[head].astype(BF16)
            kz_ref[head, spots] = jnp.where(lane_low, keys[head], 0.0).astype(BF16)
            v2_ref[head, spots] = valuess[head].astype(BF16)
            for half in (slice(0, HDIM), slice(HDIM, 2 * HDIM)):
                qt_ref[head, half, spots] = query_t[part]
                kt_ref[head, half, spots] = key_t[part]
            vt_ref[head, :, spots] = value_t[part]

    def wout_to_partner(source):
        slot = 0 if source is mine else 2
        return remote(wo_ref.at[source], wo_ref.at[source], w_send.at[slot], w_recv.at[slot], partner)

    wout_to_across = remote(wo_ref.at[mine], wo_ref.at[mine], w_send.at[1], w_recv.at[1], across)
    wout_from_across = remote(wo_ref.at[across], wo_ref.at[across], w_send.at[1], w_recv.at[1], across)
    wout_from_partner = remote(wo_ref.at[partner], wo_ref.at[partner], w_send.at[0], w_recv.at[0], partner)
    wout_from_diagonal = remote(wo_ref.at[diagonal], wo_ref.at[diagonal], w_send.at[2], w_recv.at[2], partner)

    wqkv_in.wait()
    project(mine)
    gather.wait_partner()
    project(partner)
    wout_in.wait()
    for part in range(ATTN_PIECES):
        gather.wait_across(part)
        gather.onward(part).start()
    wout_to_across.start()
    wout_to_partner(mine).start()
    project(across)
    for part in range(ATTN_PIECES):
        gather.wait_diagonal(part)
    project(diagonal)
    for source, target in zip(saved[:6], saved_hbm[:6]):
        moves.store(source, target)

    def context_copy(step, chunk):
        return remote(ct_ref.at[chunk], cf_ref.at[mine], c_send.at[step], c_recv.at[step], chunk)

    def context_from(step, chunk):
        return remote(ct_ref.at[mine], cf_ref.at[chunk], c_send.at[step], c_recv.at[step], chunk)

    def attend(chunk):
        keys = visible_keys(chunk, rows)
        limits = query_limits(chunk, rows, prefix_ref[0])
        visible = lax.broadcasted_iota(jnp.int32, (keys, rows), 0) <= limits
        spots = pl.ds(chunk * rows, rows)

        def one_head(head, carry):
            scores = dot(kz_ref[head, pl.ds(0, keys)], qt_ref[head, :, spots])
            scores = jnp.where(visible, scores, -1e30)
            top = jnp.max(scores, axis=0, keepdims=True)
            expo = jnp.exp(scores - top)
            recip = 1.0 / jnp.sum(expo, axis=0, keepdims=True)
            probs = (expo * recip).astype(BF16)
            context = dot(vt_ref[head, :, pl.ds(0, keys)], probs)
            ct_ref[chunk, pl.ds(pl.multiple_of(head * HDIM, HDIM), HDIM)] = context.astype(BF16)
            first = lax.broadcasted_iota(jnp.int32, (8, rows), 0) == 0
            stats_ref[head, :, spots] = jnp.where(first, top, recip)
            return carry

        lax.fori_loop(0, heads, one_head, 0)

    chip, core = mine // 2, mine - 2 * (mine // 2)

    def one_step(step, carry):
        near = step // 2
        flip = lax.rem(lax.rem(step, 2) + near, 2)
        to_chip = (1 - near) * (1 - chip) + near * chip
        chunk = 2 * to_chip + core + flip * (1 - 2 * core)
        for each in range(GROUP):
            @pl.when(chunk == each)
            def _():
                attend(each)

        @pl.when(step < 3)
        def _():
            context_copy(step, chunk).start()

        @pl.when(step == 1)
        def _():
            wout_from_across.wait_recv()
            wout_to_partner(across).start()
        return carry

    lax.fori_loop(0, GROUP, one_step, 0)
    for source, target in zip(saved[6:], saved_hbm[6:]):
        moves.store(source, target)
    cf_ref[mine] = ct_ref[mine]
    wout_from_partner.wait_recv()
    wout_from_diagonal.wait_recv()
    for step, chunk in enumerate((across, diagonal, partner)):
        context_from(step, chunk).wait_recv()
    depth = GROUP * wo_ref.shape[1]
    context = transposed(cf_ref[...].reshape(depth, rows)).astype(BF16)
    state_in.wait()
    total_ref[...] = (
        state_ref[...].astype(F32) + dot(context, wo_ref[...].reshape(depth, -1)) + bias_out_ref[layer : layer + 1]
    )
    second = Gather(normed_ref, *second_sems, FFN_PIECES)
    exchange = Exchange(*exchange_refs[:5], exchange_refs[5:], FFN_PIECES)
    terms_ref = exchange.terms
    part_rows = rows // FFN_PIECES
    for part in range(FFN_PIECES):
        spot = exchange.spot(part)
        result, normal, recip = layer_norm(total_ref[spot], gain_ref[layer, 0:1], shift_ref[layer, 0:1])
        normed_ref[mine, spot] = result.astype(BF16)
        second.to_across(part).start()
        total_ref[spot] = result
        normal1_ref[spot] = normal
        recip1_ref[spot] = jnp.broadcast_to(recip, (part_rows, LANES))
    second.to_partner().start()
    gather.wait_sends()
    wout_to_across.wait_send()
    wout_to_partner(mine).wait_send()
    wout_to_partner(across).wait_send()
    for step, chunk in enumerate((across, diagonal, partner)):
        context_copy(step, chunk).wait_send()

    def units(chunk, part):
        spot = exchange.spot(part)
        hidden = dot(normed_ref[chunk, spot], wup_ref[...]) + bias_up_ref[layer : layer + 1]
        below = 0.5 * (1.0 + lax.erf(hidden * math.sqrt(0.5)))
        density = jnp.exp(-0.5 * hidden * hidden) * (1.0 / math.sqrt(2.0 * math.pi))
        active = (hidden * below).astype(BF16)
        active_ref[chunk, spot] = active
        slope_ref[chunk, spot] = below + hidden * density
        terms_ref[chunk, spot] = dot(active, wdown_ref[...])

    wup_in.wait()
    wdown_in.wait()
    for part in range(FFN_PIECES):
        units(mine, part)
    for part in range(FFN_PIECES):
        second.wait_across(part)
        second.onward(part).start()
        units(across, part)
        second.wait_diagonal(part)
        units(diagonal, part)
        exchange.relay_copy(part).start()
        if part > 0:
            exchange.pass_on(part - 1)
    second.wait_partner()
    moves.store(normed_ref, ffn_saved_hbm[0])
    units(partner, 0)
    exchange.near_copy(0).start()
    exchange.pass_on(FFN_PIECES - 1)
    for part in range(1, FFN_PIECES):
        units(partner, part)
        exchange.near_copy(part).start()
    moves.store(active_ref, ffn_saved_hbm[1])
    moves.store(slope_ref, ffn_saved_hbm[2])
    for part in range(FFN_PIECES):
        spot = exchange.spot(part)
        total = total_ref[spot] + exchange.result(part) + bias_down_ref[layer : layer + 1]
        result, normal, recip = layer_norm(total, gain_ref[layer, 1:2], shift_ref[layer, 1:2])
        next_ref[spot] = result
        next_low_ref[spot] = result.astype(BF16)
        normal2_ref[spot] = normal
        recip2_ref[spot] = jnp.broadcast_to(recip, (part_rows, LANES))
    second.wait_sends()
    exchange.wait_sends()
    moves.finish()


def layer_forward(layer, state, low, wqkv, bias, wout, bias_out, gain, shift, wup, bias_up, wdown, bias_down, prefix):
    rows, width = low.shape
    depth = wout.shape[1]
    units = wup.shape[2]
    heads = depth // HDIM
    tall = GROUP * rows
    saved = [
        ((GROUP, rows, width), BF16),
        ((heads, LANES, tall), BF16), ((heads, tall, LANES), BF16), ((heads, tall, LANES), BF16),
        ((heads, LANES, tall), BF16), ((heads, tall, LANES), BF16), ((GROUP, depth, rows), BF16),
        ((heads, 8, tall), F32),
    ]
    ffn_saved = [((GROUP, rows, width), BF16), ((GROUP, rows, units), BF16), ((GROUP, rows, units), F32)]
    norms = [shape((rows, width)), shape((rows, LANES))]
    return pl.pallas_call(
        functools.partial(layer_forward_kernel, layer),
        out_shape=[shape((rows, width)), shape((rows, width), BF16)] + norms + norms
        + [shape(*each) for each in saved + ffn_saved],
        in_specs=[ANY, VM, ANY, VM, ANY, VM, VM, VM, ANY, VM, ANY, VM, SM],
        out_specs=[VM] * 6 + [ANY] * 11,
        scratch_shapes=[pltpu.VMEM(*each) for each in saved] + [
            pltpu.VMEM((rows, width), state.dtype),
            pltpu.VMEM(wqkv.shape[1:], BF16),
            pltpu.VMEM((heads, HDIM, tall), BF16),
            pltpu.VMEM((GROUP, depth, rows), BF16),
            pltpu.VMEM((GROUP, depth, width), BF16),
        ] + [pltpu.VMEM(*each) for each in ffn_saved] + [
            pltpu.VMEM((rows, width), F32), pltpu.VMEM(wup.shape[1:], BF16), pltpu.VMEM(wdown.shape[1:], BF16),
            dma_sems(16),
            *gather_sems(ATTN_PIECES),
            dma_sems(3), dma_sems(3), dma_sems(3), dma_sems(3),
        ] + exchange_scratch(rows, width, F32, FFN_PIECES) + gather_sems(FFN_PIECES),
        compiler_params=params(1 + layer),
        name="layer_fwd",
    )(state, low, wqkv, bias, wout, bias_out, gain, shift, wup, bias_up, wdown, bias_down, prefix)


def layer_norm_back(grad_in, normal, recip, gain):
    scaled = grad_in * gain
    inner = (
        scaled
        - jnp.mean(scaled, axis=-1, keepdims=True)
        - normal * jnp.mean(scaled * normal, axis=-1, keepdims=True)
    )
    return recip * inner


def column_sum(values):
    return jnp.sum(values, axis=0, keepdims=True)


def high_low(values):
    high = values.astype(BF16)
    return high, (values - high.astype(F32)).astype(BF16)


def dot_tn(left, right):
    return lax.dot_general(left, right, (((0,), (0,)), ((), ())), preferred_element_type=F32)


def owner_rows(pair, side, rows):
    return pl.ds(pl.multiple_of((2 * pair + side) * rows, 16), rows)


class PairSum:
    def __init__(self, sequences, source, columns, buffers, sems):
        self.at, self.source, self.columns = sequences, source, columns
        self.out, self.into = buffers
        self.sems = sems
        self.rows = self.out.shape[1]

    def copy(self):
        return remote_dp(
            self.out.at[:, :, self.columns], self.into.at[:, :, self.columns], *self.sems, self.at.neighbour
        )

    def start(self):
        for pair in range(self.at.pairs):
            place = (owner_rows(pair, 1 - self.at.side, self.rows), self.columns)
            self.out[pair, :, self.columns] = self.source[place].astype(BF16)
        self.copy().start()

    def finish(self):
        self.copy().wait_recv()
        for pair in range(self.at.pairs):
            place = (owner_rows(pair, self.at.side, self.rows), self.columns)
            self.source[place] = self.source[place] + self.into[pair, :, self.columns].astype(F32)

    def wait_sends(self):
        self.copy().wait_send()


class OwnerSum:
    def __init__(self, sequences, source, result, columns, buffers, sems):
        self.at, self.source, self.result, self.columns = sequences, source, result, columns
        self.out, self.into = buffers
        self.sems = sems
        self.rows = result.shape[0]

    def terms(self, pair):
        return self.source[owner_rows(pair, self.at.side, self.rows), self.columns]

    def copy(self, offset):
        return remote_dp(
            self.out.at[offset - 1, :, self.columns], self.into.at[offset - 1, :, self.columns],
            self.sems[0].at[offset - 1], self.sems[1].at[offset - 1], self.at.peer(offset),
        )

    def start(self):
        for offset in range(1, self.at.pairs):
            pair = self.at.other_pair(offset)
            self.out[offset - 1, :, self.columns] = self.terms(pair).astype(BF16)
            self.copy(offset).start()

    def finish(self):
        total = self.terms(self.at.pair)
        for offset in range(1, self.at.pairs):
            self.copy(offset).wait_recv()
            total = total + self.into[offset - 1, :, self.columns].astype(F32)
        self.result[:, self.columns] = total

    def wait_sends(self):
        for offset in range(1, self.at.pairs):
            self.copy(offset).wait_send()


def halves(columns):
    return (slice(0, columns // 2), slice(columns // 2, columns))


def tile_blocks(columns):
    tiles = columns // LANES
    ends = [0, 1, 1 + (tiles - 1) * 2 // 5, 1 + (tiles - 1) * 4 // 5, tiles]
    return [slice(first * LANES, end * LANES) for first, end in zip(ends, ends[1:])]


def pair_scratch(count, width, columns, blocks):
    dims = (count // 2, width // count, columns)
    return [pltpu.VMEM(dims, BF16), pltpu.VMEM(dims, BF16), dma_sems(blocks), dma_sems(blocks)]


def owner_scratch(count, width, columns, blocks):
    pairs = count // 2
    dims = (pairs - 1, width // count, columns)
    return [
        pltpu.VMEM(dims, BF16), pltpu.VMEM(dims, BF16), dma_sems(blocks, pairs - 1), dma_sems(blocks, pairs - 1)
    ]


def total_scratch(count, width, columns, blocks):
    return pair_scratch(count, width, columns, blocks) + owner_scratch(count, width, columns, blocks)


def pair_sums(sequences, source, scratch, blocks):
    out, into, send, recv = scratch
    return [
        PairSum(sequences, source, columns, (out, into), (send.at[block], recv.at[block]))
        for block, columns in enumerate(blocks)
    ]


def owner_sums(sequences, source, result, scratch, blocks):
    out, into, send, recv = scratch
    return [
        OwnerSum(sequences, source, result, columns, (out, into), (send.at[block], recv.at[block]))
        for block, columns in enumerate(blocks)
    ]


def total_sums(sequences, source, result, scratch, blocks):
    pairs = pair_sums(sequences, source, scratch[:4], blocks)
    owners = owner_sums(sequences, source, result, scratch[4:], blocks)
    return [BlockSum(pair, owner) for pair, owner in zip(pairs, owners)]


TOTAL_REFS = 8


class BlockSum:
    def __init__(self, pair, owner):
        self.pair, self.owner = pair, owner
        self.start, self.finish = pair.start, owner.finish

    def turn(self):
        self.pair.finish()
        self.owner.start()

    def wait_sends(self):
        self.pair.wait_sends()
        self.owner.wait_sends()


class SmallSum:
    def __init__(self, sequences, source, result, shared_rows, slots, sems):
        self.at = sequences
        self.source, self.result, self.shared_rows = source, result, shared_rows
        self.group_slots, self.side_slots, self.pair_slots = slots
        self.g_send, self.g_recv, self.s_send, self.s_recv, self.p_send, self.p_recv = sems
        self.mine, self.partner, self.across, self.diagonal = places()

    def group_copy(self, index, to, slot):
        return remote(
            self.group_slots.at[slot], self.group_slots.at[slot],
            self.g_send.at[index], self.g_recv.at[index], to,
        )

    def start(self):
        if self.shared_rows:
            self.group_slots[self.mine] = self.source[...]
            for index, other in enumerate((self.partner, self.across, self.diagonal)):
                self.group_copy(index, other, self.mine).start()

    def side_copy(self, slot):
        return remote_dp(
            self.side_slots.at[slot], self.side_slots.at[slot],
            self.s_send.at[0], self.s_recv.at[0], self.at.neighbour,
        )

    def first(self):
        values = self.source[...]
        if self.shared_rows:
            for index, other in enumerate((self.partner, self.across, self.diagonal)):
                self.group_copy(index, other, other).wait_recv()
            total = self.group_slots[0]
            for slot in range(1, GROUP):
                total = total + self.group_slots[slot]
            shared = lax.broadcasted_iota(jnp.int32, values.shape, 0) < self.shared_rows
            values = jnp.where(shared, total, values)
        self.side_slots[self.at.side] = values
        self.side_copy(self.at.side).start()

    def pair_copy(self, offset, slot):
        return remote_dp(
            self.pair_slots.at[slot], self.pair_slots.at[slot],
            self.p_send.at[offset - 1], self.p_recv.at[offset - 1], self.at.peer(offset),
        )

    def second(self):
        self.side_copy(1 - self.at.side).wait_recv()
        self.pair_slots[self.at.pair] = self.side_slots[0] + self.side_slots[1]
        for offset in range(1, self.at.pairs):
            self.pair_copy(offset, self.at.pair).start()

    def third(self):
        for offset in range(1, self.at.pairs):
            self.pair_copy(offset, self.at.other_pair(self.at.pairs - offset)).wait_recv()
        total = self.pair_slots[0]
        for slot in range(1, self.at.pairs):
            total = total + self.pair_slots[slot]
        self.result[...] = total

    def wait_sends(self):
        if self.shared_rows:
            for index, other in enumerate((self.partner, self.across, self.diagonal)):
                self.group_copy(index, other, self.mine).wait_send()
        self.side_copy(self.at.side).wait_send()
        for offset in range(1, self.at.pairs):
            self.pair_copy(offset, self.at.pair).wait_send()


def small_sum_scratch(count, width):
    pairs = count // 2
    return [
        pltpu.VMEM((GROUP, 8, width), F32), pltpu.VMEM((2, 8, width), F32), pltpu.VMEM((pairs, 8, width), F32),
        dma_sems(3), dma_sems(3), dma_sems(1), dma_sems(1), dma_sems(pairs - 1), dma_sems(pairs - 1),
    ]


def layer_backward_kernel(layer, count, split, behind, last, *refs):
    refs = Refs(refs)
    grad_ref, normal2_ref, recip2_ref, gain_ref, recip1_ref = refs.take(5)
    wdown_hbm, wup_hbm, active_hbm, slope_hbm, normed_hbm, normal1_hbm, wout_hbm, wqkv_hbm = refs.take(8)
    whole_hbm, *saved_hbm = refs.take(8)
    prefix_ref = refs.one()
    earlier_hbm, bias_in = refs.take(2) if behind else (None,) * 2
    dx_ref, bias_ref = refs.take(2)
    grads_hbm = None if last else refs.one()
    up_out, down_out, smalls_out = refs.take(3)
    earlier_sum = refs.one() if behind else None
    grads_sum, bias_sum = refs.take(2) if last else (None,) * 2
    df_ref, do_ref, du_ref, high_ref, lowbits_ref = refs.take(5)
    wdown_ref, wup_ref, active_ref, wide_ref, normed_ref, normal1_ref = refs.take(6)
    up_ref, down_ref, grads_ref, smalls_ref = refs.take(4)
    saved = refs.take(7)
    qt_ref, q2_ref, kz_ref, kt_ref, v2_ref, ct_ref, stats_ref = saved
    wout_ref, wqkv_ref = refs.take(2)
    dc_ref, dct_ref, dv_ref, xt_ref = refs.take(4)
    moves = Moves(refs.one())
    exchange_refs = refs.take(11)
    first_sems, second_sems = refs.take(2), refs.take(2)
    mine, partner, across, diagonal = places()
    rows, width = grad_ref.shape
    units = wup_ref.shape[1]
    tall = GROUP * rows
    part_rows = rows // BACK_PIECES
    heads = qt_ref.shape[0]
    depth = heads * HDIM
    span = width // 3
    scale = 1.0 / math.sqrt(HDIM)
    sequences = Sequences(count) if split else None
    entry = Entry(sequences)
    wdown_in = moves.start(wdown_hbm.at[layer], wdown_ref)
    wup_in = moves.start(wup_hbm.at[layer], wup_ref)
    slope_in = [
        moves.start(slope_hbm.at[chunk], wide_ref.at[pl.ds(chunk * rows, rows)]) for chunk in range(GROUP)
    ]
    earlier, ups, downs, own, small, own_small = [], [], [], [], None, None
    if behind:
        earlier_in = moves.start(earlier_hbm, grads_ref)
        earlier = owner_sums(sequences, grads_ref, earlier_sum, refs.take(4), halves(width))
    if split:
        downs = total_sums(sequences, down_ref, down_out, refs.take(TOTAL_REFS), halves(units))
        ups = total_sums(sequences, up_ref, up_out, refs.take(TOTAL_REFS), halves(units))
        small = SmallSum(sequences, smalls_ref, smalls_out, 6, refs.take(3), refs.take(6))
    if last:
        own = total_sums(sequences, grads_ref, grads_sum, refs.take(TOTAL_REFS), tile_blocks(width))
        own_small = SmallSum(sequences, bias_ref, bias_sum, 0, refs.take(3), refs.take(6))
    elif split:
        own = pair_sums(sequences, grads_ref, refs.take(4), tile_blocks(width))
    active_in = moves.start(active_hbm, active_ref)
    normed_in = moves.start(normed_hbm, normed_ref)
    normal1_in = moves.start(normal1_hbm, normal1_ref)
    wout_in = moves.start(wout_hbm.at[layer], wout_ref)
    wqkv_in = moves.start(wqkv_hbm.at[layer], wqkv_ref)
    saved_in = [moves.start(source, target) for source, target in zip(saved_hbm, saved)]
    first_gather = Gather(df_ref, *first_sems, BACK_PIECES)
    second_gather = Gather(do_ref, *second_sems, BACK_PIECES)
    exchange = Exchange(*exchange_refs[:5], exchange_refs[5:], BACK_PIECES)
    terms_ref = exchange.terms

    grad = grad_ref[...].astype(F32)
    normal2 = normal2_ref[...]
    du2 = layer_norm_back(grad, normal2, recip2_ref[:, :1], gain_ref[layer, 1:2])
    du_ref[...] = du2
    df_ref[mine] = du2.astype(BF16)
    entry.wait()
    first_gather.start()
    smalls_ref[0:1] = column_sum(du2)
    smalls_ref[1:2] = column_sum(grad * normal2)
    smalls_ref[2:3] = column_sum(grad)
    smalls_ref[6:7] = jnp.zeros((1, width), F32)
    smalls_ref[7:8] = bias_in[7:8] if behind else jnp.zeros((1, width), F32)
    wdown_in.wait()
    wdown_ref[...] = transposed(wdown_ref[...]).astype(BF16)
    wup_in.wait()
    wup_ref[...] = transposed(wup_ref[...]).astype(BF16)
    if behind:
        earlier_in.wait()
        for item in earlier:
            item.start()

    def part_spots(chunk, part):
        return pl.ds(pl.multiple_of(chunk * rows + part * part_rows, part_rows), part_rows)

    def back(chunk, part):
        spot, spots = exchange.spot(part), part_spots(chunk, part)
        grad_active = dot(df_ref[chunk, spot], wdown_ref[...])
        grad_hidden = grad_active * wide_ref[spots]
        smalls_ref[6:7] = smalls_ref[6:7] + column_sum(grad_hidden)
        high, low = high_low(grad_hidden)
        high_ref[spots] = high
        lowbits_ref[spots] = low
        terms_ref[chunk, spot] = dot(high, wup_ref[...]) + dot(low, wup_ref[...])

    for move in slope_in:
        move.wait()
    for part in range(BACK_PIECES):
        back(mine, part)
    for part in range(BACK_PIECES):
        first_gather.wait_across(part)
        first_gather.onward(part).start()
        back(across, part)
        first_gather.wait_diagonal(part)
        back(diagonal, part)
        exchange.relay_copy(part).start()
        if part > 0:
            exchange.pass_on(part - 1)
    first_gather.wait_partner()
    back(partner, 0)
    exchange.near_copy(0).start()
    exchange.pass_on(BACK_PIECES - 1)
    active_in.wait()
    down_ref[...] = dot_tn(df_ref[...].reshape(tall, width), active_ref[...].reshape(tall, units))
    for item in downs:
        item.start()
    for part in range(1, BACK_PIECES):
        back(partner, part)
        exchange.near_copy(part).start()
    normed_in.wait()
    normed = normed_ref[...].reshape(tall, width)
    up_ref[...] = dot_tn(normed, high_ref[...]) + dot_tn(normed, lowbits_ref[...])
    if split:
        ups[0].start()
    whole_in = moves.start(whole_hbm, normed_ref)
    if not split:
        moves.store(down_ref, down_out)
        moves.store(up_ref, up_out)
    normal1_in.wait()
    for part in range(BACK_PIECES):
        spot = exchange.spot(part)
        grad_normed = exchange.result(part) + du_ref[spot]
        normal1 = normal1_ref[spot]
        du = layer_norm_back(grad_normed, normal1, recip1_ref[spot, :1], gain_ref[layer, 0:1])
        du_ref[spot] = du
        do_ref[mine, spot] = du.astype(BF16)
        second_gather.to_across(part).start()
        sums = (column_sum(grad_normed * normal1), column_sum(grad_normed), column_sum(du))
        for index, value in enumerate(sums):
            place = slice(3 + index, 4 + index)
            smalls_ref[place] = value if part == 0 else smalls_ref[place] + value
    second_gather.to_partner().start()
    if split:
        small.start()
    else:
        smalls_out[...] = smalls_ref[...]
    exchange.wait_sends()
    first_gather.wait_sends()

    lane_low = lax.broadcasted_iota(jnp.int32, (rows, LANES), 1) < HDIM
    wide_ref[:, width // 2 :] = jnp.zeros((tall, width // 2), F32)
    dv_ref[...] = jnp.zeros_like(dv_ref)

    def context_grad(chunk):
        spots = pl.ds(pl.multiple_of(chunk * rows, rows), rows)
        wide = head_pairs(dot_nt(do_ref[chunk], wout_ref[...]), heads)
        for head in range(heads):
            high = wide[head].astype(BF16).astype(F32)
            both = jnp.where(lane_low, high, wide[head] - high)
            dc_ref[head, spots] = both.astype(BF16)
            dct_ref[head, :, spots] = both.T.astype(BF16)

    def attend_back(chunk, head):
        keys = visible_keys(chunk, rows)
        limits = query_limits(chunk, rows, prefix_ref[0])
        visible = lax.broadcasted_iota(jnp.int32, (keys, rows), 0) <= limits
        spots = pl.ds(chunk * rows, rows)
        seen = pl.ds(0, keys)
        dq_lanes = pl.ds(pl.multiple_of(head * LANES, LANES), LANES)
        dk_lanes = pl.ds(pl.multiple_of((heads + head) * LANES, LANES), LANES)
        scores = dot(kz_ref[head, seen], qt_ref[head, :, spots])
        top = stats_ref[head, 0:1, spots]
        recip = stats_ref[head, 1:2, spots]
        probs = jnp.exp(jnp.where(visible, scores - top, -1e30)) * recip
        grad_probs = dot(v2_ref[head, seen], dct_ref[head, :, spots])
        inner = column_sum(probs * grad_probs)
        grad_scores = (probs * (grad_probs - inner)).astype(BF16)
        dv_ref[head, seen] = dv_ref[head, seen] + dot(probs.astype(BF16), dc_ref[head, spots])
        wide_ref[seen, dk_lanes] = wide_ref[seen, dk_lanes] + dot(grad_scores, q2_ref[head, spots])
        wide_ref[spots, dq_lanes] = dot(kt_ref[head, :, seen], grad_scores).T * scale

    chip, core = mine // 2, mine - 2 * (mine // 2)

    def weight_grad_out():
        out_wide = dot(ct_ref[0], do_ref[0])
        for chunk in range(1, GROUP):
            out_wide = out_wide + dot(ct_ref[chunk], do_ref[chunk])
        grads_ref[:, :depth] = out_wide.T

    def gathered(step):
        if step == 1:
            second_gather.wait_partner()
        if step == 2:
            for part in range(BACK_PIECES):
                second_gather.wait_across(part)
                second_gather.onward(part).start()
        if step == 3:
            for part in range(BACK_PIECES):
                second_gather.wait_diagonal(part)

    beside = {heads: [lambda: gathered(1)], 2 * heads: [lambda: gathered(2)], 3 * heads: [lambda: gathered(3)]}
    if split:
        plan = [(2, downs[0].turn), (6, small.first), (6, ups[1].start), (5, downs[1].turn), (9, ups[0].turn), (11, small.second)]
        for when, action in plan:
            beside.setdefault(when, []).append(action)
        for item in earlier:
            beside[2 * heads].append(item.finish)
        beside[3 * heads] += [weight_grad_out, own[0].start]

    def one_turn(turn, carry):
        step = turn // heads
        head = lax.rem(turn, heads)
        near = 1 - step // 2
        flip = lax.rem(step, 2)
        to_chip = (1 - near) * (1 - chip) + near * chip
        chunk = 2 * to_chip + core + flip * (1 - 2 * core)
        for when in sorted(beside):
            @pl.when(turn == when)
            def _():
                for action in beside[when]:
                    action()

        @pl.when(head == 0)
        def _():
            context_grad(chunk)

        for each in range(GROUP):
            @pl.when(chunk == each)
            def _():
                attend_back(each, head)
        return carry

    wout_in.wait()
    wqkv_in.wait()
    for move in saved_in:
        move.wait()
    lax.fori_loop(0, GROUP * heads, one_turn, 0)

    def kind_lanes(kind):
        return slice(kind * span, kind * span + depth)

    def pack_chunk(chunk, carry):
        spots = pl.ds(pl.multiple_of(chunk * rows, rows), rows)
        xt_ref[:, spots] = transposed(normed_ref[chunk]).astype(BF16)
        for kind in range(3):
            parts = []
            for head in range(heads):
                if kind < 2:
                    wide = wide_ref[spots, slice((kind * heads + head) * LANES, (kind * heads + head + 1) * LANES)]
                else:
                    wide = dv_ref[head, spots]
                    wide = wide + pltpu.roll(wide, HDIM, 1)
                parts.append(wide[:, :HDIM])
            values = jnp.concatenate(parts, axis=1)
            high, low = high_low(values)
            high_ref[spots, kind_lanes(kind)] = high
            lowbits_ref[spots, kind_lanes(kind)] = low
            if kind != 1:
                place = slice((kind // 2) * depth, (kind // 2 + 1) * depth)
                bias_ref[:, place] = bias_ref[:, place] + column_sum(values)
        return carry

    bias_ref[...] = jnp.zeros_like(bias_ref)
    whole_in.wait()
    lax.fori_loop(0, GROUP, pack_chunk, 0)

    def weight_grad(kind):
        place = slice((kind + 1) * depth, (kind + 2) * depth)
        lanes = kind_lanes(kind)
        grads_ref[:, place] = dot(xt_ref[...], high_ref[:, lanes]) + dot(xt_ref[...], lowbits_ref[:, lanes])

    def input_terms(chunk, part):
        spots = part_spots(chunk, part)
        total = None
        for kind in range(3):
            for values in (high_ref, lowbits_ref):
                term = dot(values[spots, kind_lanes(kind)], wqkv_ref[kind])
                total = term if total is None else total + term
        terms_ref[chunk, exchange.spot(part)] = total

    if split:
        ups[1].turn()
    if last:
        own_small.first()
    if split:
        weight_grad(0)
        own[1].start()
        weight_grad(1)
        weight_grad(2)
        own[2].start()
        own[3].start()
    for part in range(BACK_PIECES):
        input_terms(diagonal, part)
        exchange.relay_copy(part).start()
        input_terms(across, part)
        if part > 0:
            exchange.pass_on(part - 1)
    input_terms(partner, 0)
    exchange.near_copy(0).start()
    exchange.pass_on(BACK_PIECES - 1)
    for part in range(1, BACK_PIECES):
        input_terms(partner, part)
        exchange.near_copy(part).start()
    for part in range(BACK_PIECES):
        input_terms(mine, part)
    if last:
        own[0].turn()
        own[1].turn()
        own[2].turn()
        own[3].turn()
        own_small.second()
    if not split:
        weight_grad_out()
        for kind in range(3):
            weight_grad(kind)
        moves.store(grads_ref, grads_hbm)
    for item in downs + ups:
        item.finish()
    for part in range(BACK_PIECES):
        spot = exchange.spot(part)
        dx_ref[spot] = exchange.result(part) + du_ref[spot]
    if split:
        small.third()
    if last:
        own_small.third()
    for item in own:
        item.finish()
    if split and not last:
        moves.store(grads_ref, grads_hbm)
    second_gather.wait_sends()
    exchange.wait_sends()
    for item in earlier + downs + ups + own:
        item.wait_sends()
    for item in (small, own_small):
        if item is not None:
            item.wait_sends()
    moves.finish()


def layer_back(layer, count, split, grad, normal2, recip2, gain, recip1, hbm, prefix, earlier):
    rows, width = grad.shape
    wdown, wup, active, slope, normed, normal1, wout, wqkv, *saved = hbm
    units, depth = wup.shape[2], wout.shape[1]
    heads = depth // HDIM
    tall = GROUP * rows
    share = width // count
    behind = split and earlier is not None
    last = split and layer == 0
    columns = 4 * depth
    if not (columns == width == units == 2 * heads * LANES):
        raise ValueError("unsupported sizes")
    outs, out_specs = [shape((rows, width)), shape((8, width))], [VM, VM]
    if not last:
        outs.append(shape((width, columns)))
        out_specs.append(ANY)
    outs += [shape((share if split else width, units))] * 2 + [shape((8, width))]
    out_specs += [VM, VM, VM] if split else [ANY, ANY, VM]
    if behind:
        outs.append(shape((share, columns)))
        out_specs.append(VM)
    if last:
        outs += [shape((share, columns)), shape((8, width))]
        out_specs += [VM, VM]
    whole_rows = pltpu.VMEM((GROUP, rows, width), BF16)
    square = pltpu.VMEM((width, units), F32)
    scratch = [
        whole_rows, whole_rows, pltpu.VMEM((rows, width), F32),
        pltpu.VMEM((tall, units), BF16), pltpu.VMEM((tall, units), BF16),
        pltpu.VMEM(wdown.shape[1:], BF16), pltpu.VMEM(wup.shape[1:], BF16), whole_rows,
        pltpu.VMEM((tall, units), F32), whole_rows, pltpu.VMEM((rows, width), F32),
        square, square, square, pltpu.VMEM((8, width), F32),
    ]
    scratch += [pltpu.VMEM(each.shape, each.dtype) for each in saved[1:]]
    scratch += [
        pltpu.VMEM(wout.shape[1:], BF16), pltpu.VMEM(wqkv.shape[1:], BF16),
        pltpu.VMEM((heads, tall, LANES), BF16), pltpu.VMEM((heads, LANES, tall), BF16),
        pltpu.VMEM((heads, tall, LANES), F32), pltpu.VMEM((width, tall), BF16),
        dma_sems(24),
    ]
    scratch += exchange_scratch(rows, width, BF16, BACK_PIECES) + gather_sems(BACK_PIECES) + gather_sems(BACK_PIECES)
    if behind:
        scratch += owner_scratch(count, width, columns, 2)
    if split:
        scratch += total_scratch(count, width, units, 2) + total_scratch(count, width, units, 2)
        scratch += small_sum_scratch(count, width)
    if last:
        scratch += total_scratch(count, width, columns, 4) + small_sum_scratch(count, width)
    elif split:
        scratch += pair_scratch(count, width, columns, 4)
    return pl.pallas_call(
        functools.partial(layer_backward_kernel, layer, count, split, behind, last),
        out_shape=outs,
        in_specs=[VM] * 5 + [ANY] * 16 + [SM] + ([ANY, VM] if behind else []),
        out_specs=out_specs,
        scratch_shapes=scratch,
        compiler_params=params(5 + layer),
        name="layer_bwd",
    )(grad, normal2, recip2, gain, recip1, *hbm, prefix, *(earlier if behind else ()))


def results_kernel(depth, *refs):
    refs = Refs(refs)
    state_in, grad_in = refs.take(2)
    attn, up, down = refs.take(2), refs.take(2), refs.take(2)
    tail, smalls = refs.one(), refs.take(2)
    state, grad, wqkv, bias_qv, wout, bias_out, gain, shift, wup, bias_up, wdown, bias_down = refs.take(12)
    state[...] = state_in[...]
    grad[...] = grad_in[...]
    for layer in range(2):
        wout[layer] = attn[layer][:, :depth].T
        for kind in range(3):
            wqkv[layer, kind] = attn[layer][:, (kind + 1) * depth : (kind + 2) * depth]
        wup[layer] = up[layer][...]
        wdown[layer] = down[layer][...]
        sums = smalls[layer]
        row = slice(layer, layer + 1)
        bias_down[row] = sums[0:1]
        gain[layer, 1:2] = sums[1:2]
        shift[layer, 1:2] = sums[2:3]
        gain[layer, 0:1] = sums[3:4]
        shift[layer, 0:1] = sums[4:5]
        bias_out[row] = sums[5:6]
        bias_up[row] = sums[6:7]
        biases = tail if layer == 0 else smalls[0]
        for kind in range(2):
            bias_qv[layer, kind : kind + 1] = biases[7:8, kind * depth : (kind + 1) * depth]


def results(state, grad, attn, up, down, tail, smalls, depth):
    rows, width = state.shape
    share, units = up[0].shape
    layers = len(attn)
    outs = pl.pallas_call(
        functools.partial(results_kernel, depth),
        out_shape=[
            shape((rows, width)), shape((rows, width)), shape((layers, 3, share, depth)),
            shape((layers, 2, depth)), shape((layers, depth, share)), shape((layers, width)),
            shape((layers, 2, width)), shape((layers, 2, width)), shape((layers, share, units)),
            shape((layers, units)), shape((layers, share, units)), shape((layers, width)),
        ],
        in_specs=[VM] * 11,
        out_specs=[VM] * 12,
        compiler_params=pltpu.CompilerParams(vmem_limit_bytes=VMEM_BYTES),
        name="results",
    )(state, grad, *attn, *up, *down, tail, *smalls)
    return (*outs[:10], jnp.swapaxes(outs[10], 1, 2), outs[11])


def local(
    tokens,
    cotangent,
    prefix,
    w_qkv,
    bias_qv,
    w_out,
    bias_out,
    norm_gain,
    norm_bias,
    w_up,
    bias_up,
    w_down,
    bias_down,
):
    width = tokens.shape[1]
    layer_count = w_qkv.shape[0]
    depth = w_out.shape[1]
    w_qkv = jnp.swapaxes(w_qkv, 2, 3)
    state, low = tokens, tokens
    stored = []
    for layer in range(layer_count):
        state, low, normal1, recip1, normal2, recip2, *saved = layer_forward(
            layer, state, low, w_qkv, bias_qv, w_out, bias_out, norm_gain, norm_bias, w_up, bias_up, w_down,
            bias_down, prefix,
        )
        normed, active, slope = saved[8:]
        stored.append(((normal2, recip2), (active, slope, normed, normal1, recip1), saved[:8]))
    count = lax.axis_size("dp")
    split = count > 2 and count % 2 == 0 and (width // count) % 16 == 0
    grad = cotangent
    earlier = None
    attn, up, down, smalls, biases = [], [], [], [], []
    for layer in reversed(range(layer_count)):
        (normal2, recip2), (active, slope, normed, normal1, recip1), saved = stored[layer]
        hbm = (w_down, w_up, active, slope, normed, normal1, w_out, w_qkv, *saved)
        grad, bias, *rest = layer_back(
            layer, count, split, grad, normal2, recip2, norm_gain, recip1, hbm, prefix, earlier
        )
        if split and layer == 0:
            up_sum, down_sum, small, *rest = rest
            attn = rest[: len(rest) - 2] + attn
            attn.insert(0, rest[-2])
            return results(
                state, grad, attn, [up_sum] + up, [down_sum] + down, rest[-1], [small] + smalls, depth
            )
        attn_grad, up_grad, down_grad, small, *rest = rest
        if split:
            earlier = (attn_grad, bias)
            attn = rest + attn
        else:
            attn.insert(0, attn_grad)
        up.insert(0, up_grad)
        down.insert(0, down_grad)
        smalls.insert(0, small)
        biases.insert(0, bias[7, : 2 * depth].reshape(2, depth))
    scatter = functools.partial(lax.psum_scatter, axis_name="dp", scatter_dimension=1, tiled=True)
    attn_sum, up_sum, down_sum = [scatter(jnp.stack(each)) for each in (attn, up, down)]
    shared = lax.psum(jnp.stack(smalls)[:, :6], ("dp", "tensor"))
    bias_qv_sum, bias_up_sum = lax.psum((jnp.stack(biases), jnp.stack(smalls)[:, 6]), "dp")
    share = attn_sum.shape[1]
    return (
        state,
        grad,
        jnp.moveaxis(attn_sum[:, :, depth:].reshape(layer_count, share, 3, depth), 2, 1),
        bias_qv_sum,
        jnp.swapaxes(attn_sum[:, :, :depth], 1, 2),
        shared[:, 5],
        jnp.stack([shared[:, 3], shared[:, 1]], axis=1),
        jnp.stack([shared[:, 4], shared[:, 2]], axis=1),
        up_sum,
        bias_up_sum,
        jnp.swapaxes(down_sum, 1, 2),
        shared[:, 0],
    )


def solution(mesh):
    in_specs = (
        P(("dp", "tensor"), None),
        P(("dp", "tensor"), None),
        P("dp"),
        P(None, None, None, "tensor"),
        P(None, None, "tensor"),
        P(None, "tensor", None),
        P(),
        P(),
        P(),
        P(None, None, "tensor"),
        P(None, "tensor"),
        P(None, "tensor", None),
        P(),
    )
    out_specs = (
        P(("dp", "tensor"), None),
        P(("dp", "tensor"), None),
        P(None, None, "dp", "tensor"),
        P(None, None, "tensor"),
        P(None, "tensor", "dp"),
        P(),
        P(),
        P(),
        P(None, "dp", "tensor"),
        P(None, "tensor"),
        P(None, "tensor", "dp"),
        P(),
    )
    return jax.shard_map(local, mesh=mesh, in_specs=in_specs, out_specs=out_specs, check_vma=False)
```

```python
import functools
import math

import jax
import jax.numpy as jnp
from jax import lax
from jax.experimental import pallas as pl
from jax.experimental.pallas import tpu as pltpu
from jax.sharding import PartitionSpec as P

HDIM = 64
LEN = 1024
MEM = 10
LANES = 128
GROUP = 4
EPSILON = 1e-06
VMEM_BYTES = 62 * 1024 * 1024
HIGHEST = lax.Precision.HIGHEST
MESH = pl.DeviceIdType.MESH
F32 = jnp.float32
BF16 = jnp.bfloat16
VM = pl.BlockSpec(memory_space=pltpu.VMEM)
SM = pl.BlockSpec(memory_space=pltpu.SMEM)
ANY = pl.BlockSpec(memory_space=pl.ANY)


def dot(left, right):
    return jnp.dot(left, right, preferred_element_type=F32)


def dot_nt(left, right):
    return lax.dot_general(left, right, (((1,), (1,)), ((), ())), preferred_element_type=F32)


def remote(src, dst, send_sem, recv_sem, tensor_index):
    return pltpu.make_async_remote_copy(
        src_ref=src,
        dst_ref=dst,
        send_sem=send_sem,
        recv_sem=recv_sem,
        device_id={"tensor": tensor_index},
        device_id_type=MESH,
    )


def places():
    mine = lax.axis_index("tensor")
    chip = mine // 2
    core = mine - 2 * chip
    partner = mine + 1 - 2 * core
    across = mine + 2 - 4 * chip
    diagonal = across + 1 - 2 * core
    return mine, partner, across, diagonal


class Refs:
    def __init__(self, refs):
        self.refs = list(refs)

    def take(self, count):
        taken, self.refs = self.refs[:count], self.refs[count:]
        return taken

    def one(self):
        return self.take(1)[0]


class Moves:
    def __init__(self, sems):
        self.sems, self.used, self.pending = sems, 0, []

    def start(self, source, target):
        move = pltpu.make_async_copy(source, target, self.sems.at[self.used])
        self.used += 1
        move.start()
        return move

    def store(self, source, target):
        self.pending.append(self.start(source, target))

    def finish(self):
        for move in self.pending:
            move.wait()


def remote_dp(src, dst, send_sem, recv_sem, dp_index):
    return pltpu.make_async_remote_copy(
        src_ref=src,
        dst_ref=dst,
        send_sem=send_sem,
        recv_sem=recv_sem,
        device_id={"dp": dp_index},
        device_id_type=MESH,
    )


class Sequences:
    def __init__(self, count):
        self.pairs = count // 2
        self.index = lax.axis_index("dp")
        self.pair = self.index // 2
        self.side = self.index - 2 * self.pair
        self.neighbour = self.index + 1 - 2 * self.side

    def other_pair(self, offset):
        return lax.rem(self.pair + offset, self.pairs)

    def peer(self, offset):
        return 2 * self.other_pair(offset) + self.side

    def everyone(self):
        return [self.neighbour] + [self.peer(offset) for offset in range(1, self.pairs)]


class Entry:
    def __init__(self, sequences=None):
        barrier = pltpu.get_barrier_semaphore()
        group = places()[1:]
        others = sequences.everyone() if sequences is not None else []
        for other in group:
            pl.semaphore_signal(barrier, inc=1, device_id={"tensor": other}, device_id_type=MESH)
        for other in others:
            pl.semaphore_signal(barrier, inc=1, device_id={"dp": other}, device_id_type=MESH)
        self.barrier, self.count = barrier, len(group) + len(others)

    def wait(self):
        pl.semaphore_wait(self.barrier, self.count)


class Gather:
    def __init__(self, whole, send_sems, recv_sems, pieces):
        self.whole = whole
        self.pieces = pieces
        self.mine, self.partner, self.across, self.diagonal = places()
        self.rows = whole.shape[1] // pieces
        self.send_sems, self.recv_sems = send_sems, recv_sems

    def piece(self, chunk, part):
        return self.whole.at[chunk, pl.ds(part * self.rows, self.rows)]

    def to_partner(self):
        return remote(
            self.whole.at[self.mine], self.whole.at[self.mine],
            self.send_sems.at[0], self.recv_sems.at[0], self.partner,
        )

    def to_across(self, part):
        return remote(
            self.piece(self.mine, part), self.piece(self.mine, part),
            self.send_sems.at[1 + part], self.recv_sems.at[1 + part], self.across,
        )

    def onward(self, part):
        return remote(
            self.piece(self.across, part), self.piece(self.across, part),
            self.send_sems.at[1 + self.pieces + part], self.recv_sems.at[1 + self.pieces + part], self.partner,
        )

    def start(self):
        for part in range(self.pieces):
            self.to_across(part).start()
        self.to_partner().start()

    def wait_partner(self):
        remote(
            self.whole.at[self.partner], self.whole.at[self.partner],
            self.send_sems.at[0], self.recv_sems.at[0], self.partner,
        ).wait_recv()

    def wait_across(self, part):
        remote(
            self.piece(self.across, part), self.piece(self.across, part),
            self.send_sems.at[1 + part], self.recv_sems.at[1 + part], self.across,
        ).wait_recv()

    def wait_diagonal(self, part):
        remote(
            self.piece(self.diagonal, part), self.piece(self.diagonal, part),
            self.send_sems.at[1 + self.pieces + part], self.recv_sems.at[1 + self.pieces + part], self.partner,
        ).wait_recv()

    def wait_sends(self):
        self.to_partner().wait_send()
        for part in range(self.pieces):
            self.to_across(part).wait_send()
            self.onward(part).wait_send()


ATTN_PIECES = 2
FFN_PIECES = 4
BACK_PIECES = 2


def gather_sems(pieces):
    return [dma_sems(1 + 2 * pieces), dma_sems(1 + 2 * pieces)]


def shape(dims, kind=F32):
    return jax.ShapeDtypeStruct(dims, kind)


def dma_sems(*dims):
    return pltpu.SemaphoreType.DMA(dims)


def params(collective_id):
    return pltpu.CompilerParams(
        collective_id=collective_id, has_side_effects=True, vmem_limit_bytes=VMEM_BYTES
    )


def layer_norm(total, gain, shift):
    row_mean = jnp.mean(total, axis=-1, keepdims=True)
    centered = total - row_mean
    spread = jnp.mean(centered * centered, axis=-1, keepdims=True)
    recip = lax.rsqrt(spread + EPSILON)
    normal = centered * recip
    return normal * gain + shift, normal, recip


def visible_keys(chunk, rows):
    first, last = chunk * rows, (chunk + 1) * rows - 1
    if first < MEM or last >= LEN - MEM:
        return LEN
    return max(last + 1, LEN // 2)


def query_limits(chunk, rows, prefix_len):
    spots = chunk * rows + lax.broadcasted_iota(jnp.int32, (1, rows), 1)
    limits = jnp.maximum(spots, prefix_len - 1)
    return jnp.where((spots < MEM) | (spots >= LEN - MEM), LEN - 1, limits)


def transposed(values):
    return values.astype(F32).T


def head_pairs(values, heads):
    wide = []
    for head in range(heads):
        columns = values[:, head * HDIM : (head + 1) * HDIM]
        wide.append(jnp.concatenate([columns, columns], axis=1))
    return wide


class Exchange:
    def __init__(self, terms, near, relay, total, far, sems, pieces):
        self.terms, self.near, self.relay, self.total, self.far = terms, near, relay, total, far
        self.n_send, self.n_recv, self.r_send, self.r_recv, self.f_send, self.f_recv = sems
        self.mine, self.partner, self.across, self.diagonal = places()
        self.pieces = pieces
        self.rows = terms.shape[1] // pieces

    def spot(self, part):
        return pl.ds(part * self.rows, self.rows)

    def near_copy(self, part):
        return remote(
            self.terms.at[self.partner, self.spot(part)], self.near.at[self.spot(part)],
            self.n_send.at[part], self.n_recv.at[part], self.partner,
        )

    def relay_copy(self, part):
        return remote(
            self.terms.at[self.diagonal, self.spot(part)], self.relay.at[self.spot(part)],
            self.r_send.at[part], self.r_recv.at[part], self.partner,
        )

    def far_copy(self, part):
        return remote(
            self.total.at[self.spot(part)], self.far.at[self.spot(part)],
            self.f_send.at[part], self.f_recv.at[part], self.across,
        )

    def pass_on(self, part):
        spot = self.spot(part)
        self.relay_copy(part).wait_recv()
        self.total[spot] = (self.terms[self.across, spot] + self.relay[spot]).astype(self.total.dtype)
        self.far_copy(part).start()

    def result(self, part):
        spot = self.spot(part)
        self.near_copy(part).wait_recv()
        self.far_copy(part).wait_recv()
        return (self.terms[self.mine, spot] + self.near[spot]) + self.far[spot].astype(F32)

    def wait_sends(self):
        for part in range(self.pieces):
            self.near_copy(part).wait_send()
            self.relay_copy(part).wait_send()
            self.far_copy(part).wait_send()


def exchange_scratch(rows, width, kind, pieces):
    return [
        pltpu.VMEM((GROUP, rows, width), F32),
        pltpu.VMEM((rows, width), F32), pltpu.VMEM((rows, width), F32),
        pltpu.VMEM((rows, width), kind), pltpu.VMEM((rows, width), kind),
    ] + [dma_sems(pieces)] * 6


def layer_forward_kernel(layer, *refs):
    refs = Refs(refs)
    state_hbm, low_ref, wqkv_hbm, bias_ref, wout_hbm, bias_out_ref, gain_ref, shift_ref = refs.take(8)
    wup_hbm, bias_up_ref, wdown_hbm, bias_down_ref, prefix_ref = refs.take(5)
    next_ref, next_low_ref, normal1_ref, recip1_ref, normal2_ref, recip2_ref = refs.take(6)
    saved_hbm, ffn_saved_hbm = refs.take(8), refs.take(3)
    saved = refs.take(8)
    whole_ref, qt_ref, q2_ref, kz_ref, kt_ref, v2_ref, ct_ref, stats_ref = saved
    state_ref, wqkv_ref, vt_ref, cf_ref, wo_ref = refs.take(5)
    normed_ref, active_ref, slope_ref = refs.take(3)
    total_ref, wup_ref, wdown_ref = refs.take(3)
    moves = Moves(refs.one())
    g_send, g_recv, c_send, c_recv, w_send, w_recv = refs.take(6)
    exchange_refs, second_sems = refs.take(11), refs.take(2)
    mine, partner, across, diagonal = places()
    rows = low_ref.shape[0]
    heads = qt_ref.shape[0]
    root = 1.0 / math.sqrt(HDIM)
    entry = Entry()
    wqkv_in = moves.start(wqkv_hbm.at[layer], wqkv_ref)
    wout_in = moves.start(wout_hbm.at[layer], wo_ref.at[mine])
    state_in = moves.start(state_hbm, state_ref)
    wup_in = moves.start(wup_hbm.at[layer], wup_ref)
    wdown_in = moves.start(wdown_hbm.at[layer], wdown_ref)
    gather = Gather(whole_ref, g_send, g_recv, ATTN_PIECES)
    whole_ref[mine] = low_ref[...]
    entry.wait()
    gather.start()
    lane_low = lax.broadcasted_iota(jnp.int32, (rows, LANES), 1) < HDIM

    def project(chunk):
        spots = pl.ds(pl.multiple_of(chunk * rows, rows), rows)
        values = whole_ref[chunk]
        query = (dot_nt(values, wqkv_ref[0]) + bias_ref[layer, 0:1]) * root
        key = dot_nt(values, wqkv_ref[1])
        value = dot_nt(values, wqkv_ref[2]) + bias_ref[layer, 1:2]
        queries, keys, valuess = [head_pairs(each, heads) for each in (query, key, value)]
        query_t, key_t, value_t = [each.T.astype(BF16) for each in (query, key, value)]
        for head in range(heads):
            part = slice(head * HDIM, (head + 1) * HDIM)
            q2_ref[head, spots] = queries[head].astype(BF16)
            kz_ref[head, spots] = jnp.where(lane_low, keys[head], 0.0).astype(BF16)
            v2_ref[head, spots] = valuess[head].astype(BF16)
            for half in (slice(0, HDIM), slice(HDIM, 2 * HDIM)):
                qt_ref[head, half, spots] = query_t[part]
                kt_ref[head, half, spots] = key_t[part]
            vt_ref[head, :, spots] = value_t[part]

    def wout_to_partner(source):
        slot = 0 if source is mine else 2
        return remote(wo_ref.at[source], wo_ref.at[source], w_send.at[slot], w_recv.at[slot], partner)

    wout_to_across = remote(wo_ref.at[mine], wo_ref.at[mine], w_send.at[1], w_recv.at[1], across)
    wout_from_across = remote(wo_ref.at[across], wo_ref.at[across], w_send.at[1], w_recv.at[1], across)
    wout_from_partner = remote(wo_ref.at[partner], wo_ref.at[partner], w_send.at[0], w_recv.at[0], partner)
    wout_from_diagonal = remote(wo_ref.at[diagonal], wo_ref.at[diagonal], w_send.at[2], w_recv.at[2], partner)

    wqkv_in.wait()
    project(mine)
    gather.wait_partner()
    project(partner)
    wout_in.wait()
    for part in range(ATTN_PIECES):
        gather.wait_across(part)
        gather.onward(part).start()
    wout_to_across.start()
    wout_to_partner(mine).start()
    project(across)
    for part in range(ATTN_PIECES):
        gather.wait_diagonal(part)
    project(diagonal)
    for source, target in zip(saved[:6], saved_hbm[:6]):
        moves.store(source, target)

    def context_copy(step, chunk):
        return remote(ct_ref.at[chunk], cf_ref.at[mine], c_send.at[step], c_recv.at[step], chunk)

    def context_from(step, chunk):
        return remote(ct_ref.at[mine], cf_ref.at[chunk], c_send.at[step], c_recv.at[step], chunk)

    def attend(chunk):
        keys = visible_keys(chunk, rows)
        limits = query_limits(chunk, rows, prefix_ref[0])
        visible = lax.broadcasted_iota(jnp.int32, (keys, rows), 0) <= limits
        spots = pl.ds(chunk * rows, rows)

        def one_head(head, carry):
            scores = dot(kz_ref[head, pl.ds(0, keys)], qt_ref[head, :, spots])
            scores = jnp.where(visible, scores, -1e30)
            top = jnp.max(scores, axis=0, keepdims=True)
            expo = jnp.exp(scores - top)
            recip = 1.0 / jnp.sum(expo, axis=0, keepdims=True)
            probs = (expo * recip).astype(BF16)
            context = dot(vt_ref[head, :, pl.ds(0, keys)], probs)
            ct_ref[chunk, pl.ds(pl.multiple_of(head * HDIM, HDIM), HDIM)] = context.astype(BF16)
            first = lax.broadcasted_iota(jnp.int32, (8, rows), 0) == 0
            stats_ref[head, :, spots] = jnp.where(first, top, recip)
            return carry

        lax.fori_loop(0, heads, one_head, 0)

    chip, core = mine // 2, mine - 2 * (mine // 2)

    def one_step(step, carry):
        near = step // 2
        flip = lax.rem(lax.rem(step, 2) + near, 2)
        to_chip = (1 - near) * (1 - chip) + near * chip
        chunk = 2 * to_chip + core + flip * (1 - 2 * core)
        for each in range(GROUP):
            @pl.when(chunk == each)
            def _():
                attend(each)

        @pl.when(step < 3)
        def _():
            context_copy(step, chunk).start()

        @pl.when(step == 1)
        def _():
            wout_from_across.wait_recv()
            wout_to_partner(across).start()
        return carry

    lax.fori_loop(0, GROUP, one_step, 0)
    for source, target in zip(saved[6:], saved_hbm[6:]):
        moves.store(source, target)
    cf_ref[mine] = ct_ref[mine]
    wout_from_partner.wait_recv()
    wout_from_diagonal.wait_recv()
    for step, chunk in enumerate((across, diagonal, partner)):
        context_from(step, chunk).wait_recv()
    depth = GROUP * wo_ref.shape[1]
    context = transposed(cf_ref[...].reshape(depth, rows)).astype(BF16)
    state_in.wait()
    total_ref[...] = (
        state_ref[...].astype(F32) + dot(context, wo_ref[...].reshape(depth, -1)) + bias_out_ref[layer : layer + 1]
    )
    second = Gather(normed_ref, *second_sems, FFN_PIECES)
    exchange = Exchange(*exchange_refs[:5], exchange_refs[5:], FFN_PIECES)
    terms_ref = exchange.terms
    part_rows = rows // FFN_PIECES
    for part in range(FFN_PIECES):
        spot = exchange.spot(part)
        result, normal, recip = layer_norm(total_ref[spot], gain_ref[layer, 0:1], shift_ref[layer, 0:1])
        normed_ref[mine, spot] = result.astype(BF16)
        second.to_across(part).start()
        total_ref[spot] = result
        normal1_ref[spot] = normal
        recip1_ref[spot] = jnp.broadcast_to(recip, (part_rows, LANES))
    second.to_partner().start()
    gather.wait_sends()
    wout_to_across.wait_send()
    wout_to_partner(mine).wait_send()
    wout_to_partner(across).wait_send()
    for step, chunk in enumerate((across, diagonal, partner)):
        context_copy(step, chunk).wait_send()

    def units(chunk, part):
        spot = exchange.spot(part)
        hidden = dot(normed_ref[chunk, spot], wup_ref[...]) + bias_up_ref[layer : layer + 1]
        below = 0.5 * (1.0 + lax.erf(hidden * math.sqrt(0.5)))
        density = jnp.exp(-0.5 * hidden * hidden) * (1.0 / math.sqrt(2.0 * math.pi))
        active = (hidden * below).astype(BF16)
        active_ref[chunk, spot] = active
        slope_ref[chunk, spot] = below + hidden * density
        terms_ref[chunk, spot] = dot(active, wdown_ref[...])

    wup_in.wait()
    wdown_in.wait()
    for part in range(FFN_PIECES):
        units(mine, part)
    for part in range(FFN_PIECES):
        second.wait_across(part)
        second.onward(part).start()
        units(across, part)
        second.wait_diagonal(part)
        units(diagonal, part)
        exchange.relay_copy(part).start()
        if part > 0:
            exchange.pass_on(part - 1)
    second.wait_partner()
    moves.store(normed_ref, ffn_saved_hbm[0])
    units(partner, 0)
    exchange.near_copy(0).start()
    exchange.pass_on(FFN_PIECES - 1)
    for part in range(1, FFN_PIECES):
        units(partner, part)
        exchange.near_copy(part).start()
    moves.store(active_ref, ffn_saved_hbm[1])
    moves.store(slope_ref, ffn_saved_hbm[2])
    for part in range(FFN_PIECES):
        spot = exchange.spot(part)
        total = total_ref[spot] + exchange.result(part) + bias_down_ref[layer : layer + 1]
        result, normal, recip = layer_norm(total, gain_ref[layer, 1:2], shift_ref[layer, 1:2])
        next_ref[spot] = result
        next_low_ref[spot] = result.astype(BF16)
        normal2_ref[spot] = normal
        recip2_ref[spot] = jnp.broadcast_to(recip, (part_rows, LANES))
    second.wait_sends()
    exchange.wait_sends()
    moves.finish()


def layer_forward(layer, state, low, wqkv, bias, wout, bias_out, gain, shift, wup, bias_up, wdown, bias_down, prefix):
    rows, width = low.shape
    depth = wout.shape[1]
    units = wup.shape[2]
    heads = depth // HDIM
    tall = GROUP * rows
    saved = [
        ((GROUP, rows, width), BF16),
        ((heads, LANES, tall), BF16), ((heads, tall, LANES), BF16), ((heads, tall, LANES), BF16),
        ((heads, LANES, tall), BF16), ((heads, tall, LANES), BF16), ((GROUP, depth, rows), BF16),
        ((heads, 8, tall), F32),
    ]
    ffn_saved = [((GROUP, rows, width), BF16), ((GROUP, rows, units), BF16), ((GROUP, rows, units), F32)]
    norms = [shape((rows, width)), shape((rows, LANES))]
    return pl.pallas_call(
        functools.partial(layer_forward_kernel, layer),
        out_shape=[shape((rows, width)), shape((rows, width), BF16)] + norms + norms
        + [shape(*each) for each in saved + ffn_saved],
        in_specs=[ANY, VM, ANY, VM, ANY, VM, VM, VM, ANY, VM, ANY, VM, SM],
        out_specs=[VM] * 6 + [ANY] * 11,
        scratch_shapes=[pltpu.VMEM(*each) for each in saved] + [
            pltpu.VMEM((rows, width), state.dtype),
            pltpu.VMEM(wqkv.shape[1:], BF16),
            pltpu.VMEM((heads, HDIM, tall), BF16),
            pltpu.VMEM((GROUP, depth, rows), BF16),
            pltpu.VMEM((GROUP, depth, width), BF16),
        ] + [pltpu.VMEM(*each) for each in ffn_saved] + [
            pltpu.VMEM((rows, width), F32), pltpu.VMEM(wup.shape[1:], BF16), pltpu.VMEM(wdown.shape[1:], BF16),
            dma_sems(16),
            *gather_sems(ATTN_PIECES),
            dma_sems(3), dma_sems(3), dma_sems(3), dma_sems(3),
        ] + exchange_scratch(rows, width, F32, FFN_PIECES) + gather_sems(FFN_PIECES),
        compiler_params=params(1 + layer),
        name="layer_fwd",
    )(state, low, wqkv, bias, wout, bias_out, gain, shift, wup, bias_up, wdown, bias_down, prefix)


def layer_norm_back(grad_in, normal, recip, gain):
    scaled = grad_in * gain
    inner = (
        scaled
        - jnp.mean(scaled, axis=-1, keepdims=True)
        - normal * jnp.mean(scaled * normal, axis=-1, keepdims=True)
    )
    return recip * inner


def column_sum(values):
    return jnp.sum(values, axis=0, keepdims=True)


def high_low(values):
    high = values.astype(BF16)
    return high, (values - high.astype(F32)).astype(BF16)


def dot_tn(left, right):
    return lax.dot_general(left, right, (((0,), (0,)), ((), ())), preferred_element_type=F32)


def owner_rows(pair, side, rows):
    return pl.ds(pl.multiple_of((2 * pair + side) * rows, 16), rows)


class PairSum:
    def __init__(self, sequences, source, columns, buffers, sems):
        self.at, self.source, self.columns = sequences, source, columns
        self.out, self.into = buffers
        self.sems = sems
        self.rows = self.out.shape[1]

    def copy(self):
        return remote_dp(
            self.out.at[:, :, self.columns], self.into.at[:, :, self.columns], *self.sems, self.at.neighbour
        )

    def start(self):
        for pair in range(self.at.pairs):
            place = (owner_rows(pair, 1 - self.at.side, self.rows), self.columns)
            self.out[pair, :, self.columns] = self.source[place].astype(BF16)
        self.copy().start()

    def finish(self):
        self.copy().wait_recv()
        for pair in range(self.at.pairs):
            place = (owner_rows(pair, self.at.side, self.rows), self.columns)
            self.source[place] = self.source[place] + self.into[pair, :, self.columns].astype(F32)

    def wait_sends(self):
        self.copy().wait_send()


class OwnerSum:
    def __init__(self, sequences, source, result, columns, buffers, sems):
        self.at, self.source, self.result, self.columns = sequences, source, result, columns
        self.out, self.into = buffers
        self.sems = sems
        self.rows = result.shape[0]

    def terms(self, pair):
        return self.source[owner_rows(pair, self.at.side, self.rows), self.columns]

    def copy(self, offset):
        return remote_dp(
            self.out.at[offset - 1, :, self.columns], self.into.at[offset - 1, :, self.columns],
            self.sems[0].at[offset - 1], self.sems[1].at[offset - 1], self.at.peer(offset),
        )

    def start(self):
        for offset in range(1, self.at.pairs):
            pair = self.at.other_pair(offset)
            self.out[offset - 1, :, self.columns] = self.terms(pair).astype(BF16)
            self.copy(offset).start()

    def finish(self):
        total = self.terms(self.at.pair)
        for offset in range(1, self.at.pairs):
            self.copy(offset).wait_recv()
            total = total + self.into[offset - 1, :, self.columns].astype(F32)
        self.result[:, self.columns] = total

    def wait_sends(self):
        for offset in range(1, self.at.pairs):
            self.copy(offset).wait_send()


def halves(columns):
    return (slice(0, columns // 2), slice(columns // 2, columns))


def tile_blocks(columns):
    tiles = columns // LANES
    ends = [0, 1, 1 + (tiles - 1) * 2 // 5, 1 + (tiles - 1) * 4 // 5, tiles]
    return [slice(first * LANES, end * LANES) for first, end in zip(ends, ends[1:])]


def pair_scratch(count, width, columns, blocks):
    dims = (count // 2, width // count, columns)
    return [pltpu.VMEM(dims, BF16), pltpu.VMEM(dims, BF16), dma_sems(blocks), dma_sems(blocks)]


def owner_scratch(count, width, columns, blocks):
    pairs = count // 2
    dims = (pairs - 1, width // count, columns)
    return [
        pltpu.VMEM(dims, BF16), pltpu.VMEM(dims, BF16), dma_sems(blocks, pairs - 1), dma_sems(blocks, pairs - 1)
    ]


def total_scratch(count, width, columns, blocks):
    return pair_scratch(count, width, columns, blocks) + owner_scratch(count, width, columns, blocks)


def pair_sums(sequences, source, scratch, blocks):
    out, into, send, recv = scratch
    return [
        PairSum(sequences, source, columns, (out, into), (send.at[block], recv.at[block]))
        for block, columns in enumerate(blocks)
    ]


def owner_sums(sequences, source, result, scratch, blocks):
    out, into, send, recv = scratch
    return [
        OwnerSum(sequences, source, result, columns, (out, into), (send.at[block], recv.at[block]))
        for block, columns in enumerate(blocks)
    ]


def total_sums(sequences, source, result, scratch, blocks):
    pairs = pair_sums(sequences, source, scratch[:4], blocks)
    owners = owner_sums(sequences, source, result, scratch[4:], blocks)
    return [BlockSum(pair, owner) for pair, owner in zip(pairs, owners)]


TOTAL_REFS = 8


class BlockSum:
    def __init__(self, pair, owner):
        self.pair, self.owner = pair, owner
        self.start, self.finish = pair.start, owner.finish

    def turn(self):
        self.pair.finish()
        self.owner.start()

    def wait_sends(self):
        self.pair.wait_sends()
        self.owner.wait_sends()


class SmallSum:
    def __init__(self, sequences, source, result, shared_rows, slots, sems):
        self.at = sequences
        self.source, self.result, self.shared_rows = source, result, shared_rows
        self.group_slots, self.side_slots, self.pair_slots = slots
        self.g_send, self.g_recv, self.s_send, self.s_recv, self.p_send, self.p_recv = sems
        self.mine, self.partner, self.across, self.diagonal = places()

    def group_copy(self, index, to, slot):
        return remote(
            self.group_slots.at[slot], self.group_slots.at[slot],
            self.g_send.at[index], self.g_recv.at[index], to,
        )

    def start(self):
        if self.shared_rows:
            self.group_slots[self.mine] = self.source[...]
            for index, other in enumerate((self.partner, self.across, self.diagonal)):
                self.group_copy(index, other, self.mine).start()

    def side_copy(self, slot):
        return remote_dp(
            self.side_slots.at[slot], self.side_slots.at[slot],
            self.s_send.at[0], self.s_recv.at[0], self.at.neighbour,
        )

    def first(self):
        values = self.source[...]
        if self.shared_rows:
            for index, other in enumerate((self.partner, self.across, self.diagonal)):
                self.group_copy(index, other, other).wait_recv()
            total = self.group_slots[0]
            for slot in range(1, GROUP):
                total = total + self.group_slots[slot]
            shared = lax.broadcasted_iota(jnp.int32, values.shape, 0) < self.shared_rows
            values = jnp.where(shared, total, values)
        self.side_slots[self.at.side] = values
        self.side_copy(self.at.side).start()

    def pair_copy(self, offset, slot):
        return remote_dp(
            self.pair_slots.at[slot], self.pair_slots.at[slot],
            self.p_send.at[offset - 1], self.p_recv.at[offset - 1], self.at.peer(offset),
        )

    def second(self):
        self.side_copy(1 - self.at.side).wait_recv()
        self.pair_slots[self.at.pair] = self.side_slots[0] + self.side_slots[1]
        for offset in range(1, self.at.pairs):
            self.pair_copy(offset, self.at.pair).start()

    def third(self):
        for offset in range(1, self.at.pairs):
            self.pair_copy(offset, self.at.other_pair(self.at.pairs - offset)).wait_recv()
        total = self.pair_slots[0]
        for slot in range(1, self.at.pairs):
            total = total + self.pair_slots[slot]
        self.result[...] = total

    def wait_sends(self):
        if self.shared_rows:
            for index, other in enumerate((self.partner, self.across, self.diagonal)):
                self.group_copy(index, other, self.mine).wait_send()
        self.side_copy(self.at.side).wait_send()
        for offset in range(1, self.at.pairs):
            self.pair_copy(offset, self.at.pair).wait_send()


def small_sum_scratch(count, width):
    pairs = count // 2
    return [
        pltpu.VMEM((GROUP, 8, width), F32), pltpu.VMEM((2, 8, width), F32), pltpu.VMEM((pairs, 8, width), F32),
        dma_sems(3), dma_sems(3), dma_sems(1), dma_sems(1), dma_sems(pairs - 1), dma_sems(pairs - 1),
    ]


def layer_backward_kernel(layer, count, split, behind, last, *refs):
    refs = Refs(refs)
    grad_ref, normal2_ref, recip2_ref, gain_ref, recip1_ref = refs.take(5)
    wdown_hbm, wup_hbm, active_hbm, slope_hbm, normed_hbm, normal1_hbm, wout_hbm, wqkv_hbm = refs.take(8)
    whole_hbm, *saved_hbm = refs.take(8)
    prefix_ref = refs.one()
    earlier_hbm, bias_in = refs.take(2) if behind else (None,) * 2
    dx_ref, bias_ref = refs.take(2)
    grads_hbm = None if last else refs.one()
    up_out, down_out, smalls_out = refs.take(3)
    earlier_sum = refs.one() if behind else None
    grads_sum, bias_sum = refs.take(2) if last else (None,) * 2
    df_ref, do_ref, du_ref, high_ref, lowbits_ref = refs.take(5)
    wdown_ref, wup_ref, active_ref, wide_ref, normed_ref, normal1_ref = refs.take(6)
    up_ref, down_ref, grads_ref, smalls_ref = refs.take(4)
    saved = refs.take(7)
    qt_ref, q2_ref, kz_ref, kt_ref, v2_ref, ct_ref, stats_ref = saved
    wout_ref, wqkv_ref = refs.take(2)
    dc_ref, dct_ref, dv_ref, xt_ref = refs.take(4)
    moves = Moves(refs.one())
    exchange_refs = refs.take(11)
    first_sems, second_sems = refs.take(2), refs.take(2)
    mine, partner, across, diagonal = places()
    rows, width = grad_ref.shape
    units = wup_ref.shape[1]
    tall = GROUP * rows
    part_rows = rows // BACK_PIECES
    heads = qt_ref.shape[0]
    depth = heads * HDIM
    span = width // 3
    scale = 1.0 / math.sqrt(HDIM)
    sequences = Sequences(count) if split else None
    entry = Entry(sequences)
    wdown_in = moves.start(wdown_hbm.at[layer], wdown_ref)
    wup_in = moves.start(wup_hbm.at[layer], wup_ref)
    slope_in = [
        moves.start(slope_hbm.at[chunk], wide_ref.at[pl.ds(chunk * rows, rows)]) for chunk in range(GROUP)
    ]
    earlier, ups, downs, own, small, own_small = [], [], [], [], None, None
    if behind:
        earlier_in = moves.start(earlier_hbm, grads_ref)
        earlier = owner_sums(sequences, grads_ref, earlier_sum, refs.take(4), halves(width))
    if split:
        downs = total_sums(sequences, down_ref, down_out, refs.take(TOTAL_REFS), halves(units))
        ups = total_sums(sequences, up_ref, up_out, refs.take(TOTAL_REFS), halves(units))
        small = SmallSum(sequences, smalls_ref, smalls_out, 6, refs.take(3), refs.take(6))
    if last:
        own = total_sums(sequences, grads_ref, grads_sum, refs.take(TOTAL_REFS), tile_blocks(width))
        own_small = SmallSum(sequences, bias_ref, bias_sum, 0, refs.take(3), refs.take(6))
    elif split:
        own = pair_sums(sequences, grads_ref, refs.take(4), tile_blocks(width))
    active_in = moves.start(active_hbm, active_ref)
    normed_in = moves.start(normed_hbm, normed_ref)
    normal1_in = moves.start(normal1_hbm, normal1_ref)
    wout_in = moves.start(wout_hbm.at[layer], wout_ref)
    wqkv_in = moves.start(wqkv_hbm.at[layer], wqkv_ref)
    saved_in = [moves.start(source, target) for source, target in zip(saved_hbm, saved)]
    first_gather = Gather(df_ref, *first_sems, BACK_PIECES)
    second_gather = Gather(do_ref, *second_sems, BACK_PIECES)
    exchange = Exchange(*exchange_refs[:5], exchange_refs[5:], BACK_PIECES)
    terms_ref = exchange.terms

    grad = grad_ref[...].astype(F32)
    normal2 = normal2_ref[...]
    du2 = layer_norm_back(grad, normal2, recip2_ref[:, :1], gain_ref[layer, 1:2])
    du_ref[...] = du2
    df_ref[mine] = du2.astype(BF16)
    entry.wait()
    first_gather.start()
    smalls_ref[0:1] = column_sum(du2)
    smalls_ref[1:2] = column_sum(grad * normal2)
    smalls_ref[2:3] = column_sum(grad)
    smalls_ref[6:7] = jnp.zeros((1, width), F32)
    smalls_ref[7:8] = bias_in[7:8] if behind else jnp.zeros((1, width), F32)
    wdown_in.wait()
    wdown_ref[...] = transposed(wdown_ref[...]).astype(BF16)
    wup_in.wait()
    wup_ref[...] = transposed(wup_ref[...]).astype(BF16)
    if behind:
        earlier_in.wait()
        for item in earlier:
            item.start()

    def part_spots(chunk, part):
        return pl.ds(pl.multiple_of(chunk * rows + part * part_rows, part_rows), part_rows)

    def back(chunk, part):
        spot, spots = exchange.spot(part), part_spots(chunk, part)
        grad_active = dot(df_ref[chunk, spot], wdown_ref[...])
        grad_hidden = grad_active * wide_ref[spots]
        smalls_ref[6:7] = smalls_ref[6:7] + column_sum(grad_hidden)
        high, low = high_low(grad_hidden)
        high_ref[spots] = high
        lowbits_ref[spots] = low
        terms_ref[chunk, spot] = dot(high, wup_ref[...]) + dot(low, wup_ref[...])

    for move in slope_in:
        move.wait()
    for part in range(BACK_PIECES):
        back(mine, part)
    for part in range(BACK_PIECES):
        first_gather.wait_across(part)
        first_gather.onward(part).start()
        back(across, part)
        first_gather.wait_diagonal(part)
        back(diagonal, part)
        exchange.relay_copy(part).start()
        if part > 0:
            exchange.pass_on(part - 1)
    first_gather.wait_partner()
    back(partner, 0)
    exchange.near_copy(0).start()
    exchange.pass_on(BACK_PIECES - 1)
    active_in.wait()
    down_ref[...] = dot_tn(df_ref[...].reshape(tall, width), active_ref[...].reshape(tall, units))
    for item in downs:
        item.start()
    for part in range(1, BACK_PIECES):
        back(partner, part)
        exchange.near_copy(part).start()
    normed_in.wait()
    normed = normed_ref[...].reshape(tall, width)
    up_ref[...] = dot_tn(normed, high_ref[...]) + dot_tn(normed, lowbits_ref[...])
    if split:
        ups[0].start()
    whole_in = moves.start(whole_hbm, normed_ref)
    if not split:
        moves.store(down_ref, down_out)
        moves.store(up_ref, up_out)
    normal1_in.wait()
    for part in range(BACK_PIECES):
        spot = exchange.spot(part)
        grad_normed = exchange.result(part) + du_ref[spot]
        normal1 = normal1_ref[spot]
        du = layer_norm_back(grad_normed, normal1, recip1_ref[spot, :1], gain_ref[layer, 0:1])
        du_ref[spot] = du
        do_ref[mine, spot] = du.astype(BF16)
        second_gather.to_across(part).start()
        sums = (column_sum(grad_normed * normal1), column_sum(grad_normed), column_sum(du))
        for index, value in enumerate(sums):
            place = slice(3 + index, 4 + index)
            smalls_ref[place] = value if part == 0 else smalls_ref[place] + value
    second_gather.to_partner().start()
    if split:
        small.start()
    else:
        smalls_out[...] = smalls_ref[...]
    exchange.wait_sends()
    first_gather.wait_sends()

    lane_low = lax.broadcasted_iota(jnp.int32, (rows, LANES), 1) < HDIM
    wide_ref[:, width // 2 :] = jnp.zeros((tall, width // 2), F32)
    dv_ref[...] = jnp.zeros_like(dv_ref)

    def context_grad(chunk):
        spots = pl.ds(pl.multiple_of(chunk * rows, rows), rows)
        wide = head_pairs(dot_nt(do_ref[chunk], wout_ref[...]), heads)
        for head in range(heads):
            high = wide[head].astype(BF16).astype(F32)
            both = jnp.where(lane_low, high, wide[head] - high)
            dc_ref[head, spots] = both.astype(BF16)
            dct_ref[head, :, spots] = both.T.astype(BF16)

    def attend_back(chunk, head):
        keys = visible_keys(chunk, rows)
        limits = query_limits(chunk, rows, prefix_ref[0])
        visible = lax.broadcasted_iota(jnp.int32, (keys, rows), 0) <= limits
        spots = pl.ds(chunk * rows, rows)
        seen = pl.ds(0, keys)
        dq_lanes = pl.ds(pl.multiple_of(head * LANES, LANES), LANES)
        dk_lanes = pl.ds(pl.multiple_of((heads + head) * LANES, LANES), LANES)
        scores = dot(kz_ref[head, seen], qt_ref[head, :, spots])
        top = stats_ref[head, 0:1, spots]
        recip = stats_ref[head, 1:2, spots]
        probs = jnp.exp(jnp.where(visible, scores - top, -1e30)) * recip
        grad_probs = dot(v2_ref[head, seen], dct_ref[head, :, spots])
        inner = column_sum(probs * grad_probs)
        grad_scores = (probs * (grad_probs - inner)).astype(BF16)
        dv_ref[head, seen] = dv_ref[head, seen] + dot(probs.astype(BF16), dc_ref[head, spots])
        wide_ref[seen, dk_lanes] = wide_ref[seen, dk_lanes] + dot(grad_scores, q2_ref[head, spots])
        wide_ref[spots, dq_lanes] = dot(kt_ref[head, :, seen], grad_scores).T * scale

    chip, core = mine // 2, mine - 2 * (mine // 2)

    def weight_grad_out():
        out_wide = dot(ct_ref[0], do_ref[0])
        for chunk in range(1, GROUP):
            out_wide = out_wide + dot(ct_ref[chunk], do_ref[chunk])
        grads_ref[:, :depth] = out_wide.T

    def gathered(step):
        if step == 1:
            second_gather.wait_partner()
        if step == 2:
            for part in range(BACK_PIECES):
                second_gather.wait_across(part)
                second_gather.onward(part).start()
        if step == 3:
            for part in range(BACK_PIECES):
                second_gather.wait_diagonal(part)

    beside = {heads: [lambda: gathered(1)], 2 * heads: [lambda: gathered(2)], 3 * heads: [lambda: gathered(3)]}
    if split:
        turns = (2, 5, 9) if last else (3, 6, 11)
        plan = [(turns[0], downs[0].turn), (6, small.first), (6, ups[1].start), (turns[1], downs[1].turn)]
        plan += [(turns[2], ups[0].turn), (11, small.second)]
        for when, action in plan:
            beside.setdefault(when, []).append(action)
        for item in earlier:
            beside[2 * heads].append(item.finish)
        beside[3 * heads] += [weight_grad_out, own[0].start]

    def one_turn(turn, carry):
        step = turn // heads
        head = lax.rem(turn, heads)
        near = 1 - step // 2
        flip = lax.rem(step, 2)
        to_chip = (1 - near) * (1 - chip) + near * chip
        chunk = 2 * to_chip + core + flip * (1 - 2 * core)
        for when in sorted(beside):
            @pl.when(turn == when)
            def _():
                for action in beside[when]:
                    action()

        @pl.when(head == 0)
        def _():
            context_grad(chunk)

        for each in range(GROUP):
            @pl.when(chunk == each)
            def _():
                attend_back(each, head)
        return carry

    wout_in.wait()
    wqkv_in.wait()
    for move in saved_in:
        move.wait()
    lax.fori_loop(0, GROUP * heads, one_turn, 0)

    def kind_lanes(kind):
        return slice(kind * span, kind * span + depth)

    def pack_chunk(chunk, carry):
        spots = pl.ds(pl.multiple_of(chunk * rows, rows), rows)
        xt_ref[:, spots] = transposed(normed_ref[chunk]).astype(BF16)
        for kind in range(3):
            parts = []
            for head in range(heads):
                if kind < 2:
                    wide = wide_ref[spots, slice((kind * heads + head) * LANES, (kind * heads + head + 1) * LANES)]
                else:
                    wide = dv_ref[head, spots]
                    wide = wide + pltpu.roll(wide, HDIM, 1)
                parts.append(wide[:, :HDIM])
            values = jnp.concatenate(parts, axis=1)
            high, low = high_low(values)
            high_ref[spots, kind_lanes(kind)] = high
            lowbits_ref[spots, kind_lanes(kind)] = low
            if kind != 1:
                place = slice((kind // 2) * depth, (kind // 2 + 1) * depth)
                bias_ref[:, place] = bias_ref[:, place] + column_sum(values)
        return carry

    bias_ref[...] = jnp.zeros_like(bias_ref)
    whole_in.wait()
    lax.fori_loop(0, GROUP, pack_chunk, 0)

    def weight_grad(kind):
        place = slice((kind + 1) * depth, (kind + 2) * depth)
        lanes = kind_lanes(kind)
        grads_ref[:, place] = dot(xt_ref[...], high_ref[:, lanes]) + dot(xt_ref[...], lowbits_ref[:, lanes])

    def input_terms(chunk, part):
        spots = part_spots(chunk, part)
        total = None
        for kind in range(3):
            for values in (high_ref, lowbits_ref):
                term = dot(values[spots, kind_lanes(kind)], wqkv_ref[kind])
                total = term if total is None else total + term
        terms_ref[chunk, exchange.spot(part)] = total

    if last:
        ups[1].turn()
        own_small.first()
    if split:
        weight_grad(0)
        own[1].start()
        weight_grad(1)
        weight_grad(2)
        own[2].start()
        own[3].start()
    for part in range(BACK_PIECES):
        input_terms(diagonal, part)
        exchange.relay_copy(part).start()
        input_terms(across, part)
        if part > 0:
            exchange.pass_on(part - 1)
    input_terms(partner, 0)
    exchange.near_copy(0).start()
    exchange.pass_on(BACK_PIECES - 1)
    for part in range(1, BACK_PIECES):
        input_terms(partner, part)
        exchange.near_copy(part).start()
    for part in range(BACK_PIECES):
        input_terms(mine, part)
    if split and not last:
        ups[1].turn()
    if last:
        own[0].turn()
        own[1].turn()
        own[2].turn()
        own[3].turn()
        own_small.second()
    if not split:
        weight_grad_out()
        for kind in range(3):
            weight_grad(kind)
        moves.store(grads_ref, grads_hbm)
    for item in downs + ups:
        item.finish()
    for part in range(BACK_PIECES):
        spot = exchange.spot(part)
        dx_ref[spot] = exchange.result(part) + du_ref[spot]
    if split:
        small.third()
    if last:
        own_small.third()
    for item in own:
        item.finish()
    if split and not last:
        moves.store(grads_ref, grads_hbm)
    second_gather.wait_sends()
    exchange.wait_sends()
    for item in earlier + downs + ups + own:
        item.wait_sends()
    for item in (small, own_small):
        if item is not None:
            item.wait_sends()
    moves.finish()


def layer_back(layer, count, split, grad, normal2, recip2, gain, recip1, hbm, prefix, earlier):
    rows, width = grad.shape
    wdown, wup, active, slope, normed, normal1, wout, wqkv, *saved = hbm
    units, depth = wup.shape[2], wout.shape[1]
    heads = depth // HDIM
    tall = GROUP * rows
    share = width // count
    behind = split and earlier is not None
    last = split and layer == 0
    columns = 4 * depth
    if not (columns == width == units == 2 * heads * LANES):
        raise ValueError("unsupported sizes")
    outs, out_specs = [shape((rows, width)), shape((8, width))], [VM, VM]
    if not last:
        outs.append(shape((width, columns)))
        out_specs.append(ANY)
    outs += [shape((share if split else width, units))] * 2 + [shape((8, width))]
    out_specs += [VM, VM, VM] if split else [ANY, ANY, VM]
    if behind:
        outs.append(shape((share, columns)))
        out_specs.append(VM)
    if last:
        outs += [shape((share, columns)), shape((8, width))]
        out_specs += [VM, VM]
    whole_rows = pltpu.VMEM((GROUP, rows, width), BF16)
    square = pltpu.VMEM((width, units), F32)
    scratch = [
        whole_rows, whole_rows, pltpu.VMEM((rows, width), F32),
        pltpu.VMEM((tall, units), BF16), pltpu.VMEM((tall, units), BF16),
        pltpu.VMEM(wdown.shape[1:], BF16), pltpu.VMEM(wup.shape[1:], BF16), whole_rows,
        pltpu.VMEM((tall, units), F32), whole_rows, pltpu.VMEM((rows, width), F32),
        square, square, square, pltpu.VMEM((8, width), F32),
    ]
    scratch += [pltpu.VMEM(each.shape, each.dtype) for each in saved[1:]]
    scratch += [
        pltpu.VMEM(wout.shape[1:], BF16), pltpu.VMEM(wqkv.shape[1:], BF16),
        pltpu.VMEM((heads, tall, LANES), BF16), pltpu.VMEM((heads, LANES, tall), BF16),
        pltpu.VMEM((heads, tall, LANES), F32), pltpu.VMEM((width, tall), BF16),
        dma_sems(24),
    ]
    scratch += exchange_scratch(rows, width, BF16, BACK_PIECES) + gather_sems(BACK_PIECES) + gather_sems(BACK_PIECES)
    if behind:
        scratch += owner_scratch(count, width, columns, 2)
    if split:
        scratch += total_scratch(count, width, units, 2) + total_scratch(count, width, units, 2)
        scratch += small_sum_scratch(count, width)
    if last:
        scratch += total_scratch(count, width, columns, 4) + small_sum_scratch(count, width)
    elif split:
        scratch += pair_scratch(count, width, columns, 4)
    return pl.pallas_call(
        functools.partial(layer_backward_kernel, layer, count, split, behind, last),
        out_shape=outs,
        in_specs=[VM] * 5 + [ANY] * 16 + [SM] + ([ANY, VM] if behind else []),
        out_specs=out_specs,
        scratch_shapes=scratch,
        compiler_params=params(5 + layer),
        name="layer_bwd",
    )(grad, normal2, recip2, gain, recip1, *hbm, prefix, *(earlier if behind else ()))


def results_kernel(depth, *refs):
    refs = Refs(refs)
    state_in, grad_in = refs.take(2)
    attn, up, down = refs.take(2), refs.take(2), refs.take(2)
    tail, smalls = refs.one(), refs.take(2)
    state, grad, wqkv, bias_qv, wout, bias_out, gain, shift, wup, bias_up, wdown, bias_down = refs.take(12)
    state[...] = state_in[...]
    grad[...] = grad_in[...]
    for layer in range(2):
        wout[layer] = attn[layer][:, :depth].T
        for kind in range(3):
            wqkv[layer, kind] = attn[layer][:, (kind + 1) * depth : (kind + 2) * depth]
        wup[layer] = up[layer][...]
        wdown[layer] = down[layer][...]
        sums = smalls[layer]
        row = slice(layer, layer + 1)
        bias_down[row] = sums[0:1]
        gain[layer, 1:2] = sums[1:2]
        shift[layer, 1:2] = sums[2:3]
        gain[layer, 0:1] = sums[3:4]
        shift[layer, 0:1] = sums[4:5]
        bias_out[row] = sums[5:6]
        bias_up[row] = sums[6:7]
        biases = tail if layer == 0 else smalls[0]
        for kind in range(2):
            bias_qv[layer, kind : kind + 1] = biases[7:8, kind * depth : (kind + 1) * depth]


def results(state, grad, attn, up, down, tail, smalls, depth):
    rows, width = state.shape
    share, units = up[0].shape
    layers = len(attn)
    outs = pl.pallas_call(
        functools.partial(results_kernel, depth),
        out_shape=[
            shape((rows, width)), shape((rows, width)), shape((layers, 3, share, depth)),
            shape((layers, 2, depth)), shape((layers, depth, share)), shape((layers, width)),
            shape((layers, 2, width)), shape((layers, 2, width)), shape((layers, share, units)),
            shape((layers, units)), shape((layers, share, units)), shape((layers, width)),
        ],
        in_specs=[VM] * 11,
        out_specs=[VM] * 12,
        compiler_params=pltpu.CompilerParams(vmem_limit_bytes=VMEM_BYTES),
        name="results",
    )(state, grad, *attn, *up, *down, tail, *smalls)
    return (*outs[:10], jnp.swapaxes(outs[10], 1, 2), outs[11])


def local(
    tokens,
    cotangent,
    prefix,
    w_qkv,
    bias_qv,
    w_out,
    bias_out,
    norm_gain,
    norm_bias,
    w_up,
    bias_up,
    w_down,
    bias_down,
):
    width = tokens.shape[1]
    layer_count = w_qkv.shape[0]
    depth = w_out.shape[1]
    w_qkv = jnp.swapaxes(w_qkv, 2, 3)
    state, low = tokens, tokens
    stored = []
    for layer in range(layer_count):
        state, low, normal1, recip1, normal2, recip2, *saved = layer_forward(
            layer, state, low, w_qkv, bias_qv, w_out, bias_out, norm_gain, norm_bias, w_up, bias_up, w_down,
            bias_down, prefix,
        )
        normed, active, slope = saved[8:]
        stored.append(((normal2, recip2), (active, slope, normed, normal1, recip1), saved[:8]))
    count = lax.axis_size("dp")
    split = count > 2 and count % 2 == 0 and (width // count) % 16 == 0
    grad = cotangent
    earlier = None
    attn, up, down, smalls, biases = [], [], [], [], []
    for layer in reversed(range(layer_count)):
        (normal2, recip2), (active, slope, normed, normal1, recip1), saved = stored[layer]
        hbm = (w_down, w_up, active, slope, normed, normal1, w_out, w_qkv, *saved)
        grad, bias, *rest = layer_back(
            layer, count, split, grad, normal2, recip2, norm_gain, recip1, hbm, prefix, earlier
        )
        if split and layer == 0:
            up_sum, down_sum, small, *rest = rest
            attn = rest[: len(rest) - 2] + attn
            attn.insert(0, rest[-2])
            return results(
                state, grad, attn, [up_sum] + up, [down_sum] + down, rest[-1], [small] + smalls, depth
            )
        attn_grad, up_grad, down_grad, small, *rest = rest
        if split:
            earlier = (attn_grad, bias)
            attn = rest + attn
        else:
            attn.insert(0, attn_grad)
        up.insert(0, up_grad)
        down.insert(0, down_grad)
        smalls.insert(0, small)
        biases.insert(0, bias[7, : 2 * depth].reshape(2, depth))
    scatter = functools.partial(lax.psum_scatter, axis_name="dp", scatter_dimension=1, tiled=True)
    attn_sum, up_sum, down_sum = [scatter(jnp.stack(each)) for each in (attn, up, down)]
    shared = lax.psum(jnp.stack(smalls)[:, :6], ("dp", "tensor"))
    bias_qv_sum, bias_up_sum = lax.psum((jnp.stack(biases), jnp.stack(smalls)[:, 6]), "dp")
    share = attn_sum.shape[1]
    return (
        state,
        grad,
        jnp.moveaxis(attn_sum[:, :, depth:].reshape(layer_count, share, 3, depth), 2, 1),
        bias_qv_sum,
        jnp.swapaxes(attn_sum[:, :, :depth], 1, 2),
        shared[:, 5],
        jnp.stack([shared[:, 3], shared[:, 1]], axis=1),
        jnp.stack([shared[:, 4], shared[:, 2]], axis=1),
        up_sum,
        bias_up_sum,
        jnp.swapaxes(down_sum, 1, 2),
        shared[:, 0],
    )


def solution(mesh):
    in_specs = (
        P(("dp", "tensor"), None),
        P(("dp", "tensor"), None),
        P("dp"),
        P(None, None, None, "tensor"),
        P(None, None, "tensor"),
        P(None, "tensor", None),
        P(),
        P(),
        P(),
        P(None, None, "tensor"),
        P(None, "tensor"),
        P(None, "tensor", None),
        P(),
    )
    out_specs = (
        P(("dp", "tensor"), None),
        P(("dp", "tensor"), None),
        P(None, None, "dp", "tensor"),
        P(None, None, "tensor"),
        P(None, "tensor", "dp"),
        P(),
        P(),
        P(),
        P(None, "dp", "tensor"),
        P(None, "tensor"),
        P(None, "tensor", "dp"),
        P(),
    )
    return jax.shard_map(local, mesh=mesh, in_specs=in_specs, out_specs=out_specs, check_vma=False)
```
